32 devices in a mesh: dp: 32 (over z, y, x, core).
Axes of the slice: x: 2, y: 2, z: 4, core: 2. Of those that a mesh axis runs over, the one named last changes fastest.
Arguments:
- tokens: bfloat16 [4096, 1088], P('dp'), may hold values from -6 to 6
- seq_lengths: int32 [8], replicated, may hold values from 1 to 1024, as said below
- w_qkv: bfloat16 [3551232], P('dp'), may hold values from -8 to 8
- w_out: bfloat16 [1183744], P('dp'), may hold values from -0.75 to 0.75
- w_up: bfloat16 [4734976], P('dp'), may hold values from -0.1875 to 0.1875
- w_down: bfloat16 [4734976], P('dp'), may hold values from -0.09375 to 0.09375
- vectors: bfloat16 [16384], P('dp'), may hold values from -4 to 4
- cotangent: bfloat16 [4096, 1088], P('dp'), may hold values from -6 to 6
Outputs:
- out_block: bfloat16 [4096, 1088], P('dp')
- grad_tokens: float32 [4096, 1088], P('dp')
- grad_w_qkv: float32 [3551232], P('dp')
- grad_w_out: float32 [1183744], P('dp')
- grad_w_up: float32 [4734976], P('dp')
- grad_w_down: float32 [4734976], P('dp')
- grad_vectors: float32 [16384], P('dp')
The draws below stay inside these ranges and needn't reach their ends.
Inputs may be any that keep to these rules, and one draw needn't show every extreme that they name: `seq_lengths`: sequences are packed end to end, each padded to whole blocks of 128 tokens, and together they fill exactly 32 blocks; a sequence covers at most 8 blocks, and some sequence covers exactly 8 full blocks.
All inputs are finite; a program needn't handle non-finite values.
Results may differ from the reference program's by a relative error of at most 0.0084.
Values may be sent and summed in bfloat16 or wider, within the bound.
A program may use at most 256 MiB of HBM per device.

```python
import jax
import jax.numpy as jnp
from jax import lax

D = 1088
HEADS = 17
HEAD = 64
FF = 4352
BLOCK = 128
MAXB = 8
NBLK = 32
NSEQ = 8
QKV_LEN = 3551232
OUT_LEN = 1183744
FF_LEN = 4734976
VEC_LEN = 16384


def draw_seq_lengths(key, part):
    key_pairs = jax.random.fold_in(key, 11)
    key_order = jax.random.fold_in(key, 12)
    key_tail = jax.random.fold_in(key, 13)
    pair_count = (NSEQ - 4) // 2
    shifted = jax.random.randint(key_pairs, (pair_count,), -3, 4, dtype=jnp.int32)
    fixed_part = jnp.array([MAXB, 2, 2, 4], dtype=jnp.int32)
    counts = jnp.concatenate([fixed_part, 4 + shifted, 4 - shifted]).astype(jnp.int32)
    order = jax.random.permutation(key_order, NSEQ)
    counts = counts[order]
    tails = jax.random.randint(key_tail, (NSEQ,), 1, BLOCK + 1, dtype=jnp.int32)
    tails = jnp.where(counts == MAXB, BLOCK, tails)
    return ((counts - 1) * BLOCK + tails).astype(jnp.int32)


def draw_w_qkv(key, part):
    base = jax.random.normal(jax.random.fold_in(key, 21), (D, 3 * D), jnp.float32) * D ** (-0.5)
    spare = jax.random.normal(jax.random.fold_in(key, 23), (QKV_LEN - 3 * D * D,), jnp.float32) * D ** (-0.5)
    return jnp.clip(jnp.concatenate([base.reshape(-1), spare]), -8.0, 8.0).astype(jnp.bfloat16)


def draw_vectors(key, part):
    table = jnp.clip(jax.random.normal(jax.random.fold_in(key, 31), (12, D), jnp.float32) * 0.4, -2.0, 2.0)
    gains = 1.0 + 0.3 * jax.random.uniform(jax.random.fold_in(key, 32), (2, D), jnp.float32, -1.0, 1.0)
    table = table.at[0].set(gains[0]).at[5].set(gains[1])
    spare = jax.random.uniform(jax.random.fold_in(key, 33), (VEC_LEN - 12 * D,), jnp.float32, -1.0, 1.0)
    return jnp.concatenate([table.reshape(-1), spare]).astype(jnp.bfloat16)


def steps_of(key, dims, split, least, high):
    gain, own = 1.0, jax.random.fold_in(key, 6)
    for axis_at, shards_of in split:
        heights = jnp.exp(jax.random.uniform(jax.random.fold_in(own, axis_at), (shards_of,), jnp.float32, least / len(split), high / len(split)))
        gain = gain * jnp.repeat(heights, dims[axis_at] // shards_of).reshape([-1 if axis == axis_at else 1 for axis in range(len(dims))])
    return gain


def gaussian(own_key, extent, spread, bound, shards=(), kind=jnp.bfloat16):
    loudness = steps_of(own_key, extent, shards, -0.22, 0.18) if shards else 1.0
    values = jax.random.normal(own_key, extent, jnp.float32) * spread * loudness
    return jnp.minimum(jnp.maximum(values, -bound), bound).astype(kind)


def setup_inputs(seed: int = 0) -> dict:
    key_list = jax.random.split(jax.random.key(seed), 9)
    return {
        "tokens": gaussian(key_list[0], (NBLK * BLOCK, D), 1.0, 6.0, ((0, 32),)),
        "seq_lengths": draw_seq_lengths(jax.random.fold_in(key_list[8], 71), 0),
        "w_qkv": draw_w_qkv(jax.random.fold_in(key_list[8], 71), 0),
        "w_out": gaussian(key_list[3], (OUT_LEN,), (D // 16) ** -0.5, 0.75, ((0, 32),)),
        "w_up": gaussian(key_list[4], (FF_LEN,), D ** -0.5, 0.1875, ((0, 32),)),
        "w_down": gaussian(key_list[5], (FF_LEN,), FF ** -0.5, 0.09375, ((0, 32),)),
        "vectors": draw_vectors(jax.random.fold_in(key_list[8], 71), 0),
        "cotangent": gaussian(key_list[7], (NBLK * BLOCK, D), 1.0, 6.0, ((0, 32),)),
    }


EPS = 1e-05

def block_layout(seq_lengths, block_ids):
    counts = ((seq_lengths + BLOCK - 1) // BLOCK).astype(jnp.int32)
    end_pos = jnp.cumsum(counts).astype(jnp.int32)
    start_pos = (end_pos - counts).astype(jnp.int32)
    owns_block = (block_ids[:, None] >= start_pos[None, :]) & (block_ids[:, None] < end_pos[None, :])
    first_blk = lax.optimization_barrier(jnp.sum(jnp.where(owns_block, start_pos[None, :], 0), axis=1)).astype(jnp.int32)
    seq_len = lax.optimization_barrier(jnp.sum(jnp.where(owns_block, seq_lengths[None, :], 0), axis=1)).astype(jnp.int32)
    inside = (block_ids - first_blk).astype(jnp.int32)
    filled = jnp.clip(seq_len - inside * BLOCK, 0, BLOCK).astype(jnp.int32)
    return (inside, filled)

def window_mask(inside):
    row_ids = jnp.arange(BLOCK, dtype=jnp.int32)[:, None]
    col_ids = jnp.arange(MAXB * BLOCK, dtype=jnp.int32)[None, :]
    slot_ids = col_ids // BLOCK
    return (slot_ids <= inside) & ((slot_ids > 0) | (col_ids <= row_ids))

def layer_norm(values, gain_vec, bias_vec):
    average = lax.optimization_barrier(jnp.mean(values, axis=-1, keepdims=True))
    centred = values - average
    variance = lax.optimization_barrier(jnp.mean(centred * centred, axis=-1, keepdims=True))
    inv_std = lax.rsqrt(variance + EPS)
    normalized = centred * inv_std
    return (normalized * gain_vec + bias_vec, normalized, inv_std)

def norm_back(grad_out, normalized, inv_std, gain_vec):
    grad_hat = grad_out * gain_vec
    first_mean = lax.optimization_barrier(jnp.mean(grad_hat, axis=-1, keepdims=True))
    second_mean = lax.optimization_barrier(jnp.mean(grad_hat * normalized, axis=-1, keepdims=True))
    return inv_std * (grad_hat - first_mean - normalized * second_mean)

def split_heads(matrix):
    return matrix.reshape(matrix.shape[0], HEADS, HEAD).transpose(1, 0, 2)

def join_heads(matrix):
    return matrix.transpose(1, 0, 2).reshape(matrix.shape[1], HEADS * HEAD)

def head_forward(query, keys, values, allowed):
    scores = jnp.dot(query, keys.T, preferred_element_type=jnp.float32)
    scores = jnp.where(allowed, scores, -1e+30)
    row_max = lax.optimization_barrier(jnp.max(scores, axis=-1))
    row_total = lax.optimization_barrier(jnp.sum(jnp.exp(scores - row_max[:, None]), axis=-1))
    log_sums = row_max + jnp.log(row_total)
    prob_bf = jnp.where(allowed, jnp.exp(scores - log_sums[:, None]), 0.0).astype(jnp.bfloat16)
    output = jnp.dot(prob_bf, values, preferred_element_type=jnp.float32).astype(jnp.bfloat16)
    return (output, log_sums)

def head_backward(query, keys, values, output, grad_output, log_sums, allowed):
    scores = jnp.dot(query, keys.T, preferred_element_type=jnp.float32)
    probs = jnp.where(allowed, jnp.exp(scores - log_sums[:, None]), 0.0)
    prob_bf = probs.astype(jnp.bfloat16)
    grad_value = jnp.dot(prob_bf.T, grad_output, preferred_element_type=jnp.float32)
    grad_prob = jnp.dot(grad_output, values.T, preferred_element_type=jnp.float32)
    row_delta = lax.optimization_barrier(jnp.sum(grad_output.astype(jnp.float32) * output.astype(jnp.float32), axis=-1))
    grad_score = (probs * (grad_prob - row_delta[:, None])).astype(jnp.bfloat16)
    grad_query = jnp.dot(grad_score, keys, preferred_element_type=jnp.float32)
    grad_key = jnp.dot(grad_score.T, query, preferred_element_type=jnp.float32)
    return (grad_query, grad_key, grad_value)

def attend(query, keys, values, allowed):

    def one_head(packed):
        return head_forward(packed[0], packed[1], packed[2], allowed)
    outputs, log_sums = lax.map(one_head, (split_heads(query), split_heads(keys), split_heads(values)))
    return (join_heads(outputs), log_sums)

def attend_back(query, keys, values, output, grad_output, log_sums, allowed):

    def one_head(packed):
        return head_backward(packed[0], packed[1], packed[2], packed[3], packed[4], packed[5], allowed)
    grad_query, grad_key, grad_value = lax.map(one_head, (split_heads(query), split_heads(keys), split_heads(values), split_heads(output), split_heads(grad_output), log_sums))
    return (join_heads(grad_query), join_heads(grad_key), join_heads(grad_value))

def pad_flat(matrix, length):
    flat = matrix.reshape(-1)
    return jnp.concatenate([flat, jnp.zeros((length - flat.shape[0],), jnp.float32)])

def reference(tokens, seq_lengths, w_qkv, w_out, w_up, w_down, vectors, cotangent):
    total_rows = NBLK * BLOCK
    block_ids = jnp.arange(NBLK, dtype=jnp.int32)
    inside, filled = block_layout(seq_lengths, block_ids)
    valid = (jnp.arange(BLOCK, dtype=jnp.int32)[None, :] < filled[:, None]).reshape(total_rows)
    weight_qkv = w_qkv[:3 * D * D].reshape(D, 3 * D)
    weight_out = w_out[:D * D].reshape(D, D)
    weight_up = w_up[:D * FF].reshape(D, FF)
    weight_down = w_down[:FF * D].reshape(FF, D)
    vector_rows = vectors[:12 * D].reshape(12, D).astype(jnp.float32)
    bias_up = vector_rows[8:12].reshape(FF)
    query_scale = HEAD ** (-0.5)
    inputs = tokens.astype(jnp.float32)
    normed_attn, hat_one, inv_one = layer_norm(inputs, vector_rows[0], vector_rows[1])
    normed_attn = normed_attn.astype(jnp.bfloat16)
    projected = jnp.dot(normed_attn, weight_qkv, preferred_element_type=jnp.float32)
    query = (query_scale * (projected[:, :D] + vector_rows[2])).astype(jnp.bfloat16)
    keys = projected[:, D:2 * D].astype(jnp.bfloat16)
    values = (projected[:, 2 * D:] + vector_rows[3]).astype(jnp.bfloat16)
    kv_blocks = jnp.stack([keys.reshape(NBLK, BLOCK, D), values.reshape(NBLK, BLOCK, D)], axis=1)
    query_blocks = query.reshape(NBLK, BLOCK, D)

    def window(block_num):
        source_blk = block_num - jnp.arange(MAXB, dtype=jnp.int32)
        clipped = jnp.maximum(source_blk, 0)
        window_kv = kv_blocks[clipped]
        return (window_kv[:, 0].reshape(MAXB * BLOCK, D), window_kv[:, 1].reshape(MAXB * BLOCK, D))

    def forward_block(packed):
        block_num, query_blk, inside_blk = packed
        window_k, window_v = window(block_num)
        return attend(query_blk, window_k, window_v, window_mask(inside_blk))
    attended, log_sums = lax.map(forward_block, (block_ids, query_blocks, inside))
    attended = attended.reshape(total_rows, D)
    residual = inputs + jnp.dot(attended, weight_out, preferred_element_type=jnp.float32) + vector_rows[4]
    normed_mlp, hat_two, inv_two = layer_norm(residual, vector_rows[5], vector_rows[6])
    normed_mlp = normed_mlp.astype(jnp.bfloat16)
    up_pre = jnp.dot(normed_mlp, weight_up, preferred_element_type=jnp.float32) + bias_up
    normal_cdf = 0.5 * (1.0 + lax.erf(up_pre * 2.0 ** (-0.5)))
    activated = (up_pre * normal_cdf).astype(jnp.bfloat16)
    result = residual + jnp.dot(activated, weight_down, preferred_element_type=jnp.float32) + vector_rows[7]
    out_block = jnp.where(valid[:, None], result, 0.0).astype(jnp.bfloat16)
    cot_rows = jnp.where(valid[:, None], cotangent.astype(jnp.float32), 0.0)
    cot_bf = cot_rows.astype(jnp.bfloat16)
    grad_down = jnp.dot(activated.T, cot_bf, preferred_element_type=jnp.float32)
    grad_bias_down = lax.optimization_barrier(jnp.sum(cot_rows, axis=0))
    grad_act = jnp.dot(cot_bf, weight_down.T, preferred_element_type=jnp.float32)
    normal_pdf = jnp.exp(-0.5 * up_pre * up_pre) * (2.0 * jnp.pi) ** (-0.5)
    grad_pre = grad_act * (normal_cdf + up_pre * normal_pdf)
    grad_pre_bf = grad_pre.astype(jnp.bfloat16)
    grad_up = jnp.dot(normed_mlp.T, grad_pre_bf, preferred_element_type=jnp.float32)
    grad_bias_up = lax.optimization_barrier(jnp.sum(grad_pre, axis=0))
    grad_normed_mlp = jnp.dot(grad_pre_bf, weight_up.T, preferred_element_type=jnp.float32)
    grad_gain_two = lax.optimization_barrier(jnp.sum(grad_normed_mlp * hat_two, axis=0))
    grad_bias_two = lax.optimization_barrier(jnp.sum(grad_normed_mlp, axis=0))
    grad_residual = cot_rows + norm_back(grad_normed_mlp, hat_two, inv_two, vector_rows[5])
    grad_bias_out = lax.optimization_barrier(jnp.sum(grad_residual, axis=0))
    grad_res_bf = grad_residual.astype(jnp.bfloat16)
    grad_out = jnp.dot(attended.T, grad_res_bf, preferred_element_type=jnp.float32)
    grad_attended = jnp.dot(grad_res_bf, weight_out.T, preferred_element_type=jnp.float32).astype(jnp.bfloat16)

    def backward_block(dkv_total, packed):
        block_num, query_blk, attended_blk, grad_blk, sums_blk, inside_blk = packed
        window_k, window_v = window(block_num)
        grad_query, grad_key, grad_value = attend_back(query_blk, window_k, window_v, attended_blk, grad_blk, sums_blk, window_mask(inside_blk))
        window_grads = jnp.stack([grad_key.reshape(MAXB, BLOCK, D), grad_value.reshape(MAXB, BLOCK, D)], axis=1)
        in_window = jnp.arange(MAXB, dtype=jnp.int32) <= inside_blk
        window_grads = jnp.where(in_window[:, None, None, None], window_grads, 0.0)
        source_blk = jnp.maximum(block_num - jnp.arange(MAXB, dtype=jnp.int32), 0)
        return (dkv_total.at[source_blk].add(window_grads), grad_query)
    dkv_start = jnp.zeros((NBLK, 2, BLOCK, D), jnp.float32)
    dkv_total, grad_query = lax.scan(backward_block, dkv_start, (block_ids, query_blocks, attended.reshape(NBLK, BLOCK, D), grad_attended.reshape(NBLK, BLOCK, D), log_sums, inside))
    grad_query = query_scale * grad_query.reshape(total_rows, D)
    grad_key = dkv_total[:, 0].reshape(total_rows, D)
    grad_value = dkv_total[:, 1].reshape(total_rows, D)
    grad_project = jnp.concatenate([grad_query, grad_key, grad_value], axis=1).astype(jnp.bfloat16)
    grad_bias_q = lax.optimization_barrier(jnp.sum(grad_query, axis=0))
    grad_bias_v = lax.optimization_barrier(jnp.sum(grad_value, axis=0))
    grad_qkv = jnp.dot(normed_attn.T, grad_project, preferred_element_type=jnp.float32)
    grad_normed_attn = jnp.dot(grad_project, weight_qkv.T, preferred_element_type=jnp.float32)
    grad_gain_one = lax.optimization_barrier(jnp.sum(grad_normed_attn * hat_one, axis=0))
    grad_bias_one = lax.optimization_barrier(jnp.sum(grad_normed_attn, axis=0))
    grad_tokens = grad_residual + norm_back(grad_normed_attn, hat_one, inv_one, vector_rows[0])
    grad_vectors = jnp.concatenate([jnp.stack([grad_gain_one, grad_bias_one, grad_bias_q, grad_bias_v, grad_bias_out, grad_gain_two, grad_bias_two, grad_bias_down]), grad_bias_up.reshape(4, D)], axis=0)
    return (out_block, grad_tokens, pad_flat(grad_qkv, QKV_LEN), pad_flat(grad_out, OUT_LEN), pad_flat(grad_up, FF_LEN), pad_flat(grad_down, FF_LEN), pad_flat(grad_vectors, VEC_LEN))
```

```python
import jax
import jax.numpy as jnp
from jax import lax
from jax.experimental.layout import Layout, with_layout_constraint
from jax.sharding import PartitionSpec as P

D = 1088
HEADS = 17
HEAD = 64
FF = 4352
BLOCK = 128
MAXB = 8


EPS = 1e-05
WIRE = jnp.bfloat16


def shifted(value, axis, steps):
    count = lax.axis_size(axis)
    first, last = (max(0, -steps), min(count, count - steps))
    return lax.ppermute(value, axis, [(source, source + steps) for source in range(first, last)])


def block_layout(seq_lengths, block_ids):
    counts = (seq_lengths + BLOCK - 1) // BLOCK
    order = jnp.arange(counts.shape[0])
    end_pos = jnp.sum(jnp.where(order[None, :] <= order[:, None], counts[None, :], 0), axis=1)
    start_pos = end_pos - counts
    owns_block = (block_ids[:, None] >= start_pos[None, :]) & (
        block_ids[:, None] < end_pos[None, :]
    )
    first_blk = jnp.sum(jnp.where(owns_block, start_pos[None, :], 0), axis=1)
    seq_len = jnp.sum(jnp.where(owns_block, seq_lengths[None, :], 0), axis=1)
    inside = block_ids - first_blk
    filled = jnp.clip(seq_len - inside * BLOCK, 0, BLOCK)
    return (inside, filled)


def window_mask(inside):
    row_ids = jnp.arange(BLOCK, dtype=jnp.int32)[:, None]
    col_ids = jnp.arange(MAXB * BLOCK, dtype=jnp.int32)[None, :]
    slot_ids = col_ids // BLOCK
    return (slot_ids <= inside) & ((slot_ids > 0) | (col_ids <= row_ids))


def layer_norm(values, gain_vec, bias_vec):
    average = jnp.mean(values, axis=-1, keepdims=True)
    centred = values - average
    variance = jnp.mean(centred * centred, axis=-1, keepdims=True)
    inv_std = lax.rsqrt(variance + EPS)
    normalized = centred * inv_std
    return (normalized * gain_vec + bias_vec, normalized, inv_std)


def norm_back(grad_out, normalized, inv_std, gain_vec):
    grad_hat = grad_out * gain_vec
    first_mean = jnp.mean(grad_hat, axis=-1, keepdims=True)
    second_mean = jnp.mean(grad_hat * normalized, axis=-1, keepdims=True)
    return inv_std * (grad_hat - first_mean - normalized * second_mean)


def split_heads(matrix):
    return matrix.reshape(matrix.shape[0], HEADS, HEAD).transpose(1, 0, 2)


def join_heads(matrix):
    return matrix.transpose(1, 0, 2).reshape(matrix.shape[1], HEADS * HEAD)


def head_forward(query, keys, values, allowed):
    scores = jnp.dot(query, keys.T, preferred_element_type=jnp.float32)
    scores = jnp.where(allowed, scores, -1e30)
    row_max = jnp.max(scores, axis=-1)
    row_total = jnp.sum(jnp.exp(scores - row_max[:, None]), axis=-1)
    log_sums = row_max + jnp.log(row_total)
    prob_bf = jnp.where(allowed, jnp.exp(scores - log_sums[:, None]), 0.0).astype(jnp.bfloat16)
    output = jnp.dot(prob_bf, values, preferred_element_type=jnp.float32).astype(jnp.bfloat16)
    return (output, log_sums)


def head_backward(query, keys, values, output, grad_output, log_sums, allowed):
    scores = jnp.dot(query, keys.T, preferred_element_type=jnp.float32)
    probs = jnp.where(allowed, jnp.exp(scores - log_sums[:, None]), 0.0)
    prob_bf = probs.astype(jnp.bfloat16)
    grad_value = jnp.dot(prob_bf.T, grad_output, preferred_element_type=jnp.float32)
    grad_prob = jnp.dot(grad_output, values.T, preferred_element_type=jnp.float32)
    row_delta = jnp.sum(grad_output.astype(jnp.float32) * output.astype(jnp.float32), axis=-1)
    grad_score = (probs * (grad_prob - row_delta[:, None])).astype(jnp.bfloat16)
    grad_query = jnp.dot(grad_score, keys, preferred_element_type=jnp.float32)
    grad_key = jnp.dot(grad_score.T, query, preferred_element_type=jnp.float32)
    return (grad_query, grad_key, grad_value)


def attend(query, keys, values, allowed):
    outputs, log_sums = jax.vmap(head_forward, (0, 0, 0, None))(
        split_heads(query), split_heads(keys), split_heads(values), allowed
    )
    return (join_heads(outputs), log_sums)


def attend_back(query, keys, values, output, grad_output, log_sums, allowed):
    grad_query, grad_key, grad_value = jax.vmap(head_backward, (0, 0, 0, 0, 0, 0, None))(
        split_heads(query),
        split_heads(keys),
        split_heads(values),
        split_heads(output),
        split_heads(grad_output),
        log_sums,
        allowed,
    )
    return (join_heads(grad_query), join_heads(grad_key), join_heads(grad_value))


def whole_rows(shard, rows, cols):
    count = lax.axis_size("dp")
    return shard.shape[0] % cols == 0 and shard.shape[0] * count == rows * cols


def gather_matrix(shard, rows, cols):
    if whole_rows(shard, rows, cols):
        return lax.all_gather(shard.reshape(-1, cols), "dp", axis=0, tiled=True)
    flat = lax.all_gather(shard, "dp", axis=0, tiled=True)
    return flat[: rows * cols].reshape(rows, cols)


def scatter_matrix(grad, shard):
    rows, cols = grad.shape
    grad = with_layout_constraint(grad.astype(WIRE), Layout((0, 1)))
    if whole_rows(shard, rows, cols):
        split = grad.reshape(lax.axis_size("dp"), -1, cols)
        own = lax.psum_scatter(split, "dp", scatter_dimension=0, tiled=False)
        return own.reshape(-1).astype(jnp.float32)
    flat = pad_flat(grad, shard.shape[0] * lax.axis_size("dp"))
    return lax.psum_scatter(flat, "dp", scatter_dimension=0, tiled=True).astype(jnp.float32)


def pad_flat(matrix, length):
    flat = matrix.reshape(-1)
    return jnp.concatenate([flat, jnp.zeros((length - flat.shape[0],), flat.dtype)])


def local(tokens, seq_lengths, w_qkv, w_out, w_up, w_down, vectors, cotangent):
    device_pos = lax.axis_index("dp")
    inside_all, filled_all = block_layout(seq_lengths, jnp.reshape(device_pos, (1,)))
    inside = inside_all[0]
    valid = jnp.arange(BLOCK, dtype=jnp.int32) < filled_all[0]
    allowed = window_mask(inside)
    vec_length = vectors.shape[0] * lax.axis_size("dp")
    vector_rows = lax.all_gather(vectors, "dp", axis=0, tiled=True)
    vector_rows = vector_rows[: 12 * D].reshape(12, D).astype(jnp.float32)
    weight_qkv = gather_matrix(w_qkv, D, 3 * D)
    weight_out = gather_matrix(w_out, D, D)
    weight_up = gather_matrix(w_up, D, FF)
    weight_down = gather_matrix(w_down, FF, D)
    bias_up = vector_rows[8:12].reshape(FF)
    query_scale = HEAD ** (-0.5)
    inputs = tokens.astype(jnp.float32)
    normed_attn, hat_one, inv_one = layer_norm(inputs, vector_rows[0], vector_rows[1])
    normed_attn = normed_attn.astype(jnp.bfloat16)
    projected = jnp.dot(normed_attn, weight_qkv, preferred_element_type=jnp.float32)
    query = (query_scale * (projected[:, :D] + vector_rows[2])).astype(jnp.bfloat16)
    keys = projected[:, D : 2 * D].astype(jnp.bfloat16)
    values = (projected[:, 2 * D :] + vector_rows[3]).astype(jnp.bfloat16)
    key_value = jnp.stack([keys, values])
    pieces = [key_value]
    for offset in range(1, MAXB):
        pieces.append(shifted(key_value, "dp", offset))
    window_kv = jnp.stack(pieces)
    window_k = window_kv[:, 0].reshape(MAXB * BLOCK, D)
    window_v = window_kv[:, 1].reshape(MAXB * BLOCK, D)
    attended, log_sums = attend(query, window_k, window_v, allowed)
    residual = (
        inputs + jnp.dot(attended, weight_out, preferred_element_type=jnp.float32) + vector_rows[4]
    )
    normed_mlp, hat_two, inv_two = layer_norm(residual, vector_rows[5], vector_rows[6])
    normed_mlp = normed_mlp.astype(jnp.bfloat16)
    up_pre = jnp.dot(normed_mlp, weight_up, preferred_element_type=jnp.float32) + bias_up
    normal_cdf = 0.5 * (1.0 + lax.erf(up_pre * 2.0 ** (-0.5)))
    activated = (up_pre * normal_cdf).astype(jnp.bfloat16)
    result = (
        residual
        + jnp.dot(activated, weight_down, preferred_element_type=jnp.float32)
        + vector_rows[7]
    )
    out_block = jnp.where(valid[:, None], result, 0.0).astype(jnp.bfloat16)
    cot_rows = jnp.where(valid[:, None], cotangent.astype(jnp.float32), 0.0)
    cot_bf = cot_rows.astype(jnp.bfloat16)
    grad_down = jnp.dot(activated.T, cot_bf, preferred_element_type=jnp.float32)
    grad_bias_down = jnp.sum(cot_rows, axis=0)
    grad_act = jnp.dot(cot_bf, weight_down.T, preferred_element_type=jnp.float32)
    normal_pdf = jnp.exp(-0.5 * up_pre * up_pre) * (2.0 * jnp.pi) ** (-0.5)
    grad_pre = grad_act * (normal_cdf + up_pre * normal_pdf)
    grad_pre_bf = grad_pre.astype(jnp.bfloat16)
    grad_up = jnp.dot(normed_mlp.T, grad_pre_bf, preferred_element_type=jnp.float32)
    grad_bias_up = jnp.sum(grad_pre, axis=0)
    grad_normed_mlp = jnp.dot(grad_pre_bf, weight_up.T, preferred_element_type=jnp.float32)
    grad_gain_two = jnp.sum(grad_normed_mlp * hat_two, axis=0)
    grad_bias_two = jnp.sum(grad_normed_mlp, axis=0)
    grad_residual = cot_rows + norm_back(grad_normed_mlp, hat_two, inv_two, vector_rows[5])
    grad_bias_out = jnp.sum(grad_residual, axis=0)
    grad_res_bf = grad_residual.astype(jnp.bfloat16)
    grad_out = jnp.dot(attended.T, grad_res_bf, preferred_element_type=jnp.float32)
    grad_attended = jnp.dot(grad_res_bf, weight_out.T, preferred_element_type=jnp.float32).astype(
        jnp.bfloat16
    )
    grad_down, grad_up, grad_out, grad_attended = lax.optimization_barrier(
        (grad_down.astype(WIRE), grad_up.astype(WIRE), grad_out.astype(WIRE), grad_attended)
    )
    shard_down = scatter_matrix(grad_down, w_down)
    shard_up = scatter_matrix(grad_up, w_up)
    shard_out = scatter_matrix(grad_out, w_out)
    grad_query, grad_key, grad_value = attend_back(
        query, window_k, window_v, attended, grad_attended, log_sums, allowed
    )
    grad_query, grad_key, grad_value, shard_down = lax.optimization_barrier(
        (grad_query, grad_key, grad_value, shard_down)
    )
    window_grads = jnp.stack(
        [grad_key.reshape(MAXB, BLOCK, D), grad_value.reshape(MAXB, BLOCK, D)], axis=1
    )
    sent_grads = window_grads.astype(WIRE)
    own_grads = window_grads[0]
    for offset in range(1, MAXB):
        own_grads = own_grads + shifted(sent_grads[offset], "dp", -offset).astype(jnp.float32)
    grad_query = query_scale * grad_query
    grad_project = jnp.concatenate([grad_query, own_grads[0], own_grads[1]], axis=1).astype(
        jnp.bfloat16
    )
    grad_project, shard_up, shard_out = lax.optimization_barrier(
        (grad_project, shard_up, shard_out)
    )
    grad_bias_q = jnp.sum(grad_query, axis=0)
    grad_bias_v = jnp.sum(own_grads[1], axis=0)
    grad_qkv = jnp.dot(normed_attn.T, grad_project, preferred_element_type=jnp.float32)
    grad_normed_attn = jnp.dot(grad_project, weight_qkv.T, preferred_element_type=jnp.float32)
    grad_gain_one = jnp.sum(grad_normed_attn * hat_one, axis=0)
    grad_bias_one = jnp.sum(grad_normed_attn, axis=0)
    grad_tokens = grad_residual + norm_back(grad_normed_attn, hat_one, inv_one, vector_rows[0])
    grad_vectors = jnp.concatenate(
        [
            jnp.stack(
                [
                    grad_gain_one,
                    grad_bias_one,
                    grad_bias_q,
                    grad_bias_v,
                    grad_bias_out,
                    grad_gain_two,
                    grad_bias_two,
                    grad_bias_down,
                ]
            ),
            grad_bias_up.reshape(4, D),
        ],
        axis=0,
    )
    shard_qkv = scatter_matrix(grad_qkv, w_qkv)
    shard_vec = lax.psum_scatter(
        pad_flat(grad_vectors, vec_length), "dp", scatter_dimension=0, tiled=True
    )
    return (out_block, grad_tokens, shard_qkv, shard_out, shard_up, shard_down, shard_vec)


def solution(mesh):
    in_specs = (P("dp", None), P(), P("dp"), P("dp"), P("dp"), P("dp"), P("dp"), P("dp", None))
    out_specs = (P("dp", None), P("dp", None), P("dp"), P("dp"), P("dp"), P("dp"), P("dp"))
    return jax.shard_map(local, mesh=mesh, in_specs=in_specs, out_specs=out_specs, check_vma=False)
```

```python
import functools

import jax
import jax.numpy as jnp
from jax import lax
from jax.experimental import pallas as pl
from jax.experimental.pallas import tpu as pltpu
from jax.experimental.layout import Layout, with_layout_constraint
from jax.sharding import PartitionSpec as P

D = 1088
HEADS = 17
HEAD = 64
FF = 4352
BLOCK = 128
MAXB = 8


EPS = 1e-05
WIRE = jnp.bfloat16


def shifted(value, axis, steps):
    count = lax.axis_size(axis)
    first, last = (max(0, -steps), min(count, count - steps))
    return lax.ppermute(value, axis, [(source, source + steps) for source in range(first, last)])


def block_layout(seq_lengths, block_ids):
    counts = (seq_lengths + BLOCK - 1) // BLOCK
    order = jnp.arange(counts.shape[0])
    end_pos = jnp.sum(jnp.where(order[None, :] <= order[:, None], counts[None, :], 0), axis=1)
    start_pos = end_pos - counts
    owns_block = (block_ids[:, None] >= start_pos[None, :]) & (
        block_ids[:, None] < end_pos[None, :]
    )
    first_blk = jnp.sum(jnp.where(owns_block, start_pos[None, :], 0), axis=1)
    seq_len = jnp.sum(jnp.where(owns_block, seq_lengths[None, :], 0), axis=1)
    inside = block_ids - first_blk
    filled = jnp.clip(seq_len - inside * BLOCK, 0, BLOCK)
    return (inside, filled)


def window_mask(inside):
    row_ids = jnp.arange(BLOCK, dtype=jnp.int32)[:, None]
    col_ids = jnp.arange(MAXB * BLOCK, dtype=jnp.int32)[None, :]
    slot_ids = col_ids // BLOCK
    return (slot_ids <= inside) & ((slot_ids > 0) | (col_ids <= row_ids))


def layer_norm(values, gain_vec, bias_vec):
    average = jnp.mean(values, axis=-1, keepdims=True)
    centred = values - average
    variance = jnp.mean(centred * centred, axis=-1, keepdims=True)
    inv_std = lax.rsqrt(variance + EPS)
    normalized = centred * inv_std
    return (normalized * gain_vec + bias_vec, normalized, inv_std)


def norm_back(grad_out, normalized, inv_std, gain_vec):
    grad_hat = grad_out * gain_vec
    first_mean = jnp.mean(grad_hat, axis=-1, keepdims=True)
    second_mean = jnp.mean(grad_hat * normalized, axis=-1, keepdims=True)
    return inv_std * (grad_hat - first_mean - normalized * second_mean)


def split_heads(matrix):
    return matrix.reshape(matrix.shape[0], HEADS, HEAD).transpose(1, 0, 2)


def join_heads(matrix):
    return matrix.transpose(1, 0, 2).reshape(matrix.shape[1], HEADS * HEAD)


def head_forward(query, keys, values, allowed):
    scores = jnp.dot(query, keys.T, preferred_element_type=jnp.float32)
    scores = jnp.where(allowed, scores, -1e30)
    row_max = jnp.max(scores, axis=-1)
    row_total = jnp.sum(jnp.exp(scores - row_max[:, None]), axis=-1)
    log_sums = row_max + jnp.log(row_total)
    prob_bf = jnp.where(allowed, jnp.exp(scores - log_sums[:, None]), 0.0).astype(jnp.bfloat16)
    output = jnp.dot(prob_bf, values, preferred_element_type=jnp.float32).astype(jnp.bfloat16)
    return (output, log_sums)


def head_backward(query, keys, values, output, grad_output, log_sums, allowed):
    scores = jnp.dot(query, keys.T, preferred_element_type=jnp.float32)
    probs = jnp.where(allowed, jnp.exp(scores - log_sums[:, None]), 0.0)
    prob_bf = probs.astype(jnp.bfloat16)
    grad_value = jnp.dot(prob_bf.T, grad_output, preferred_element_type=jnp.float32)
    grad_prob = jnp.dot(grad_output, values.T, preferred_element_type=jnp.float32)
    row_delta = jnp.sum(grad_output.astype(jnp.float32) * output.astype(jnp.float32), axis=-1)
    grad_score = (probs * (grad_prob - row_delta[:, None])).astype(jnp.bfloat16)
    grad_query = jnp.dot(grad_score, keys, preferred_element_type=jnp.float32)
    grad_key = jnp.dot(grad_score.T, query, preferred_element_type=jnp.float32)
    return (grad_query, grad_key, grad_value)


def attend(query, keys, values, allowed):
    outputs, log_sums = jax.vmap(head_forward, (0, 0, 0, None))(
        split_heads(query), split_heads(keys), split_heads(values), allowed
    )
    return (join_heads(outputs), log_sums)


def attend_back(query, keys, values, output, grad_output, log_sums, allowed):
    grad_query, grad_key, grad_value = jax.vmap(head_backward, (0, 0, 0, 0, 0, 0, None))(
        split_heads(query),
        split_heads(keys),
        split_heads(values),
        split_heads(output),
        split_heads(grad_output),
        log_sums,
        allowed,
    )
    return (join_heads(grad_query), join_heads(grad_key), join_heads(grad_value))


def whole_rows(shard, rows, cols):
    count = lax.axis_size("dp")
    return shard.shape[0] % cols == 0 and shard.shape[0] * count == rows * cols


def gather_matrix(shard, rows, cols):
    if whole_rows(shard, rows, cols):
        return lax.all_gather(shard.reshape(-1, cols), "dp", axis=0, tiled=True)
    flat = lax.all_gather(shard, "dp", axis=0, tiled=True)
    return flat[: rows * cols].reshape(rows, cols)


def scatter_matrix(grad, shard):
    rows, cols = grad.shape
    grad = with_layout_constraint(grad.astype(WIRE), Layout((0, 1)))
    if whole_rows(shard, rows, cols):
        split = grad.reshape(lax.axis_size("dp"), -1, cols)
        own = lax.psum_scatter(split, "dp", scatter_dimension=0, tiled=False)
        return own.reshape(-1).astype(jnp.float32)
    flat = pad_flat(grad, shard.shape[0] * lax.axis_size("dp"))
    return lax.psum_scatter(flat, "dp", scatter_dimension=0, tiled=True).astype(jnp.float32)


def pad_flat(matrix, length):
    flat = matrix.reshape(-1)
    return jnp.concatenate([flat, jnp.zeros((length - flat.shape[0],), flat.dtype)])


def local_gathered(tokens, seq_lengths, w_qkv, w_out, w_up, w_down, vectors, cotangent):
    device_pos = lax.axis_index("dp")
    inside_all, filled_all = block_layout(seq_lengths, jnp.reshape(device_pos, (1,)))
    inside = inside_all[0]
    valid = jnp.arange(BLOCK, dtype=jnp.int32) < filled_all[0]
    allowed = window_mask(inside)
    vec_length = vectors.shape[0] * lax.axis_size("dp")
    vector_rows = lax.all_gather(vectors, "dp", axis=0, tiled=True)
    vector_rows = vector_rows[: 12 * D].reshape(12, D).astype(jnp.float32)
    weight_qkv = gather_matrix(w_qkv, D, 3 * D)
    weight_out = gather_matrix(w_out, D, D)
    weight_up = gather_matrix(w_up, D, FF)
    weight_down = gather_matrix(w_down, FF, D)
    bias_up = vector_rows[8:12].reshape(FF)
    query_scale = HEAD ** (-0.5)
    inputs = tokens.astype(jnp.float32)
    normed_attn, hat_one, inv_one = layer_norm(inputs, vector_rows[0], vector_rows[1])
    normed_attn = normed_attn.astype(jnp.bfloat16)
    projected = jnp.dot(normed_attn, weight_qkv, preferred_element_type=jnp.float32)
    query = (query_scale * (projected[:, :D] + vector_rows[2])).astype(jnp.bfloat16)
    keys = projected[:, D : 2 * D].astype(jnp.bfloat16)
    values = (projected[:, 2 * D :] + vector_rows[3]).astype(jnp.bfloat16)
    key_value = jnp.stack([keys, values])
    pieces = [key_value]
    for offset in range(1, MAXB):
        pieces.append(shifted(key_value, "dp", offset))
    window_kv = jnp.stack(pieces)
    window_k = window_kv[:, 0].reshape(MAXB * BLOCK, D)
    window_v = window_kv[:, 1].reshape(MAXB * BLOCK, D)
    attended, log_sums = attend(query, window_k, window_v, allowed)
    residual = (
        inputs + jnp.dot(attended, weight_out, preferred_element_type=jnp.float32) + vector_rows[4]
    )
    normed_mlp, hat_two, inv_two = layer_norm(residual, vector_rows[5], vector_rows[6])
    normed_mlp = normed_mlp.astype(jnp.bfloat16)
    up_pre = jnp.dot(normed_mlp, weight_up, preferred_element_type=jnp.float32) + bias_up
    normal_cdf = 0.5 * (1.0 + lax.erf(up_pre * 2.0 ** (-0.5)))
    activated = (up_pre * normal_cdf).astype(jnp.bfloat16)
    result = (
        residual
        + jnp.dot(activated, weight_down, preferred_element_type=jnp.float32)
        + vector_rows[7]
    )
    out_block = jnp.where(valid[:, None], result, 0.0).astype(jnp.bfloat16)
    cot_rows = jnp.where(valid[:, None], cotangent.astype(jnp.float32), 0.0)
    cot_bf = cot_rows.astype(jnp.bfloat16)
    grad_down = jnp.dot(activated.T, cot_bf, preferred_element_type=jnp.float32)
    grad_bias_down = jnp.sum(cot_rows, axis=0)
    grad_act = jnp.dot(cot_bf, weight_down.T, preferred_element_type=jnp.float32)
    normal_pdf = jnp.exp(-0.5 * up_pre * up_pre) * (2.0 * jnp.pi) ** (-0.5)
    grad_pre = grad_act * (normal_cdf + up_pre * normal_pdf)
    grad_pre_bf = grad_pre.astype(jnp.bfloat16)
    grad_up = jnp.dot(normed_mlp.T, grad_pre_bf, preferred_element_type=jnp.float32)
    grad_bias_up = jnp.sum(grad_pre, axis=0)
    grad_normed_mlp = jnp.dot(grad_pre_bf, weight_up.T, preferred_element_type=jnp.float32)
    grad_gain_two = jnp.sum(grad_normed_mlp * hat_two, axis=0)
    grad_bias_two = jnp.sum(grad_normed_mlp, axis=0)
    grad_residual = cot_rows + norm_back(grad_normed_mlp, hat_two, inv_two, vector_rows[5])
    grad_bias_out = jnp.sum(grad_residual, axis=0)
    grad_res_bf = grad_residual.astype(jnp.bfloat16)
    grad_out = jnp.dot(attended.T, grad_res_bf, preferred_element_type=jnp.float32)
    grad_attended = jnp.dot(grad_res_bf, weight_out.T, preferred_element_type=jnp.float32).astype(
        jnp.bfloat16
    )
    grad_down, grad_up, grad_out, grad_attended = lax.optimization_barrier(
        (grad_down.astype(WIRE), grad_up.astype(WIRE), grad_out.astype(WIRE), grad_attended)
    )
    shard_down = scatter_matrix(grad_down, w_down)
    shard_up = scatter_matrix(grad_up, w_up)
    shard_out = scatter_matrix(grad_out, w_out)
    grad_query, grad_key, grad_value = attend_back(
        query, window_k, window_v, attended, grad_attended, log_sums, allowed
    )
    grad_query, grad_key, grad_value, shard_down = lax.optimization_barrier(
        (grad_query, grad_key, grad_value, shard_down)
    )
    window_grads = jnp.stack(
        [grad_key.reshape(MAXB, BLOCK, D), grad_value.reshape(MAXB, BLOCK, D)], axis=1
    )
    sent_grads = window_grads.astype(WIRE)
    own_grads = window_grads[0]
    for offset in range(1, MAXB):
        own_grads = own_grads + shifted(sent_grads[offset], "dp", -offset).astype(jnp.float32)
    grad_query = query_scale * grad_query
    grad_project = jnp.concatenate([grad_query, own_grads[0], own_grads[1]], axis=1).astype(
        jnp.bfloat16
    )
    grad_project, shard_up, shard_out = lax.optimization_barrier(
        (grad_project, shard_up, shard_out)
    )
    grad_bias_q = jnp.sum(grad_query, axis=0)
    grad_bias_v = jnp.sum(own_grads[1], axis=0)
    grad_qkv = jnp.dot(normed_attn.T, grad_project, preferred_element_type=jnp.float32)
    grad_normed_attn = jnp.dot(grad_project, weight_qkv.T, preferred_element_type=jnp.float32)
    grad_gain_one = jnp.sum(grad_normed_attn * hat_one, axis=0)
    grad_bias_one = jnp.sum(grad_normed_attn, axis=0)
    grad_tokens = grad_residual + norm_back(grad_normed_attn, hat_one, inv_one, vector_rows[0])
    grad_vectors = jnp.concatenate(
        [
            jnp.stack(
                [
                    grad_gain_one,
                    grad_bias_one,
                    grad_bias_q,
                    grad_bias_v,
                    grad_bias_out,
                    grad_gain_two,
                    grad_bias_two,
                    grad_bias_down,
                ]
            ),
            grad_bias_up.reshape(4, D),
        ],
        axis=0,
    )
    shard_qkv = scatter_matrix(grad_qkv, w_qkv)
    shard_vec = lax.psum_scatter(
        pad_flat(grad_vectors, vec_length), "dp", scatter_dimension=0, tiled=True
    )
    return (out_block, grad_tokens, shard_qkv, shard_out, shard_up, shard_down, shard_vec)


CORES = 2
CHIPS = 4
SPAN = CORES * CHIPS
SLOTS = -(-HEADS // CHIPS)
WIDE = SLOTS * HEAD
WINDOW = MAXB * BLOCK
MESH = pl.DeviceIdType.MESH
HBM = pl.BlockSpec(memory_space=pl.ANY)
F32 = jnp.float32
BF16 = jnp.bfloat16


class Place:
    def __init__(self):
        self.me = lax.axis_index("dp")
        self.planes = lax.axis_size("dp") // SPAN
        self.z = self.me // SPAN
        self.m = lax.rem(self.me // CORES, CHIPS)
        self.c = lax.rem(self.me, CORES)
        self.sibling = self.me + 1 - 2 * self.c

    def index(self, z, m):
        return z * SPAN + m * CORES + self.c

    def ahead(self, dz, dm):
        return (
            lax.rem(self.z + (dz + self.planes) % self.planes, self.planes),
            lax.rem(self.m + (dm + CHIPS) % CHIPS, CHIPS),
        )


def exchange_body(plan, n_in, n_out, *refs):
    ins, outs = refs[:n_in], refs[n_in : n_in + n_out]
    send_sem, recv_sem, local_sem = refs[n_in + n_out :]
    partners, kept, sends, forwards = plan(Place(), ins, outs)
    barrier = pltpu.get_barrier_semaphore()
    for partner in partners:
        pl.semaphore_signal(barrier, inc=1, device_id=(partner,), device_id_type=MESH)
    pl.semaphore_wait(barrier, len(partners))

    def remote(slot, source, target, partner):
        return pltpu.make_async_remote_copy(
            src_ref=source,
            dst_ref=target,
            send_sem=send_sem.at[slot],
            recv_sem=recv_sem.at[slot],
            device_id=(partner,),
            device_id_type=MESH,
        )

    going = [remote(slot, *send) for slot, send in enumerate(sends)]
    for copy in going:
        copy.start()
    staying = [
        pltpu.make_async_copy(source, target, local_sem.at[slot])
        for slot, (source, target) in enumerate(kept)
    ]
    for copy in staying:
        copy.start()
    landed, passed = set(), []
    for slot, (trigger, *send) in enumerate(forwards):
        if trigger not in landed:
            going[trigger].wait_recv()
            landed.add(trigger)
        copy = remote(len(sends) + slot, *send)
        copy.start()
        passed.append(copy)
    for slot, copy in enumerate(going):
        copy.wait_send()
        if slot not in landed:
            copy.wait_recv()
    for copy in passed:
        copy.wait()
    for copy in staying:
        copy.wait()


def exchange(plan, ins, outs, ident, copies, stays):
    return pl.pallas_call(
        functools.partial(exchange_body, plan, len(ins), len(outs)),
        out_shape=tuple(jax.ShapeDtypeStruct(shape, dtype) for shape, dtype in outs),
        in_specs=[HBM] * len(ins),
        out_specs=tuple([HBM] * len(outs)),
        scratch_shapes=[
            pltpu.SemaphoreType.DMA((copies,)),
            pltpu.SemaphoreType.DMA((copies,)),
            pltpu.SemaphoreType.DMA((max(stays, 1),)),
        ],
        compiler_params=pltpu.CompilerParams(collective_id=ident, has_side_effects=True),
    )(*ins)


def same_parity(at):
    return [
        at.index(*at.ahead(dz, dm))
        for dz in range(at.planes)
        for dm in range(CHIPS)
        if dz or dm
    ]


def opening(at, ins, outs):
    tokens, w_qkv, w_up, vectors = ins
    tokens_out, qkv_out, up_out, vectors_out = outs
    kept = [
        (tokens, tokens_out.at[at.m]),
        (w_up.at[at.m], up_out.at[at.m]),
        (w_qkv.at[at.m], qkv_out.at[at.me]),
        (vectors, vectors_out.at[at.me]),
    ]
    sends = [
        (w_qkv.at[at.m], qkv_out.at[at.me], at.sibling),
        (vectors, vectors_out.at[at.me], at.sibling),
    ]
    forwards = []
    for dz in reversed(range(at.planes)):
        for dm in range(CHIPS):
            if not (dz or dm):
                continue
            z, m = at.ahead(dz, dm)
            peer = at.index(z, m)
            source = at.index(*at.ahead(-dz, -dm))
            if dz == 0:
                sends.append((tokens, tokens_out.at[at.m], peer))
                sends.append((w_up.at[m], up_out.at[at.m], peer))
            forwards.append((len(sends), qkv_out.at[source], qkv_out.at[source], at.sibling))
            sends.append((w_qkv.at[m], qkv_out.at[at.me], peer))
            forwards.append((len(sends), vectors_out.at[source], vectors_out.at[source], at.sibling))
            sends.append((vectors, vectors_out.at[at.me], peer))
    return [*same_parity(at), at.sibling], kept, sends, forwards


def windows(at, ins, outs):
    (own,), (held,) = ins, outs
    here, before = held.at[1, :, at.c], held.at[0, :, at.c]
    after = at.index(at.ahead(1, 0)[0], at.m)
    prior = at.index(at.ahead(-1, 0)[0], at.m)
    sends = [(own, before, after), (own, here, at.sibling)]
    return [after, prior, at.sibling], [(own, here)], sends, [(0, before, before, at.sibling)]


def windows_back(at, ins, outs):
    (grads, partial), (grads_out, partial_out) = ins, outs
    after = at.index(at.ahead(1, 0)[0], at.m)
    prior = at.index(at.ahead(-1, 0)[0], at.m)
    partners, kept, sends, _ = across(1, 0, 0, at, (partial,), (partial_out,))
    return [after, prior, *partners], kept, [(grads, grads_out, prior), *sends], []


def across(turned, spread, halves, at, ins, outs):
    kept, sends, partners = [], [], []
    for dm in range(1, CHIPS) if turned + spread else ():
        m = at.ahead(0, dm)[1]
        peer = at.index(at.z, m)
        partners.append(peer)
        for k in range(turned):
            sends.append((ins[k].at[m], outs[k].at[at.m], peer))
        for k in range(turned, turned + spread):
            sends.append((ins[k], outs[k].at[at.m], peer))
    for k in range(turned):
        kept.append((ins[k].at[at.m], outs[k].at[at.m]))
    for k in range(turned, turned + spread):
        kept.append((ins[k], outs[k].at[at.m]))
    if halves:
        partners.append(at.sibling)
    for k in range(turned + spread, turned + spread + halves):
        lead = (slice(None),) * (len(ins[k].shape) - 3)
        sends.append((ins[k].at[(*lead, 1 - at.c)], outs[k], at.sibling))
    return partners, kept, sends, []


def closing(at, ins, outs):
    grads, vectors = ins[:2]
    grads_out, vectors_out = outs[:2]
    kept = [
        (grads.at[at.z, at.m], grads_out.at[at.z, at.m]),
        (vectors.at[at.z, at.m], vectors_out.at[at.z, at.m]),
    ]
    _, kept_in, sends_in, _ = across(len(ins) - 2, 0, 0, at, ins[2:], outs[2:])
    sends = []
    for dz in reversed(range(at.planes)):
        for dm in range(CHIPS):
            if dz or dm:
                z, m = at.ahead(dz, dm)
                peer = at.index(z, m)
                sends.append((grads.at[z, m], grads_out.at[at.z, at.m], peer))
                sends.append((vectors.at[z, m], vectors_out.at[at.z, at.m], peer))
    return same_parity(at), kept + kept_in, sends + sends_in, []


def swap(ident, turned=(), spread=(), halves=()):
    outs = [(x.shape, x.dtype) for x in turned]
    outs += [((CHIPS, *x.shape), x.dtype) for x in spread]
    outs += [((*x.shape[:-3], *x.shape[-2:]), x.dtype) for x in halves]
    plan = functools.partial(across, len(turned), len(spread), len(halves))
    stays = len(turned) + len(spread)
    return exchange(plan, (*turned, *spread, *halves), outs, ident, 3 * stays + len(halves), stays)


def window_of(info_ref):
    step = pl.program_id(0)
    inside = info_ref[step]
    start = pl.multiple_of((CORES * step + info_ref[CHIPS] + 1) * BLOCK, BLOCK)
    row = lax.broadcasted_iota(jnp.int32, (WINDOW, BLOCK), 0)
    query = lax.broadcasted_iota(jnp.int32, (WINDOW, BLOCK), 1)
    slot = MAXB - 1 - lax.shift_right_logical(row, 7)
    column = lax.bitwise_and(row, BLOCK - 1)
    return pl.ds(start, WINDOW), (slot <= inside) & ((slot > 0) | (column <= query))


def contract(a, b, over):
    return lax.dot_general(a, b, (((over[0],), (over[1],)), ((), ())), preferred_element_type=F32)


def attend_kernel(info_ref, q_ref, kv_ref, out_ref, lse_ref):
    span, allowed = window_of(info_ref)
    for head in range(SLOTS):
        part = pl.ds(head * HEAD, HEAD)
        keys = kv_ref[span, part]
        values = kv_ref[span, pl.ds(WIDE + head * HEAD, HEAD)]
        scores = jnp.where(allowed, contract(keys, q_ref[:, part], (1, 1)), -1e30)
        top = jnp.max(scores, axis=0, keepdims=True)
        powers = jnp.exp(scores - top)
        total = jnp.sum(powers, axis=0, keepdims=True)
        probs = (powers * (1.0 / total)).astype(BF16)
        out_ref[:, part] = contract(probs, values, (0, 0)).astype(BF16)
        lse_ref[0, pl.ds(head, 1), :] = top + jnp.log(total)


def attend_back_kernel(info_ref, q_ref, kv_ref, grad_ref, lse_ref, grad_q_ref, grad_kv_ref):
    @pl.when(pl.program_id(0) == 0)
    def _():
        grad_kv_ref[...] = jnp.zeros_like(grad_kv_ref)

    span, allowed = window_of(info_ref)
    for head in range(SLOTS):
        part = pl.ds(head * HEAD, HEAD)
        part_v = pl.ds(WIDE + head * HEAD, HEAD)
        keys, values = kv_ref[span, part], kv_ref[span, part_v]
        query, grad = q_ref[:, part], grad_ref[:, part]
        scores = jnp.where(allowed, contract(keys, query, (1, 1)), -1e30)
        probs = jnp.exp(scores - lse_ref[0, pl.ds(head, 1), :])
        grad_probs = contract(values, grad, (1, 1))
        delta = jnp.sum(probs * grad_probs, axis=0, keepdims=True)
        grad_scores = (probs * (grad_probs - delta)).astype(BF16)
        grad_q_ref[:, part] = contract(grad_scores, keys, (0, 0))
        grad_kv_ref[span, part] += contract(grad_scores, query, (1, 0))
        grad_kv_ref[span, part_v] += contract(probs.astype(BF16), grad, (1, 0))


def block_rows(width):
    return pl.BlockSpec((BLOCK, width), lambda i: (i, 0))


def whole_of(x):
    return pl.BlockSpec(x.shape, lambda i: (0,) * len(x.shape))


LSE = pl.BlockSpec((1, 8, BLOCK), lambda i: (i, 0, 0))
SMEM = pl.BlockSpec(memory_space=pltpu.SMEM)


def attend_heads(info, query, held):
    return pl.pallas_call(
        attend_kernel,
        grid=(CHIPS,),
        in_specs=[SMEM, block_rows(WIDE), whole_of(held)],
        out_specs=(block_rows(WIDE), LSE),
        out_shape=(
            jax.ShapeDtypeStruct(query.shape, BF16),
            jax.ShapeDtypeStruct((CHIPS, 8, BLOCK), F32),
        ),
        compiler_params=pltpu.CompilerParams(vmem_limit_bytes=40 * 2**20),
    )(info, query, held)


def attend_heads_back(info, query, held, grad, lse):
    return pl.pallas_call(
        attend_back_kernel,
        grid=(CHIPS,),
        in_specs=[SMEM, block_rows(WIDE), whole_of(held), block_rows(WIDE), LSE],
        out_specs=(block_rows(WIDE), whole_of(held)),
        out_shape=(
            jax.ShapeDtypeStruct(query.shape, F32),
            jax.ShapeDtypeStruct(held.shape, F32),
        ),
        compiler_params=pltpu.CompilerParams(vmem_limit_bytes=48 * 2**20),
    )(info, query, held, grad, lse)


def dot(a, b):
    return jnp.dot(a, b, preferred_element_type=F32)


def local_split(tokens, seq_lengths, w_qkv, w_out, w_up, w_down, vectors, cotangent):
    count = lax.axis_size("dp")
    planes = count // SPAN
    me = lax.axis_index("dp")
    z, m, c = me // SPAN, (me // CORES) % CHIPS, me % CORES
    along_z = [[p + SPAN * k for k in range(planes)] for p in range(SPAN)]
    in_plane = [
        [SPAN * k + CORES * i + core for i in range(CHIPS)]
        for k in range(planes)
        for core in range(CORES)
    ]
    to_sibling = [(i, i + 1 - 2 * (i % CORES)) for i in range(count)]
    turned = [
        (SPAN * a + CORES * b + core, SPAN * b + CORES * a + core)
        for a in range(CHIPS)
        for b in range(CHIPS)
        for core in range(CORES)
    ]

    def gather_z(x):
        return lax.all_gather(x, "dp", axis_index_groups=along_z)

    def scatter_z(x):
        return lax.psum_scatter(
            x, "dp", axis_index_groups=along_z, scatter_dimension=0, tiled=False
        )

    def both(x, axis):
        other = lax.ppermute(x, "dp", to_sibling)
        first = jnp.where(c == 0, x, other)
        second = jnp.where(c == 0, other, x)
        return jnp.stack([first, second], axis=axis)

    def own(x, axis):
        return lax.dynamic_index_in_dim(x, c, axis, keepdims=False)

    rows_in = D // count
    hidden = FF // CHIPS
    rows_ff = FF // count
    out_part = gather_z(w_out.reshape(rows_in, D))
    down_part = lax.ppermute(w_down.reshape(rows_ff, D), "dp", turned)

    heads_of = w_qkv.reshape(rows_in, 3, D)
    heads_of = jnp.pad(heads_of, ((0, 0), (0, 0), (0, CHIPS * WIDE - D)))
    heads_of = heads_of.reshape(rows_in, 3, CHIPS, WIDE).transpose(2, 0, 1, 3)
    heads_of = heads_of.reshape(CHIPS, rows_in, 3 * WIDE)
    up_slices = w_up.reshape(rows_in, CHIPS, hidden).transpose(1, 0, 2)
    vec_own = vectors.reshape(1, -1)
    tokens4, weight_qkv, up_part, vecs = exchange(
        opening,
        (tokens, heads_of, up_slices, vec_own),
        [
            ((CHIPS, BLOCK, D), BF16),
            ((count, rows_in, 3 * WIDE), BF16),
            (up_slices.shape, BF16),
            ((count, *vec_own.shape), BF16),
        ],
        1,
        4 * (planes * CHIPS - 1) + 2 * (CHIPS - 1) + 2,
        4,
    )
    up_part = gather_z(up_part)
    down_part = gather_z(down_part)
    cotangent4 = lax.all_gather(cotangent, "dp", axis_index_groups=in_plane)

    blocks = SPAN * z + CORES * jnp.arange(CHIPS, dtype=jnp.int32) + c
    inside, filled = block_layout(seq_lengths, blocks)
    valid4 = (jnp.arange(BLOCK, dtype=jnp.int32)[None, :] < filled[:, None]).reshape(-1, 1)
    filled_own = lax.dynamic_index_in_dim(filled, m, 0, keepdims=False)
    valid = (jnp.arange(BLOCK, dtype=jnp.int32) < filled_own)[:, None]
    info = jnp.concatenate([inside, jnp.reshape(c, (1,))]).astype(jnp.int32)

    vec = vecs.reshape(-1)[: 12 * D].reshape(12, D).astype(F32)

    def head_bias(row):
        padded = jnp.pad(vec[row], (0, CHIPS * WIDE - D)).reshape(CHIPS, WIDE)
        return lax.dynamic_index_in_dim(padded, m, 0, keepdims=False)

    bias_up = lax.dynamic_index_in_dim(vec[8:12].reshape(CHIPS, hidden), m, 0, keepdims=False)
    query_scale = HEAD ** (-0.5)

    inputs4 = tokens4.reshape(CHIPS * BLOCK, D).astype(F32)
    normed_attn, hat_one, inv_one = layer_norm(inputs4, vec[0], vec[1])
    normed_attn = normed_attn.astype(BF16)
    weight_qkv = weight_qkv.reshape(D, 3 * WIDE)
    projected = dot(normed_attn, weight_qkv)
    query = (query_scale * (projected[:, :WIDE] + head_bias(2))).astype(BF16)
    keys = projected[:, WIDE : 2 * WIDE].astype(BF16)
    values = (projected[:, 2 * WIDE :] + head_bias(3)).astype(BF16)
    key_value = jnp.concatenate([keys, values], axis=1).reshape(CHIPS, BLOCK, 2 * WIDE)
    (held,) = exchange(
        windows, (key_value,), [((2, CHIPS, CORES, BLOCK, 2 * WIDE), BF16)], 2, 3, 1
    )
    held = held.reshape(2 * SPAN * BLOCK, 2 * WIDE)
    attended_heads, lse = attend_heads(info, query, held)
    (attended_own,) = swap(3, turned=(attended_heads.reshape(CHIPS, BLOCK, WIDE),))
    attended = attended_own.transpose(1, 0, 2).reshape(BLOCK, CHIPS * WIDE)[:, :D]

    weight_out = both(lax.all_gather(out_part, "dp", axis_index_groups=in_plane), 2)
    weight_out = weight_out.transpose(1, 0, 2, 3, 4).reshape(D, D)
    inputs = tokens.astype(F32)
    residual = inputs + dot(attended, weight_out) + vec[4]
    normed_mlp, hat_two, inv_two = layer_norm(residual, vec[5], vec[6])
    (mlp4,) = swap(4, spread=(normed_mlp.astype(BF16),))
    mlp4 = mlp4.reshape(CHIPS * BLOCK, D)

    weight_up = both(up_part, 2).reshape(D, hidden)
    weight_down = both(down_part, 1).reshape(hidden, D)
    up_pre = dot(mlp4, weight_up) + bias_up
    normal_cdf = 0.5 * (1.0 + lax.erf(up_pre * 2.0 ** (-0.5)))
    activated = (up_pre * normal_cdf).astype(BF16)
    result_part = dot(activated, weight_down).astype(BF16).reshape(CHIPS, BLOCK, D)
    cot4 = jnp.where(valid4, cotangent4.reshape(CHIPS * BLOCK, D), 0)
    grad_act = contract(cot4, weight_down, (1, 1))
    normal_pdf = jnp.exp(-0.5 * up_pre * up_pre) * (2.0 * jnp.pi) ** (-0.5)
    grad_pre = grad_act * (normal_cdf + up_pre * normal_pdf)
    grad_pre_bf = grad_pre.astype(BF16)
    grad_mlp_part = contract(grad_pre_bf, weight_up, (1, 1)).astype(BF16)
    grad_mlp_part = grad_mlp_part.reshape(CHIPS, BLOCK, D)
    grad_bias_up = jnp.sum(grad_pre, axis=0)
    grad_down = contract(activated, cot4, (0, 0)).astype(BF16)
    grad_up = contract(mlp4, grad_pre_bf, (0, 0)).astype(BF16)
    grad_down = grad_down.reshape(planes, CORES, rows_ff, D)
    grad_up = grad_up.reshape(planes, CHIPS, CORES, rows_in, hidden)
    grad_mlp, down_half, up_half = swap(5, turned=(grad_mlp_part,), halves=(grad_down, grad_up))

    def joined(mine, other):
        return (mine.astype(F32) + other.astype(F32)).astype(BF16)

    grad_down = scatter_z(joined(own(grad_down, 1), down_half))
    grad_up = scatter_z(joined(own(grad_up, 2), up_half))
    shard_down = lax.ppermute(grad_down, "dp", turned).astype(F32).reshape(w_down.shape)

    cot = jnp.where(valid, cotangent.astype(F32), 0.0)
    grad_normed_mlp = jnp.sum(grad_mlp.astype(F32), axis=0)
    grad_gain_two = jnp.sum(grad_normed_mlp * hat_two, axis=0)
    grad_bias_two = jnp.sum(grad_normed_mlp, axis=0)
    grad_residual = cot + norm_back(grad_normed_mlp, hat_two, inv_two, vec[5])
    grad_res_bf = grad_residual.astype(BF16)
    grad_attended = contract(grad_res_bf, weight_out, (1, 1)).astype(BF16)
    grad_attended = jnp.pad(grad_attended, ((0, 0), (0, CHIPS * WIDE - D)))
    grad_attended = grad_attended.reshape(BLOCK, CHIPS, WIDE).transpose(1, 0, 2)
    grad_out = contract(attended, grad_res_bf, (0, 0)).astype(BF16)
    grad_out = grad_out.reshape(planes, CHIPS, CORES, rows_in, D)
    grad_heads, out_half = swap(6, turned=(grad_attended,), halves=(grad_out,))
    grad_out = scatter_z(joined(own(grad_out, 2), out_half))

    grad_query, grad_held = attend_heads_back(
        info, query, held, grad_heads.reshape(CHIPS * BLOCK, WIDE), lse
    )
    grad_held = grad_held.reshape(2, CHIPS, CORES, BLOCK, 2 * WIDE)
    (held_half,) = swap(7, halves=(grad_held.astype(BF16),))
    grad_held = own(grad_held, 2) + held_half.astype(F32)
    grad_before, result = exchange(
        windows_back,
        (grad_held[0].astype(BF16), result_part),
        [((CHIPS, BLOCK, 2 * WIDE), BF16), (result_part.shape, BF16)],
        8,
        1 + CHIPS - 1,
        1,
    )
    result = residual + jnp.sum(result.astype(F32), axis=0) + vec[7]
    out_block = jnp.where(valid, result, 0.0).astype(BF16)

    grad_kv = (grad_held[1] + grad_before.astype(F32)).reshape(CHIPS * BLOCK, 2 * WIDE)
    grad_query = query_scale * grad_query
    grad_project = jnp.concatenate([grad_query, grad_kv], axis=1).astype(BF16)
    grad_attn_part = contract(grad_project, weight_qkv, (1, 1))
    grad_qkv = contract(normed_attn, grad_project, (0, 0)).astype(BF16)
    grad_qkv = grad_qkv.reshape(planes, CHIPS, CORES, rows_in, 3 * WIDE)

    def placed(values, width, length):
        start = jnp.zeros((CHIPS * width,), F32)
        return lax.dynamic_update_slice(start, values, (m * width,))[:length]

    rows = [
        jnp.sum(grad_attn_part * hat_one, axis=0),
        jnp.sum(grad_attn_part, axis=0),
        placed(jnp.sum(grad_query, axis=0), WIDE, D),
        placed(jnp.sum(grad_kv[:, WIDE:], axis=0), WIDE, D),
        jnp.sum(grad_residual, axis=0),
        grad_gain_two,
        grad_bias_two,
        jnp.sum(cot, axis=0),
        placed(grad_bias_up, hidden, FF),
    ]
    grad_vec = pad_flat(jnp.concatenate(rows), vectors.shape[0] * count)
    grad_vec = grad_vec.reshape(planes, CHIPS, CORES, 1, -1)
    qkv_half, vec_half = swap(9, halves=(grad_qkv, grad_vec))
    grad_qkv = joined(own(grad_qkv, 2), qkv_half)
    grad_vec = own(grad_vec, 2) + vec_half
    ins = (
        grad_qkv,
        grad_vec,
        grad_attn_part.astype(BF16).reshape(CHIPS, BLOCK, D),
        grad_up,
        grad_out,
    )
    grad_qkv, grad_vec, grad_attn, grad_up, grad_out = exchange(
        closing,
        ins,
        [(x.shape, x.dtype) for x in ins],
        10,
        2 * (planes * CHIPS - 1) + 3 * (CHIPS - 1),
        5,
    )
    shard_vec = jnp.sum(grad_vec, axis=(0, 1)).reshape(-1)
    shard_qkv = jnp.sum(grad_qkv.astype(F32), axis=0).reshape(CHIPS, rows_in, 3, WIDE)
    shard_qkv = shard_qkv.transpose(1, 2, 0, 3).reshape(rows_in, 3, CHIPS * WIDE)[:, :, :D]
    shard_qkv = shard_qkv.reshape(-1)
    shard_up = grad_up.astype(F32).transpose(1, 0, 2).reshape(-1)
    shard_out = jnp.sum(grad_out.astype(F32), axis=0).reshape(-1)
    hat_own = lax.dynamic_slice(hat_one, (m * BLOCK, 0), (BLOCK, D))
    inv_own = lax.dynamic_slice(inv_one, (m * BLOCK, 0), (BLOCK, 1))
    grad_normed_attn = jnp.sum(grad_attn.astype(F32), axis=0)
    grad_tokens = grad_residual + norm_back(grad_normed_attn, hat_own, inv_own, vec[0])
    return (out_block, grad_tokens, shard_qkv, shard_out, shard_up, shard_down, shard_vec)


def local(*args):
    count = lax.axis_size("dp")
    _, _, w_qkv, w_out, w_up, w_down, vectors, _ = args
    fits = count == SPAN * CHIPS and vectors.shape[0] * count >= 12 * D
    for shard, rows, cols in ((w_qkv, D, 3 * D), (w_out, D, D), (w_up, D, FF), (w_down, FF, D)):
        fits = fits and whole_rows(shard, rows, cols)
    return local_split(*args) if fits else local_gathered(*args)


def solution(mesh):
    in_specs = (P("dp", None), P(), P("dp"), P("dp"), P("dp"), P("dp"), P("dp"), P("dp", None))
    out_specs = (P("dp", None), P("dp", None), P("dp"), P("dp"), P("dp"), P("dp"), P("dp"))
    return jax.shard_map(local, mesh=mesh, in_specs=in_specs, out_specs=out_specs, check_vma=False)
```

```python
import functools

import jax
import jax.numpy as jnp
from jax import lax
from jax.experimental import pallas as pl
from jax.experimental.pallas import tpu as pltpu
from jax.experimental.layout import Layout, with_layout_constraint
from jax.sharding import PartitionSpec as P

D = 1088
HEADS = 17
HEAD = 64
FF = 4352
BLOCK = 128
MAXB = 8


EPS = 1e-05
WIRE = jnp.bfloat16


def shifted(value, axis, steps):
    count = lax.axis_size(axis)
    first, last = (max(0, -steps), min(count, count - steps))
    return lax.ppermute(value, axis, [(source, source + steps) for source in range(first, last)])


def block_layout(seq_lengths, block_ids):
    counts = (seq_lengths + BLOCK - 1) // BLOCK
    order = jnp.arange(counts.shape[0])
    end_pos = jnp.sum(jnp.where(order[None, :] <= order[:, None], counts[None, :], 0), axis=1)
    start_pos = end_pos - counts
    owns_block = (block_ids[:, None] >= start_pos[None, :]) & (
        block_ids[:, None] < end_pos[None, :]
    )
    first_blk = jnp.sum(jnp.where(owns_block, start_pos[None, :], 0), axis=1)
    seq_len = jnp.sum(jnp.where(owns_block, seq_lengths[None, :], 0), axis=1)
    inside = block_ids - first_blk
    filled = jnp.clip(seq_len - inside * BLOCK, 0, BLOCK)
    return (inside, filled)


def window_mask(inside):
    row_ids = jnp.arange(BLOCK, dtype=jnp.int32)[:, None]
    col_ids = jnp.arange(MAXB * BLOCK, dtype=jnp.int32)[None, :]
    slot_ids = col_ids // BLOCK
    return (slot_ids <= inside) & ((slot_ids > 0) | (col_ids <= row_ids))


def layer_norm(values, gain_vec, bias_vec):
    average = jnp.mean(values, axis=-1, keepdims=True)
    centred = values - average
    variance = jnp.mean(centred * centred, axis=-1, keepdims=True)
    inv_std = lax.rsqrt(variance + EPS)
    normalized = centred * inv_std
    return (normalized * gain_vec + bias_vec, normalized, inv_std)


def norm_back(grad_out, normalized, inv_std, gain_vec):
    grad_hat = grad_out * gain_vec
    first_mean = jnp.mean(grad_hat, axis=-1, keepdims=True)
    second_mean = jnp.mean(grad_hat * normalized, axis=-1, keepdims=True)
    return inv_std * (grad_hat - first_mean - normalized * second_mean)


def split_heads(matrix):
    return matrix.reshape(matrix.shape[0], HEADS, HEAD).transpose(1, 0, 2)


def join_heads(matrix):
    return matrix.transpose(1, 0, 2).reshape(matrix.shape[1], HEADS * HEAD)


def head_forward(query, keys, values, allowed):
    scores = jnp.dot(query, keys.T, preferred_element_type=jnp.float32)
    scores = jnp.where(allowed, scores, -1e30)
    row_max = jnp.max(scores, axis=-1)
    row_total = jnp.sum(jnp.exp(scores - row_max[:, None]), axis=-1)
    log_sums = row_max + jnp.log(row_total)
    prob_bf = jnp.where(allowed, jnp.exp(scores - log_sums[:, None]), 0.0).astype(jnp.bfloat16)
    output = jnp.dot(prob_bf, values, preferred_element_type=jnp.float32).astype(jnp.bfloat16)
    return (output, log_sums)


def head_backward(query, keys, values, output, grad_output, log_sums, allowed):
    scores = jnp.dot(query, keys.T, preferred_element_type=jnp.float32)
    probs = jnp.where(allowed, jnp.exp(scores - log_sums[:, None]), 0.0)
    prob_bf = probs.astype(jnp.bfloat16)
    grad_value = jnp.dot(prob_bf.T, grad_output, preferred_element_type=jnp.float32)
    grad_prob = jnp.dot(grad_output, values.T, preferred_element_type=jnp.float32)
    row_delta = jnp.sum(grad_output.astype(jnp.float32) * output.astype(jnp.float32), axis=-1)
    grad_score = (probs * (grad_prob - row_delta[:, None])).astype(jnp.bfloat16)
    grad_query = jnp.dot(grad_score, keys, preferred_element_type=jnp.float32)
    grad_key = jnp.dot(grad_score.T, query, preferred_element_type=jnp.float32)
    return (grad_query, grad_key, grad_value)


def attend(query, keys, values, allowed):
    outputs, log_sums = jax.vmap(head_forward, (0, 0, 0, None))(
        split_heads(query), split_heads(keys), split_heads(values), allowed
    )
    return (join_heads(outputs), log_sums)


def attend_back(query, keys, values, output, grad_output, log_sums, allowed):
    grad_query, grad_key, grad_value = jax.vmap(head_backward, (0, 0, 0, 0, 0, 0, None))(
        split_heads(query),
        split_heads(keys),
        split_heads(values),
        split_heads(output),
        split_heads(grad_output),
        log_sums,
        allowed,
    )
    return (join_heads(grad_query), join_heads(grad_key), join_heads(grad_value))


def whole_rows(shard, rows, cols):
    count = lax.axis_size("dp")
    return shard.shape[0] % cols == 0 and shard.shape[0] * count == rows * cols


def gather_matrix(shard, rows, cols):
    if whole_rows(shard, rows, cols):
        return lax.all_gather(shard.reshape(-1, cols), "dp", axis=0, tiled=True)
    flat = lax.all_gather(shard, "dp", axis=0, tiled=True)
    return flat[: rows * cols].reshape(rows, cols)


def scatter_matrix(grad, shard):
    rows, cols = grad.shape
    grad = with_layout_constraint(grad.astype(WIRE), Layout((0, 1)))
    if whole_rows(shard, rows, cols):
        split = grad.reshape(lax.axis_size("dp"), -1, cols)
        own = lax.psum_scatter(split, "dp", scatter_dimension=0, tiled=False)
        return own.reshape(-1).astype(jnp.float32)
    flat = pad_flat(grad, shard.shape[0] * lax.axis_size("dp"))
    return lax.psum_scatter(flat, "dp", scatter_dimension=0, tiled=True).astype(jnp.float32)


def pad_flat(matrix, length):
    flat = matrix.reshape(-1)
    return jnp.concatenate([flat, jnp.zeros((length - flat.shape[0],), flat.dtype)])


def local_gathered(tokens, seq_lengths, w_qkv, w_out, w_up, w_down, vectors, cotangent):
    device_pos = lax.axis_index("dp")
    inside_all, filled_all = block_layout(seq_lengths, jnp.reshape(device_pos, (1,)))
    inside = inside_all[0]
    valid = jnp.arange(BLOCK, dtype=jnp.int32) < filled_all[0]
    allowed = window_mask(inside)
    vec_length = vectors.shape[0] * lax.axis_size("dp")
    vector_rows = lax.all_gather(vectors, "dp", axis=0, tiled=True)
    vector_rows = vector_rows[: 12 * D].reshape(12, D).astype(jnp.float32)
    weight_qkv = gather_matrix(w_qkv, D, 3 * D)
    weight_out = gather_matrix(w_out, D, D)
    weight_up = gather_matrix(w_up, D, FF)
    weight_down = gather_matrix(w_down, FF, D)
    bias_up = vector_rows[8:12].reshape(FF)
    query_scale = HEAD ** (-0.5)
    inputs = tokens.astype(jnp.float32)
    normed_attn, hat_one, inv_one = layer_norm(inputs, vector_rows[0], vector_rows[1])
    normed_attn = normed_attn.astype(jnp.bfloat16)
    projected = jnp.dot(normed_attn, weight_qkv, preferred_element_type=jnp.float32)
    query = (query_scale * (projected[:, :D] + vector_rows[2])).astype(jnp.bfloat16)
    keys = projected[:, D : 2 * D].astype(jnp.bfloat16)
    values = (projected[:, 2 * D :] + vector_rows[3]).astype(jnp.bfloat16)
    key_value = jnp.stack([keys, values])
    pieces = [key_value]
    for offset in range(1, MAXB):
        pieces.append(shifted(key_value, "dp", offset))
    window_kv = jnp.stack(pieces)
    window_k = window_kv[:, 0].reshape(MAXB * BLOCK, D)
    window_v = window_kv[:, 1].reshape(MAXB * BLOCK, D)
    attended, log_sums = attend(query, window_k, window_v, allowed)
    residual = (
        inputs + jnp.dot(attended, weight_out, preferred_element_type=jnp.float32) + vector_rows[4]
    )
    normed_mlp, hat_two, inv_two = layer_norm(residual, vector_rows[5], vector_rows[6])
    normed_mlp = normed_mlp.astype(jnp.bfloat16)
    up_pre = jnp.dot(normed_mlp, weight_up, preferred_element_type=jnp.float32) + bias_up
    normal_cdf = 0.5 * (1.0 + lax.erf(up_pre * 2.0 ** (-0.5)))
    activated = (up_pre * normal_cdf).astype(jnp.bfloat16)
    result = (
        residual
        + jnp.dot(activated, weight_down, preferred_element_type=jnp.float32)
        + vector_rows[7]
    )
    out_block = jnp.where(valid[:, None], result, 0.0).astype(jnp.bfloat16)
    cot_rows = jnp.where(valid[:, None], cotangent.astype(jnp.float32), 0.0)
    cot_bf = cot_rows.astype(jnp.bfloat16)
    grad_down = jnp.dot(activated.T, cot_bf, preferred_element_type=jnp.float32)
    grad_bias_down = jnp.sum(cot_rows, axis=0)
    grad_act = jnp.dot(cot_bf, weight_down.T, preferred_element_type=jnp.float32)
    normal_pdf = jnp.exp(-0.5 * up_pre * up_pre) * (2.0 * jnp.pi) ** (-0.5)
    grad_pre = grad_act * (normal_cdf + up_pre * normal_pdf)
    grad_pre_bf = grad_pre.astype(jnp.bfloat16)
    grad_up = jnp.dot(normed_mlp.T, grad_pre_bf, preferred_element_type=jnp.float32)
    grad_bias_up = jnp.sum(grad_pre, axis=0)
    grad_normed_mlp = jnp.dot(grad_pre_bf, weight_up.T, preferred_element_type=jnp.float32)
    grad_gain_two = jnp.sum(grad_normed_mlp * hat_two, axis=0)
    grad_bias_two = jnp.sum(grad_normed_mlp, axis=0)
    grad_residual = cot_rows + norm_back(grad_normed_mlp, hat_two, inv_two, vector_rows[5])
    grad_bias_out = jnp.sum(grad_residual, axis=0)
    grad_res_bf = grad_residual.astype(jnp.bfloat16)
    grad_out = jnp.dot(attended.T, grad_res_bf, preferred_element_type=jnp.float32)
    grad_attended = jnp.dot(grad_res_bf, weight_out.T, preferred_element_type=jnp.float32).astype(
        jnp.bfloat16
    )
    grad_down, grad_up, grad_out, grad_attended = lax.optimization_barrier(
        (grad_down.astype(WIRE), grad_up.astype(WIRE), grad_out.astype(WIRE), grad_attended)
    )
    shard_down = scatter_matrix(grad_down, w_down)
    shard_up = scatter_matrix(grad_up, w_up)
    shard_out = scatter_matrix(grad_out, w_out)
    grad_query, grad_key, grad_value = attend_back(
        query, window_k, window_v, attended, grad_attended, log_sums, allowed
    )
    grad_query, grad_key, grad_value, shard_down = lax.optimization_barrier(
        (grad_query, grad_key, grad_value, shard_down)
    )
    window_grads = jnp.stack(
        [grad_key.reshape(MAXB, BLOCK, D), grad_value.reshape(MAXB, BLOCK, D)], axis=1
    )
    sent_grads = window_grads.astype(WIRE)
    own_grads = window_grads[0]
    for offset in range(1, MAXB):
        own_grads = own_grads + shifted(sent_grads[offset], "dp", -offset).astype(jnp.float32)
    grad_query = query_scale * grad_query
    grad_project = jnp.concatenate([grad_query, own_grads[0], own_grads[1]], axis=1).astype(
        jnp.bfloat16
    )
    grad_project, shard_up, shard_out = lax.optimization_barrier(
        (grad_project, shard_up, shard_out)
    )
    grad_bias_q = jnp.sum(grad_query, axis=0)
    grad_bias_v = jnp.sum(own_grads[1], axis=0)
    grad_qkv = jnp.dot(normed_attn.T, grad_project, preferred_element_type=jnp.float32)
    grad_normed_attn = jnp.dot(grad_project, weight_qkv.T, preferred_element_type=jnp.float32)
    grad_gain_one = jnp.sum(grad_normed_attn * hat_one, axis=0)
    grad_bias_one = jnp.sum(grad_normed_attn, axis=0)
    grad_tokens = grad_residual + norm_back(grad_normed_attn, hat_one, inv_one, vector_rows[0])
    grad_vectors = jnp.concatenate(
        [
            jnp.stack(
                [
                    grad_gain_one,
                    grad_bias_one,
                    grad_bias_q,
                    grad_bias_v,
                    grad_bias_out,
                    grad_gain_two,
                    grad_bias_two,
                    grad_bias_down,
                ]
            ),
            grad_bias_up.reshape(4, D),
        ],
        axis=0,
    )
    shard_qkv = scatter_matrix(grad_qkv, w_qkv)
    shard_vec = lax.psum_scatter(
        pad_flat(grad_vectors, vec_length), "dp", scatter_dimension=0, tiled=True
    )
    return (out_block, grad_tokens, shard_qkv, shard_out, shard_up, shard_down, shard_vec)


CORES = 2
CHIPS = 4
SPAN = CORES * CHIPS
SLOTS = -(-HEADS // CHIPS)
WIDE = SLOTS * HEAD
WINDOW = MAXB * BLOCK
MESH = pl.DeviceIdType.MESH
HBM = pl.BlockSpec(memory_space=pl.ANY)
F32 = jnp.float32
COST = pl.CostEstimate(flops=0, transcendentals=0, bytes_accessed=48 * 2**20)
BF16 = jnp.bfloat16


class Place:
    def __init__(self):
        self.me = lax.axis_index("dp")
        self.planes = lax.axis_size("dp") // SPAN
        self.z = self.me // SPAN
        self.m = lax.rem(self.me // CORES, CHIPS)
        self.c = lax.rem(self.me, CORES)
        self.sibling = self.me + 1 - 2 * self.c

    def index(self, z, m):
        return z * SPAN + m * CORES + self.c

    def ahead(self, dz, dm):
        return (
            lax.rem(self.z + (dz + self.planes) % self.planes, self.planes),
            lax.rem(self.m + (dm + CHIPS) % CHIPS, CHIPS),
        )


def exchange_body(plan, n_in, n_out, n_after, *refs):
    ins, refs = refs[:n_in], refs[n_in + n_after :]
    outs, (send_sem, recv_sem, local_sem) = refs[:n_out], refs[n_out:]
    partners, kept, sends, forwards = plan(Place(), ins, outs)
    barrier = pltpu.get_barrier_semaphore()
    for partner in partners:
        pl.semaphore_signal(barrier, inc=1, device_id=(partner,), device_id_type=MESH)
    pl.semaphore_wait(barrier, len(partners))

    def remote(slot, source, target, partner):
        return pltpu.make_async_remote_copy(
            src_ref=source,
            dst_ref=target,
            send_sem=send_sem.at[slot],
            recv_sem=recv_sem.at[slot],
            device_id=(partner,),
            device_id_type=MESH,
        )

    going = [remote(slot, *send) for slot, send in enumerate(sends)]
    for copy in going:
        copy.start()
    staying = [
        pltpu.make_async_copy(source, target, local_sem.at[slot])
        for slot, (source, target) in enumerate(kept)
    ]
    for copy in staying:
        copy.start()
    landed = set()
    if forwards:
        for copy in staying:
            copy.wait()
    for triggers, *send in forwards:
        for trigger in triggers:
            if trigger not in landed:
                going[trigger].wait_recv()
                landed.add(trigger)
        going.append(remote(len(going), *send))
        going[-1].start()
    for slot, copy in enumerate(going):
        copy.wait_send()
        if slot not in landed:
            copy.wait_recv()
    if not forwards:
        for copy in staying:
            copy.wait()


def exchange(plan, ins, outs, ident, copies, stays, far=0, after=()):
    return pl.pallas_call(
        functools.partial(exchange_body, plan, len(ins), len(outs), len(after)),
        out_shape=tuple(jax.ShapeDtypeStruct(shape, dtype) for shape, dtype in outs),
        in_specs=[pl.BlockSpec(memory_space=pltpu.VMEM)] * (len(ins) - far) + [HBM] * (far + len(after)),
        out_specs=tuple([HBM] * len(outs)),
        scratch_shapes=[
            pltpu.SemaphoreType.DMA((copies,)),
            pltpu.SemaphoreType.DMA((copies,)),
            pltpu.SemaphoreType.DMA((max(stays, 1),)),
        ],
        cost_estimate=COST,
        compiler_params=pltpu.CompilerParams(
            collective_id=ident, has_side_effects=True, vmem_limit_bytes=40 * 2**20
        ),
    )(*ins, *after)


def same_parity(at):
    return [
        at.index(*at.ahead(dz, dm))
        for dz in range(at.planes)
        for dm in range(CHIPS)
        if dz or dm
    ]


def opening(at, ins, outs):
    tokens, w_qkv, w_up, vectors, w_out = ins
    tokens_out, qkv_out, up_out, vectors_out, rows_out = outs
    kept = [
        (w_qkv.at[at.m], qkv_out.at[at.z, at.m, at.c]),
        (vectors, vectors_out.at[at.z, at.m, at.c]),
        (tokens, tokens_out.at[at.m]),
        (w_up.at[at.m], up_out.at[at.m]),
        (w_out, rows_out.at[at.z]),
    ]
    peers = [at.ahead(0, dm)[1] for dm in range(1, CHIPS)]
    first = [(w_qkv.at[m], qkv_out.at[at.z, at.m, at.c], at.index(at.z, m)) for m in peers]
    first += [(vectors, vectors_out.at[at.z, at.m, at.c], at.index(at.z, m)) for m in peers]
    rest = [(tokens, tokens_out.at[at.m], at.index(at.z, m)) for m in peers]
    rest += [(w_up.at[m], up_out.at[at.m], at.index(at.z, m)) for m in peers]
    sends = first
    forwards, columns = [], []
    for k, out in enumerate((qkv_out, vectors_out)):
        slab = out.at[at.z, :, at.c]
        here = [k * (CHIPS - 1) + i for i in range(CHIPS - 1)]
        for dz in range(1, at.planes):
            columns.append((len(sends) + len(forwards), out.at[at.ahead(-dz, 0)[0], :, at.c]))
            peer = at.index(at.ahead(dz, 0)[0], at.m)
            forwards.append((here, slab, slab, peer))
        forwards.append((here, slab, slab, at.sibling))
    for dz in range(1, at.planes):
        rest.append((w_out, rows_out.at[at.z], at.index(at.ahead(dz, 0)[0], at.m)))
    forwards += [([], *send) for send in rest]
    for slot, slab in columns:
        forwards.append(([slot], slab, slab, at.sibling))
    partners = [at.index(at.z, m) for m in peers] + [at.sibling]
    partners += [at.index(at.ahead(dz, 0)[0], at.m) for dz in range(1, at.planes)]
    return partners, kept, sends, forwards


def windows(at, ins, outs):
    own, cotangent, rows = ins
    held, cotangent_out, rows_out = outs
    here, before = held.at[1, :, at.c], held.at[0, :, at.c]
    after = at.index(at.ahead(1, 0)[0], at.m)
    prior = at.index(at.ahead(-1, 0)[0], at.m)
    partners, kept, sends, _ = across(0, 1, 0, 0, at, (cotangent,), (cotangent_out,))
    column = rows_out.at[:, at.m]
    kept.append((rows, column))
    sends += [(rows, column, peer) for peer in partners]
    sends = [(own, before, after), (own, here, at.sibling), *sends]
    forwards = [([0], before, before, at.sibling)]
    return [after, prior, at.sibling, *partners], [(own, here), *kept], sends, forwards


def windows_back(at, ins, outs):
    (grads, partial), (grads_out, partial_out) = ins, outs
    after = at.index(at.ahead(1, 0)[0], at.m)
    prior = at.index(at.ahead(-1, 0)[0], at.m)
    partners, kept, sends, _ = across(1, 0, 0, 0, at, (partial,), (partial_out,))
    return [after, prior, *partners], kept, [(grads, grads_out, prior), *sends], []


def across(turned, spread, merged, halves, at, ins, outs):
    kept, sends, partners = [], [], []
    for dm in range(1, CHIPS) if turned + spread else ():
        m = at.ahead(0, dm)[1]
        peer = at.index(at.z, m)
        partners.append(peer)
        for k in range(turned):
            sends.append((ins[k].at[m], outs[k].at[at.m], peer))
        for k in range(turned, turned + spread):
            sends.append((ins[k], outs[k].at[at.m], peer))
    for k in range(turned):
        kept.append((ins[k].at[at.m], outs[k].at[at.m]))
    for k in range(turned, turned + spread):
        kept.append((ins[k], outs[k].at[at.m]))
    if halves + merged:
        partners.append(at.sibling)
    for k in range(turned + spread, turned + spread + merged):
        mine = outs[k].at[(*(slice(None),) * (len(ins[k].shape) - 2), at.c)]
        sends.append((ins[k], mine, at.sibling))
        kept.append((ins[k], mine))
    for k in range(turned + spread + merged, len(ins)):
        lead = (slice(None),) * (len(ins[k].shape) - 3)
        sends.append((ins[k].at[(*lead, 1 - at.c)], outs[k], at.sibling))
    return partners, kept, sends, []


def closing(at, ins, outs):
    grads, vectors, rows = ins[:3]
    grads_out, vectors_out, rows_out = outs[:3]
    kept = [
        (grads.at[at.z, at.m], grads_out.at[at.z, at.m]),
        (vectors.at[at.z, at.m], vectors_out.at[at.z, at.m]),
        (rows.at[at.z], rows_out.at[at.z]),
    ]
    _, kept_in, sends_in, _ = across(len(ins) - 3, 0, 0, 0, at, ins[3:], outs[3:])
    sends = []
    for dz in reversed(range(at.planes)):
        for dm in range(CHIPS):
            if dz or dm:
                z, m = at.ahead(dz, dm)
                peer = at.index(z, m)
                sends.append((grads.at[z, m], grads_out.at[at.z, at.m], peer))
                sends.append((vectors.at[z, m], vectors_out.at[at.z, at.m], peer))
                if dm == 0:
                    sends.append((rows.at[z], rows_out.at[at.z], peer))
    return same_parity(at), kept + kept_in, sends + sends_in, []


def swap(ident, turned=(), spread=(), merged=(), halves=(), after=()):
    outs = [(x.shape, x.dtype) for x in turned]
    outs += [((CHIPS, *x.shape), x.dtype) for x in spread]
    outs += [((*x.shape[:-2], CORES, *x.shape[-2:]), x.dtype) for x in merged]
    outs += [((*x.shape[:-3], *x.shape[-2:]), x.dtype) for x in halves]
    plan = functools.partial(across, len(turned), len(spread), len(merged), len(halves))
    stays = len(turned) + len(spread)
    copies = (CHIPS - 1) * stays + len(halves) + len(merged)
    ins = (*turned, *spread, *merged, *halves)
    return exchange(plan, ins, outs, ident, copies, stays + len(merged), len(halves), after)


def window_of(info_ref):
    step = pl.program_id(0)
    inside = info_ref[step]
    start = pl.multiple_of((CORES * step + info_ref[CHIPS] + 1) * BLOCK, BLOCK)
    row = lax.broadcasted_iota(jnp.int32, (WINDOW, BLOCK), 0)
    query = lax.broadcasted_iota(jnp.int32, (WINDOW, BLOCK), 1)
    slot = MAXB - 1 - lax.shift_right_logical(row, 7)
    column = lax.bitwise_and(row, BLOCK - 1)
    return pl.ds(start, WINDOW), (slot <= inside) & ((slot > 0) | (column <= query))


def contract(a, b, over):
    return lax.dot_general(a, b, (((over[0],), (over[1],)), ((), ())), preferred_element_type=F32)


def attend_kernel(info_ref, q_ref, kv_ref, out_ref, lse_ref):
    span, allowed = window_of(info_ref)
    for head in range(SLOTS):
        part = pl.ds(head * HEAD, HEAD)
        keys = kv_ref[span, part]
        values = kv_ref[span, pl.ds(WIDE + head * HEAD, HEAD)]
        scores = jnp.where(allowed, contract(keys, q_ref[:, part], (1, 1)), -1e30)
        top = jnp.max(scores, axis=0, keepdims=True)
        powers = jnp.exp(scores - top)
        total = jnp.sum(powers, axis=0, keepdims=True)
        probs = (powers * (1.0 / total)).astype(BF16)
        out_ref[:, part] = contract(probs, values, (0, 0)).astype(BF16)
        lse_ref[0, pl.ds(head, 1), :] = top + jnp.log(total)


def attend_back_kernel(info_ref, q_ref, kv_ref, grad_ref, lse_ref, grad_q_ref, grad_kv_ref):
    @pl.when(pl.program_id(0) == 0)
    def _():
        grad_kv_ref[...] = jnp.zeros_like(grad_kv_ref)

    span, allowed = window_of(info_ref)
    for head in range(SLOTS):
        part = pl.ds(head * HEAD, HEAD)
        part_v = pl.ds(WIDE + head * HEAD, HEAD)
        keys, values = kv_ref[span, part], kv_ref[span, part_v]
        query, grad = q_ref[:, part], grad_ref[:, part]
        scores = jnp.where(allowed, contract(keys, query, (1, 1)), -1e30)
        probs = jnp.exp(scores - lse_ref[0, pl.ds(head, 1), :])
        grad_probs = contract(values, grad, (1, 1))
        delta = jnp.sum(probs * grad_probs, axis=0, keepdims=True)
        grad_scores = (probs * (grad_probs - delta)).astype(BF16)
        grad_q_ref[:, part] = contract(grad_scores, keys, (0, 0))
        grad_kv_ref[span, part] += contract(grad_scores, query, (1, 0))
        grad_kv_ref[span, part_v] += contract(probs.astype(BF16), grad, (1, 0))


def block_rows(width):
    return pl.BlockSpec((BLOCK, width), lambda i: (i, 0))


def whole_of(x):
    return pl.BlockSpec(x.shape, lambda i: (0,) * len(x.shape))


LSE = pl.BlockSpec((1, 8, BLOCK), lambda i: (i, 0, 0))
SMEM = pl.BlockSpec(memory_space=pltpu.SMEM)


def attend_heads(info, query, held):
    return pl.pallas_call(
        attend_kernel,
        grid=(CHIPS,),
        in_specs=[SMEM, block_rows(WIDE), whole_of(held)],
        out_specs=(block_rows(WIDE), LSE),
        out_shape=(
            jax.ShapeDtypeStruct(query.shape, BF16),
            jax.ShapeDtypeStruct((CHIPS, 8, BLOCK), F32),
        ),
        cost_estimate=COST,
        compiler_params=pltpu.CompilerParams(vmem_limit_bytes=40 * 2**20),
    )(info, query, held)


def attend_heads_back(info, query, held, grad, lse):
    return pl.pallas_call(
        attend_back_kernel,
        grid=(CHIPS,),
        in_specs=[SMEM, block_rows(WIDE), whole_of(held), block_rows(WIDE), LSE],
        out_specs=(block_rows(WIDE), whole_of(held)),
        out_shape=(
            jax.ShapeDtypeStruct(query.shape, F32),
            jax.ShapeDtypeStruct(held.shape, F32),
        ),
        cost_estimate=COST,
        compiler_params=pltpu.CompilerParams(vmem_limit_bytes=48 * 2**20),
    )(info, query, held, grad, lse)


def dot(a, b):
    return jnp.dot(a, b, preferred_element_type=F32)


def local_split(tokens, seq_lengths, w_qkv, w_out, w_up, w_down, vectors, cotangent):
    count = lax.axis_size("dp")
    planes = count // SPAN
    me = lax.axis_index("dp")
    z, m, c = me // SPAN, (me // CORES) % CHIPS, me % CORES
    along_z = [[p + SPAN * k for k in range(planes)] for p in range(SPAN)]
    in_plane = [
        [SPAN * k + CORES * i + core for i in range(CHIPS)]
        for k in range(planes)
        for core in range(CORES)
    ]

    def gather_z(x):
        return lax.all_gather(x, "dp", axis_index_groups=along_z)

    def scatter(x, groups, axis):
        return lax.psum_scatter(
            x, "dp", axis_index_groups=groups, scatter_dimension=axis, tiled=False
        )

    def own(x, axis):
        return lax.dynamic_index_in_dim(x, c, axis, keepdims=False)

    rows_in = D // count
    hidden = FF // CHIPS
    share = hidden // planes
    rows_ff = FF // count
    heads_of = w_qkv.reshape(rows_in, 3, D)
    heads_of = jnp.pad(heads_of, ((0, 0), (0, 0), (0, CHIPS * WIDE - D)))
    heads_of = heads_of.reshape(rows_in, 3, CHIPS, WIDE).transpose(2, 0, 1, 3)
    heads_of = heads_of.reshape(CHIPS, rows_in, 3 * WIDE)
    up_slices = w_up.reshape(rows_in, planes, CHIPS, share).transpose(2, 0, 1, 3)
    up_slices = up_slices.reshape(CHIPS, rows_in, hidden)
    vec_own = vectors.reshape(1, -1)
    tokens4, weight_qkv, up_part, vecs, out_part = exchange(
        opening,
        (tokens, heads_of, up_slices, vec_own, w_out.reshape(rows_in, D)),
        [
            ((CHIPS, BLOCK, D), BF16),
            ((planes, CHIPS, CORES, rows_in, 3 * WIDE), BF16),
            (up_slices.shape, BF16),
            ((planes, CHIPS, CORES, *vec_own.shape), BF16),
            ((planes, rows_in, D), BF16),
        ],
        1,
        4 * (CHIPS - 1) + 5 * (planes - 1) + 2,
        5,
    )
    w_down, weight_qkv = lax.optimization_barrier((w_down, weight_qkv))
    down_part = gather_z(w_down.reshape(rows_ff, D))

    blocks = SPAN * z + CORES * jnp.arange(CHIPS, dtype=jnp.int32) + c
    inside, filled = block_layout(seq_lengths, blocks)
    valid4 = (jnp.arange(BLOCK, dtype=jnp.int32)[None, :] < filled[:, None]).reshape(-1, 1)
    filled_own = lax.dynamic_index_in_dim(filled, m, 0, keepdims=False)
    valid = (jnp.arange(BLOCK, dtype=jnp.int32) < filled_own)[:, None]
    info = jnp.concatenate([inside, jnp.reshape(c, (1,))]).astype(jnp.int32)

    vec = vecs.reshape(-1)[: 12 * D].reshape(12, D).astype(F32)

    def head_bias(row):
        padded = jnp.pad(vec[row], (0, CHIPS * WIDE - D)).reshape(CHIPS, WIDE)
        return lax.dynamic_index_in_dim(padded, m, 0, keepdims=False)

    bias_up = vec[8:12].reshape(planes, CHIPS, share)
    bias_up = lax.dynamic_index_in_dim(bias_up, m, 1, keepdims=False).reshape(hidden)
    query_scale = HEAD ** (-0.5)

    inputs4 = tokens4.reshape(CHIPS * BLOCK, D).astype(F32)
    normed_attn, hat_one, inv_one = layer_norm(inputs4, vec[0], vec[1])
    normed_attn = normed_attn.astype(BF16)
    weight_qkv = weight_qkv.reshape(D, 3 * WIDE)
    projected = dot(normed_attn, weight_qkv)
    query = (query_scale * (projected[:, :WIDE] + head_bias(2))).astype(BF16)
    keys = projected[:, WIDE : 2 * WIDE].astype(BF16)
    values = (projected[:, 2 * WIDE :] + head_bias(3)).astype(BF16)
    key_value = jnp.concatenate([keys, values], axis=1).reshape(CHIPS, BLOCK, 2 * WIDE)
    held, cotangent4, out_part = exchange(
        windows,
        (key_value, cotangent, out_part),
        [
            ((2, CHIPS, CORES, BLOCK, 2 * WIDE), BF16),
            ((CHIPS, BLOCK, D), BF16),
            ((planes, CHIPS, rows_in, D), BF16),
        ],
        2,
        3 + 2 * (CHIPS - 1),
        3,
    )
    up_part, held = lax.optimization_barrier((up_part, held))
    up_part = gather_z(up_part)
    held = held.reshape(2 * SPAN * BLOCK, 2 * WIDE)
    attended_heads, lse = attend_heads(info, query, held)
    attended_own, weight_out = swap(
        3, turned=(attended_heads.reshape(CHIPS, BLOCK, WIDE),), merged=(out_part,)
    )
    weight_out = weight_out.reshape(D, D)
    attended = attended_own.transpose(1, 0, 2).reshape(BLOCK, CHIPS * WIDE)[:, :D]

    inputs = tokens.astype(F32)
    residual = inputs + dot(attended, weight_out) + vec[4]
    normed_mlp, hat_two, inv_two = layer_norm(residual, vec[5], vec[6])
    mlp4, weight_up, weight_down = swap(
        4, spread=(normed_mlp.astype(BF16),), merged=(up_part, down_part)
    )
    mlp4 = mlp4.reshape(CHIPS * BLOCK, D)

    weight_up = weight_up.reshape(D, hidden)
    weight_down = weight_down.reshape(hidden, D)
    up_pre = dot(mlp4, weight_up) + bias_up
    normal_cdf = 0.5 * (1.0 + lax.erf(up_pre * 2.0 ** (-0.5)))
    activated = (up_pre * normal_cdf).astype(BF16)
    result_part = dot(activated, weight_down).astype(BF16).reshape(CHIPS, BLOCK, D)
    cot4 = jnp.where(valid4, cotangent4.reshape(CHIPS * BLOCK, D), 0)
    grad_act = contract(cot4, weight_down, (1, 1))
    normal_pdf = jnp.exp(-0.5 * up_pre * up_pre) * (2.0 * jnp.pi) ** (-0.5)
    grad_pre = grad_act * (normal_cdf + up_pre * normal_pdf)
    grad_pre_bf = grad_pre.astype(BF16)
    grad_mlp_part = contract(grad_pre_bf, weight_up, (1, 1)).astype(BF16)
    grad_mlp_part = grad_mlp_part.reshape(CHIPS, BLOCK, D)
    grad_bias_up = jnp.sum(grad_pre, axis=0)
    grad_down = contract(activated, cot4, (0, 0)).astype(BF16)
    grad_up = contract(mlp4, grad_pre_bf, (0, 0)).astype(BF16)
    grad_down = grad_down.reshape(planes, CORES, rows_ff, D)
    grad_up = grad_up.reshape(planes, CHIPS, CORES, rows_in, hidden)
    grad_mlp, down_half, up_half = swap(5, turned=(grad_mlp_part,), halves=(grad_down, grad_up))

    def joined(mine, other):
        return (mine.astype(F32) + other.astype(F32)).astype(BF16)

    grad_down, grad_up, grad_mlp = lax.optimization_barrier(
        (joined(own(grad_down, 1), down_half), joined(own(grad_up, 2), up_half), grad_mlp)
    )
    grad_down = scatter(grad_down, along_z, 0)
    grad_up = scatter(grad_up, along_z, 0)
    shard_down = grad_down.astype(F32).reshape(w_down.shape)

    cot = jnp.where(valid, cotangent.astype(F32), 0.0)
    grad_normed_mlp = jnp.sum(grad_mlp.astype(F32), axis=0)
    grad_gain_two = jnp.sum(grad_normed_mlp * hat_two, axis=0)
    grad_bias_two = jnp.sum(grad_normed_mlp, axis=0)
    grad_residual = cot + norm_back(grad_normed_mlp, hat_two, inv_two, vec[5])
    grad_res_bf = grad_residual.astype(BF16)
    grad_attended = contract(grad_res_bf, weight_out, (1, 1)).astype(BF16)
    grad_attended = jnp.pad(grad_attended, ((0, 0), (0, CHIPS * WIDE - D)))
    grad_attended = grad_attended.reshape(BLOCK, CHIPS, WIDE).transpose(1, 0, 2)
    grad_out = contract(attended, grad_res_bf, (0, 0)).astype(BF16)
    grad_out = grad_out.reshape(planes, CHIPS, CORES, rows_in, D)
    grad_heads, out_half = swap(6, turned=(grad_attended,), halves=(grad_out,))
    grad_out = joined(own(grad_out, 2), out_half).transpose(1, 0, 2, 3)

    grad_query, grad_held = attend_heads_back(
        info, query, held, grad_heads.reshape(CHIPS * BLOCK, WIDE), lse
    )
    grad_held = grad_held.reshape(2, CHIPS, CORES, BLOCK, 2 * WIDE)
    out_parts, held_half = swap(
        7, turned=(grad_out,), halves=(grad_held.astype(BF16),), after=(grad_down,)
    )
    grad_out = jnp.sum(out_parts.astype(F32), axis=0).astype(BF16)
    grad_held = own(grad_held, 2) + held_half.astype(F32)
    grad_before, result = exchange(
        windows_back,
        (grad_held[0].astype(BF16), result_part),
        [((CHIPS, BLOCK, 2 * WIDE), BF16), (result_part.shape, BF16)],
        8,
        1 + CHIPS - 1,
        1,
    )
    result = residual + jnp.sum(result.astype(F32), axis=0) + vec[7]
    out_block = jnp.where(valid, result, 0.0).astype(BF16)

    grad_kv = (grad_held[1] + grad_before.astype(F32)).reshape(CHIPS * BLOCK, 2 * WIDE)
    grad_query = query_scale * grad_query
    grad_project = jnp.concatenate([grad_query, grad_kv], axis=1).astype(BF16)
    grad_attn_part = contract(grad_project, weight_qkv, (1, 1))
    grad_qkv = contract(normed_attn, grad_project, (0, 0)).astype(BF16)
    grad_qkv = grad_qkv.reshape(planes, CHIPS, CORES, rows_in, 3 * WIDE)

    def placed(values, width, length):
        start = jnp.zeros((CHIPS * width,), F32)
        return lax.dynamic_update_slice(start, values, (m * width,))[:length]

    placed_up = jnp.where(
        jnp.arange(CHIPS)[None, :, None] == m, grad_bias_up.reshape(planes, 1, share), 0.0
    )
    rows = [
        jnp.sum(grad_attn_part * hat_one, axis=0),
        jnp.sum(grad_attn_part, axis=0),
        placed(jnp.sum(grad_query, axis=0), WIDE, D),
        placed(jnp.sum(grad_kv[:, WIDE:], axis=0), WIDE, D),
        jnp.sum(grad_residual, axis=0),
        grad_gain_two,
        grad_bias_two,
        jnp.sum(cot, axis=0),
        placed_up.reshape(FF),
    ]
    grad_vec = pad_flat(jnp.concatenate(rows), vectors.shape[0] * count)
    grad_vec = grad_vec.reshape(planes, CHIPS, CORES, 1, -1)
    qkv_half, vec_half = swap(9, halves=(grad_qkv, grad_vec), after=(grad_up,))
    grad_qkv = joined(own(grad_qkv, 2), qkv_half)
    grad_vec = own(grad_vec, 2) + vec_half
    ins = (
        grad_qkv,
        grad_vec,
        grad_out,
        grad_attn_part.astype(BF16).reshape(CHIPS, BLOCK, D),
        grad_up,
    )
    grad_qkv, grad_vec, grad_out, grad_attn, grad_up = exchange(
        closing,
        ins,
        [(x.shape, x.dtype) for x in ins],
        10,
        2 * (planes * CHIPS - 1) + planes - 1 + 2 * (CHIPS - 1),
        5,
    )
    shard_vec = jnp.sum(grad_vec, axis=(0, 1)).reshape(-1)
    shard_qkv = jnp.sum(grad_qkv.astype(F32), axis=0).reshape(CHIPS, rows_in, 3, WIDE)
    shard_qkv = shard_qkv.transpose(1, 2, 0, 3).reshape(rows_in, 3, CHIPS * WIDE)[:, :, :D]
    shard_qkv = shard_qkv.reshape(-1)
    shard_up = grad_up.astype(F32).reshape(CHIPS, rows_in, planes, share)
    shard_up = shard_up.transpose(1, 2, 0, 3).reshape(-1)
    shard_out = jnp.sum(grad_out.astype(F32), axis=0).reshape(-1)
    hat_own = lax.dynamic_slice(hat_one, (m * BLOCK, 0), (BLOCK, D))
    inv_own = lax.dynamic_slice(inv_one, (m * BLOCK, 0), (BLOCK, 1))
    grad_normed_attn = jnp.sum(grad_attn.astype(F32), axis=0)
    grad_tokens = grad_residual + norm_back(grad_normed_attn, hat_own, inv_own, vec[0])
    return (out_block, grad_tokens, shard_qkv, shard_out, shard_up, shard_down, shard_vec)


def local(*args):
    count = lax.axis_size("dp")
    _, _, w_qkv, w_out, w_up, w_down, vectors, _ = args
    fits = count == SPAN * CHIPS and vectors.shape[0] * count >= 12 * D
    for shard, rows, cols in ((w_qkv, D, 3 * D), (w_out, D, D), (w_up, D, FF), (w_down, FF, D)):
        fits = fits and whole_rows(shard, rows, cols)
    return local_split(*args) if fits else local_gathered(*args)


def solution(mesh):
    in_specs = (P("dp", None), P(), P("dp"), P("dp"), P("dp"), P("dp"), P("dp"), P("dp", None))
    out_specs = (P("dp", None), P("dp", None), P("dp"), P("dp"), P("dp"), P("dp"), P("dp"))
    return jax.shard_map(local, mesh=mesh, in_specs=in_specs, out_specs=out_specs, check_vma=False)
```

```python
import functools

import jax
import jax.numpy as jnp
from jax import lax
from jax.experimental import pallas as pl
from jax.experimental.pallas import tpu as pltpu
from jax.experimental.layout import Layout, with_layout_constraint
from jax.sharding import PartitionSpec as P

D = 1088
HEADS = 17
HEAD = 64
FF = 4352
BLOCK = 128
MAXB = 8


EPS = 1e-05
WIRE = jnp.bfloat16


def shifted(value, axis, steps):
    count = lax.axis_size(axis)
    first, last = (max(0, -steps), min(count, count - steps))
    return lax.ppermute(value, axis, [(source, source + steps) for source in range(first, last)])


def block_layout(seq_lengths, block_ids):
    counts = (seq_lengths + BLOCK - 1) // BLOCK
    order = jnp.arange(counts.shape[0])
    end_pos = jnp.sum(jnp.where(order[None, :] <= order[:, None], counts[None, :], 0), axis=1)
    start_pos = end_pos - counts
    owns_block = (block_ids[:, None] >= start_pos[None, :]) & (
        block_ids[:, None] < end_pos[None, :]
    )
    first_blk = jnp.sum(jnp.where(owns_block, start_pos[None, :], 0), axis=1)
    seq_len = jnp.sum(jnp.where(owns_block, seq_lengths[None, :], 0), axis=1)
    inside = block_ids - first_blk
    filled = jnp.clip(seq_len - inside * BLOCK, 0, BLOCK)
    return (inside, filled)


def window_mask(inside):
    row_ids = jnp.arange(BLOCK, dtype=jnp.int32)[:, None]
    col_ids = jnp.arange(MAXB * BLOCK, dtype=jnp.int32)[None, :]
    slot_ids = col_ids // BLOCK
    return (slot_ids <= inside) & ((slot_ids > 0) | (col_ids <= row_ids))


def layer_norm(values, gain_vec, bias_vec):
    average = jnp.mean(values, axis=-1, keepdims=True)
    centred = values - average
    variance = jnp.mean(centred * centred, axis=-1, keepdims=True)
    inv_std = lax.rsqrt(variance + EPS)
    normalized = centred * inv_std
    return (normalized * gain_vec + bias_vec, normalized, inv_std)


def norm_back(grad_out, normalized, inv_std, gain_vec):
    grad_hat = grad_out * gain_vec
    first_mean = jnp.mean(grad_hat, axis=-1, keepdims=True)
    second_mean = jnp.mean(grad_hat * normalized, axis=-1, keepdims=True)
    return inv_std * (grad_hat - first_mean - normalized * second_mean)


def split_heads(matrix):
    return matrix.reshape(matrix.shape[0], HEADS, HEAD).transpose(1, 0, 2)


def join_heads(matrix):
    return matrix.transpose(1, 0, 2).reshape(matrix.shape[1], HEADS * HEAD)


def head_forward(query, keys, values, allowed):
    scores = jnp.dot(query, keys.T, preferred_element_type=jnp.float32)
    scores = jnp.where(allowed, scores, -1e30)
    row_max = jnp.max(scores, axis=-1)
    row_total = jnp.sum(jnp.exp(scores - row_max[:, None]), axis=-1)
    log_sums = row_max + jnp.log(row_total)
    prob_bf = jnp.where(allowed, jnp.exp(scores - log_sums[:, None]), 0.0).astype(jnp.bfloat16)
    output = jnp.dot(prob_bf, values, preferred_element_type=jnp.float32).astype(jnp.bfloat16)
    return (output, log_sums)


def head_backward(query, keys, values, output, grad_output, log_sums, allowed):
    scores = jnp.dot(query, keys.T, preferred_element_type=jnp.float32)
    probs = jnp.where(allowed, jnp.exp(scores - log_sums[:, None]), 0.0)
    prob_bf = probs.astype(jnp.bfloat16)
    grad_value = jnp.dot(prob_bf.T, grad_output, preferred_element_type=jnp.float32)
    grad_prob = jnp.dot(grad_output, values.T, preferred_element_type=jnp.float32)
    row_delta = jnp.sum(grad_output.astype(jnp.float32) * output.astype(jnp.float32), axis=-1)
    grad_score = (probs * (grad_prob - row_delta[:, None])).astype(jnp.bfloat16)
    grad_query = jnp.dot(grad_score, keys, preferred_element_type=jnp.float32)
    grad_key = jnp.dot(grad_score.T, query, preferred_element_type=jnp.float32)
    return (grad_query, grad_key, grad_value)


def attend(query, keys, values, allowed):
    outputs, log_sums = jax.vmap(head_forward, (0, 0, 0, None))(
        split_heads(query), split_heads(keys), split_heads(values), allowed
    )
    return (join_heads(outputs), log_sums)


def attend_back(query, keys, values, output, grad_output, log_sums, allowed):
    grad_query, grad_key, grad_value = jax.vmap(head_backward, (0, 0, 0, 0, 0, 0, None))(
        split_heads(query),
        split_heads(keys),
        split_heads(values),
        split_heads(output),
        split_heads(grad_output),
        log_sums,
        allowed,
    )
    return (join_heads(grad_query), join_heads(grad_key), join_heads(grad_value))


def whole_rows(shard, rows, cols):
    count = lax.axis_size("dp")
    return shard.shape[0] % cols == 0 and shard.shape[0] * count == rows * cols


def gather_matrix(shard, rows, cols):
    if whole_rows(shard, rows, cols):
        return lax.all_gather(shard.reshape(-1, cols), "dp", axis=0, tiled=True)
    flat = lax.all_gather(shard, "dp", axis=0, tiled=True)
    return flat[: rows * cols].reshape(rows, cols)


def scatter_matrix(grad, shard):
    rows, cols = grad.shape
    grad = with_layout_constraint(grad.astype(WIRE), Layout((0, 1)))
    if whole_rows(shard, rows, cols):
        split = grad.reshape(lax.axis_size("dp"), -1, cols)
        own = lax.psum_scatter(split, "dp", scatter_dimension=0, tiled=False)
        return own.reshape(-1).astype(jnp.float32)
    flat = pad_flat(grad, shard.shape[0] * lax.axis_size("dp"))
    return lax.psum_scatter(flat, "dp", scatter_dimension=0, tiled=True).astype(jnp.float32)


def pad_flat(matrix, length):
    flat = matrix.reshape(-1)
    return jnp.concatenate([flat, jnp.zeros((length - flat.shape[0],), flat.dtype)])


def local_gathered(tokens, seq_lengths, w_qkv, w_out, w_up, w_down, vectors, cotangent):
    device_pos = lax.axis_index("dp")
    inside_all, filled_all = block_layout(seq_lengths, jnp.reshape(device_pos, (1,)))
    inside = inside_all[0]
    valid = jnp.arange(BLOCK, dtype=jnp.int32) < filled_all[0]
    allowed = window_mask(inside)
    vec_length = vectors.shape[0] * lax.axis_size("dp")
    vector_rows = lax.all_gather(vectors, "dp", axis=0, tiled=True)
    vector_rows = vector_rows[: 12 * D].reshape(12, D).astype(jnp.float32)
    weight_qkv = gather_matrix(w_qkv, D, 3 * D)
    weight_out = gather_matrix(w_out, D, D)
    weight_up = gather_matrix(w_up, D, FF)
    weight_down = gather_matrix(w_down, FF, D)
    bias_up = vector_rows[8:12].reshape(FF)
    query_scale = HEAD ** (-0.5)
    inputs = tokens.astype(jnp.float32)
    normed_attn, hat_one, inv_one = layer_norm(inputs, vector_rows[0], vector_rows[1])
    normed_attn = normed_attn.astype(jnp.bfloat16)
    projected = jnp.dot(normed_attn, weight_qkv, preferred_element_type=jnp.float32)
    query = (query_scale * (projected[:, :D] + vector_rows[2])).astype(jnp.bfloat16)
    keys = projected[:, D : 2 * D].astype(jnp.bfloat16)
    values = (projected[:, 2 * D :] + vector_rows[3]).astype(jnp.bfloat16)
    key_value = jnp.stack([keys, values])
    pieces = [key_value]
    for offset in range(1, MAXB):
        pieces.append(shifted(key_value, "dp", offset))
    window_kv = jnp.stack(pieces)
    window_k = window_kv[:, 0].reshape(MAXB * BLOCK, D)
    window_v = window_kv[:, 1].reshape(MAXB * BLOCK, D)
    attended, log_sums = attend(query, window_k, window_v, allowed)
    residual = (
        inputs + jnp.dot(attended, weight_out, preferred_element_type=jnp.float32) + vector_rows[4]
    )
    normed_mlp, hat_two, inv_two = layer_norm(residual, vector_rows[5], vector_rows[6])
    normed_mlp = normed_mlp.astype(jnp.bfloat16)
    up_pre = jnp.dot(normed_mlp, weight_up, preferred_element_type=jnp.float32) + bias_up
    normal_cdf = 0.5 * (1.0 + lax.erf(up_pre * 2.0 ** (-0.5)))
    activated = (up_pre * normal_cdf).astype(jnp.bfloat16)
    result = (
        residual
        + jnp.dot(activated, weight_down, preferred_element_type=jnp.float32)
        + vector_rows[7]
    )
    out_block = jnp.where(valid[:, None], result, 0.0).astype(jnp.bfloat16)
    cot_rows = jnp.where(valid[:, None], cotangent.astype(jnp.float32), 0.0)
    cot_bf = cot_rows.astype(jnp.bfloat16)
    grad_down = jnp.dot(activated.T, cot_bf, preferred_element_type=jnp.float32)
    grad_bias_down = jnp.sum(cot_rows, axis=0)
    grad_act = jnp.dot(cot_bf, weight_down.T, preferred_element_type=jnp.float32)
    normal_pdf = jnp.exp(-0.5 * up_pre * up_pre) * (2.0 * jnp.pi) ** (-0.5)
    grad_pre = grad_act * (normal_cdf + up_pre * normal_pdf)
    grad_pre_bf = grad_pre.astype(jnp.bfloat16)
    grad_up = jnp.dot(normed_mlp.T, grad_pre_bf, preferred_element_type=jnp.float32)
    grad_bias_up = jnp.sum(grad_pre, axis=0)
    grad_normed_mlp = jnp.dot(grad_pre_bf, weight_up.T, preferred_element_type=jnp.float32)
    grad_gain_two = jnp.sum(grad_normed_mlp * hat_two, axis=0)
    grad_bias_two = jnp.sum(grad_normed_mlp, axis=0)
    grad_residual = cot_rows + norm_back(grad_normed_mlp, hat_two, inv_two, vector_rows[5])
    grad_bias_out = jnp.sum(grad_residual, axis=0)
    grad_res_bf = grad_residual.astype(jnp.bfloat16)
    grad_out = jnp.dot(attended.T, grad_res_bf, preferred_element_type=jnp.float32)
    grad_attended = jnp.dot(grad_res_bf, weight_out.T, preferred_element_type=jnp.float32).astype(
        jnp.bfloat16
    )
    grad_down, grad_up, grad_out, grad_attended = lax.optimization_barrier(
        (grad_down.astype(WIRE), grad_up.astype(WIRE), grad_out.astype(WIRE), grad_attended)
    )
    shard_down = scatter_matrix(grad_down, w_down)
    shard_up = scatter_matrix(grad_up, w_up)
    shard_out = scatter_matrix(grad_out, w_out)
    grad_query, grad_key, grad_value = attend_back(
        query, window_k, window_v, attended, grad_attended, log_sums, allowed
    )
    grad_query, grad_key, grad_value, shard_down = lax.optimization_barrier(
        (grad_query, grad_key, grad_value, shard_down)
    )
    window_grads = jnp.stack(
        [grad_key.reshape(MAXB, BLOCK, D), grad_value.reshape(MAXB, BLOCK, D)], axis=1
    )
    sent_grads = window_grads.astype(WIRE)
    own_grads = window_grads[0]
    for offset in range(1, MAXB):
        own_grads = own_grads + shifted(sent_grads[offset], "dp", -offset).astype(jnp.float32)
    grad_query = query_scale * grad_query
    grad_project = jnp.concatenate([grad_query, own_grads[0], own_grads[1]], axis=1).astype(
        jnp.bfloat16
    )
    grad_project, shard_up, shard_out = lax.optimization_barrier(
        (grad_project, shard_up, shard_out)
    )
    grad_bias_q = jnp.sum(grad_query, axis=0)
    grad_bias_v = jnp.sum(own_grads[1], axis=0)
    grad_qkv = jnp.dot(normed_attn.T, grad_project, preferred_element_type=jnp.float32)
    grad_normed_attn = jnp.dot(grad_project, weight_qkv.T, preferred_element_type=jnp.float32)
    grad_gain_one = jnp.sum(grad_normed_attn * hat_one, axis=0)
    grad_bias_one = jnp.sum(grad_normed_attn, axis=0)
    grad_tokens = grad_residual + norm_back(grad_normed_attn, hat_one, inv_one, vector_rows[0])
    grad_vectors = jnp.concatenate(
        [
            jnp.stack(
                [
                    grad_gain_one,
                    grad_bias_one,
                    grad_bias_q,
                    grad_bias_v,
                    grad_bias_out,
                    grad_gain_two,
                    grad_bias_two,
                    grad_bias_down,
                ]
            ),
            grad_bias_up.reshape(4, D),
        ],
        axis=0,
    )
    shard_qkv = scatter_matrix(grad_qkv, w_qkv)
    shard_vec = lax.psum_scatter(
        pad_flat(grad_vectors, vec_length), "dp", scatter_dimension=0, tiled=True
    )
    return (out_block, grad_tokens, shard_qkv, shard_out, shard_up, shard_down, shard_vec)


CORES = 2
CHIPS = 4
SPAN = CORES * CHIPS
SLOTS = -(-HEADS // CHIPS)
WIDE = SLOTS * HEAD
WINDOW = MAXB * BLOCK
MESH = pl.DeviceIdType.MESH
HBM = pl.BlockSpec(memory_space=pl.ANY)
F32 = jnp.float32
COST = pl.CostEstimate(flops=0, transcendentals=0, bytes_accessed=48 * 2**20)
BF16 = jnp.bfloat16


class Place:
    def __init__(self):
        self.me = lax.axis_index("dp")
        self.planes = lax.axis_size("dp") // SPAN
        self.z = self.me // SPAN
        self.m = lax.rem(self.me // CORES, CHIPS)
        self.c = lax.rem(self.me, CORES)
        self.sibling = self.me + 1 - 2 * self.c

    def index(self, z, m):
        return z * SPAN + m * CORES + self.c

    def ahead(self, dz, dm):
        return (
            lax.rem(self.z + (dz + self.planes) % self.planes, self.planes),
            lax.rem(self.m + (dm + CHIPS) % CHIPS, CHIPS),
        )


def exchange_body(plan, n_in, n_out, n_after, *refs):
    ins, refs = refs[:n_in], refs[n_in + n_after :]
    outs, (send_sem, recv_sem, local_sem) = refs[:n_out], refs[n_out:]
    partners, kept, sends, forwards = plan(Place(), ins, outs)
    barrier = pltpu.get_barrier_semaphore()
    for partner in partners:
        pl.semaphore_signal(barrier, inc=1, device_id=(partner,), device_id_type=MESH)
    pl.semaphore_wait(barrier, len(partners))

    def remote(slot, source, target, partner):
        return pltpu.make_async_remote_copy(
            src_ref=source,
            dst_ref=target,
            send_sem=send_sem.at[slot],
            recv_sem=recv_sem.at[slot],
            device_id=(partner,),
            device_id_type=MESH,
        )

    going = [remote(slot, *send) for slot, send in enumerate(sends)]
    for copy in going:
        copy.start()
    staying = [
        pltpu.make_async_copy(source, target, local_sem.at[slot])
        for slot, (source, target) in enumerate(kept)
    ]
    for copy in staying:
        copy.start()
    landed = set()
    if forwards:
        for copy in staying:
            copy.wait()
    for triggers, *send in forwards:
        for trigger in triggers:
            if trigger not in landed:
                going[trigger].wait_recv()
                landed.add(trigger)
        going.append(remote(len(going), *send))
        going[-1].start()
    for slot, copy in enumerate(going):
        copy.wait_send()
        if slot not in landed:
            copy.wait_recv()
    if not forwards:
        for copy in staying:
            copy.wait()


def exchange(plan, ins, outs, ident, copies, stays, far=0, after=()):
    return pl.pallas_call(
        functools.partial(exchange_body, plan, len(ins), len(outs), len(after)),
        out_shape=tuple(jax.ShapeDtypeStruct(shape, dtype) for shape, dtype in outs),
        in_specs=[pl.BlockSpec(memory_space=pltpu.VMEM)] * (len(ins) - far) + [HBM] * (far + len(after)),
        out_specs=tuple([HBM] * len(outs)),
        scratch_shapes=[
            pltpu.SemaphoreType.DMA((copies,)),
            pltpu.SemaphoreType.DMA((copies,)),
            pltpu.SemaphoreType.DMA((max(stays, 1),)),
        ],
        cost_estimate=COST,
        compiler_params=pltpu.CompilerParams(
            collective_id=ident, has_side_effects=True, vmem_limit_bytes=40 * 2**20
        ),
    )(*ins, *after)


def same_parity(at):
    return [
        at.index(*at.ahead(dz, dm))
        for dz in range(at.planes)
        for dm in range(CHIPS)
        if dz or dm
    ]


def opening(at, ins, outs):
    tokens, w_qkv, w_up, vectors, w_out = ins
    tokens_out, qkv_out, up_out, vectors_out, rows_out = outs
    kept = [
        (w_qkv.at[at.m], qkv_out.at[at.z, at.m, at.c]),
        (vectors, vectors_out.at[at.z, at.m, at.c]),
        (tokens, tokens_out.at[at.m]),
        (w_up.at[at.m], up_out.at[at.m]),
        (w_out, rows_out.at[at.z]),
    ]
    peers = [at.ahead(0, dm)[1] for dm in range(1, CHIPS)]
    first = [(w_qkv.at[m], qkv_out.at[at.z, at.m, at.c], at.index(at.z, m)) for m in peers]
    first += [(vectors, vectors_out.at[at.z, at.m, at.c], at.index(at.z, m)) for m in peers]
    rest = [(tokens, tokens_out.at[at.m], at.index(at.z, m)) for m in peers]
    rest += [(w_up.at[m], up_out.at[at.m], at.index(at.z, m)) for m in peers]
    sends = first
    forwards, columns = [], []
    for k, out in enumerate((qkv_out, vectors_out)):
        slab = out.at[at.z, :, at.c]
        here = [k * (CHIPS - 1) + i for i in range(CHIPS - 1)]
        for dz in range(1, at.planes):
            columns.append((len(sends) + len(forwards), out.at[at.ahead(-dz, 0)[0], :, at.c]))
            peer = at.index(at.ahead(dz, 0)[0], at.m)
            forwards.append((here, slab, slab, peer))
        forwards.append((here, slab, slab, at.sibling))
    for dz in range(1, at.planes):
        rest.append((w_out, rows_out.at[at.z], at.index(at.ahead(dz, 0)[0], at.m)))
    forwards += [([], *send) for send in rest]
    for slot, slab in columns:
        forwards.append(([slot], slab, slab, at.sibling))
    partners = [at.index(at.z, m) for m in peers] + [at.sibling]
    partners += [at.index(at.ahead(dz, 0)[0], at.m) for dz in range(1, at.planes)]
    return partners, kept, sends, forwards


def windows(at, ins, outs):
    own, cotangent, rows = ins
    held, cotangent_out, rows_out = outs
    here, before = held.at[1, :, at.c], held.at[0, :, at.c]
    after = at.index(at.ahead(1, 0)[0], at.m)
    prior = at.index(at.ahead(-1, 0)[0], at.m)
    partners, kept, sends, _ = across(0, 1, 0, 0, at, (cotangent,), (cotangent_out,))
    column = rows_out.at[:, at.m]
    kept.append((rows, column))
    sends += [(rows, column, peer) for peer in partners]
    sends = [(own, before, after), (own, here, at.sibling), *sends]
    forwards = [([0], before, before, at.sibling)]
    return [after, prior, at.sibling, *partners], [(own, here), *kept], sends, forwards


def windows_back(at, ins, outs):
    (grads, partial), (grads_out, partial_out) = ins, outs
    after = at.index(at.ahead(1, 0)[0], at.m)
    prior = at.index(at.ahead(-1, 0)[0], at.m)
    partners, kept, sends, _ = across(1, 0, 0, 0, at, (partial,), (partial_out,))
    return [after, prior, *partners], kept, [(grads, grads_out, prior), *sends], []


def across(turned, spread, merged, halves, at, ins, outs):
    kept, sends, partners = [], [], []
    for dm in range(1, CHIPS) if turned + spread else ():
        m = at.ahead(0, dm)[1]
        peer = at.index(at.z, m)
        partners.append(peer)
        for k in range(turned):
            sends.append((ins[k].at[m], outs[k].at[at.m], peer))
        for k in range(turned, turned + spread):
            sends.append((ins[k], outs[k].at[at.m], peer))
    for k in range(turned):
        kept.append((ins[k].at[at.m], outs[k].at[at.m]))
    for k in range(turned, turned + spread):
        kept.append((ins[k], outs[k].at[at.m]))
    if halves + merged:
        partners.append(at.sibling)
    for k in range(turned + spread, turned + spread + merged):
        mine = outs[k].at[(*(slice(None),) * (len(ins[k].shape) - 2), at.c)]
        sends.append((ins[k], mine, at.sibling))
        kept.append((ins[k], mine))
    for k in range(turned + spread + merged, len(ins)):
        lead = (slice(None),) * (len(ins[k].shape) - 3)
        sends.append((ins[k].at[(*lead, 1 - at.c)], outs[k], at.sibling))
    return partners, kept, sends, []


def closing(at, ins, outs):
    grads, vectors, rows = ins[:3]
    grads_out, vectors_out, rows_out = outs[:3]
    kept = [
        (grads.at[at.z, at.m], grads_out.at[at.z, at.m]),
        (vectors.at[at.z, at.m], vectors_out.at[at.z, at.m]),
        (rows.at[at.z], rows_out.at[at.z]),
    ]
    _, kept_in, sends_in, _ = across(len(ins) - 3, 0, 0, 0, at, ins[3:], outs[3:])
    sends = []
    for dz in reversed(range(at.planes)):
        for dm in range(CHIPS):
            if dz or dm:
                z, m = at.ahead(dz, dm)
                peer = at.index(z, m)
                sends.append((grads.at[z, m], grads_out.at[at.z, at.m], peer))
                sends.append((vectors.at[z, m], vectors_out.at[at.z, at.m], peer))
                if dm == 0:
                    sends.append((rows.at[z], rows_out.at[at.z], peer))
    return same_parity(at), kept + kept_in, sends + sends_in, []


def swap(ident, turned=(), spread=(), merged=(), halves=(), after=()):
    outs = [(x.shape, x.dtype) for x in turned]
    outs += [((CHIPS, *x.shape), x.dtype) for x in spread]
    outs += [((*x.shape[:-2], CORES, *x.shape[-2:]), x.dtype) for x in merged]
    outs += [((*x.shape[:-3], *x.shape[-2:]), x.dtype) for x in halves]
    plan = functools.partial(across, len(turned), len(spread), len(merged), len(halves))
    stays = len(turned) + len(spread)
    copies = (CHIPS - 1) * stays + len(halves) + len(merged)
    ins = (*turned, *spread, *merged, *halves)
    return exchange(plan, ins, outs, ident, copies, stays + len(merged), len(halves), after)


def window_of(info_ref):
    step = pl.program_id(0)
    inside = info_ref[step]
    start = pl.multiple_of((CORES * step + info_ref[CHIPS] + 1) * BLOCK, BLOCK)
    row = lax.broadcasted_iota(jnp.int32, (WINDOW, BLOCK), 0)
    query = lax.broadcasted_iota(jnp.int32, (WINDOW, BLOCK), 1)
    slot = MAXB - 1 - lax.shift_right_logical(row, 7)
    column = lax.bitwise_and(row, BLOCK - 1)
    return pl.ds(start, WINDOW), (slot <= inside) & ((slot > 0) | (column <= query))


def contract(a, b, over):
    return lax.dot_general(a, b, (((over[0],), (over[1],)), ((), ())), preferred_element_type=F32)


def attend_kernel(info_ref, q_ref, kv_ref, out_ref, lse_ref):
    span, allowed = window_of(info_ref)
    for head in range(SLOTS):
        part = pl.ds(head * HEAD, HEAD)
        keys = kv_ref[span, part]
        values = kv_ref[span, pl.ds(WIDE + head * HEAD, HEAD)]
        scores = jnp.where(allowed, contract(keys, q_ref[:, part], (1, 1)), -1e30)
        top = jnp.max(scores, axis=0, keepdims=True)
        powers = jnp.exp(scores - top)
        total = jnp.sum(powers, axis=0, keepdims=True)
        probs = (powers * (1.0 / total)).astype(BF16)
        out_ref[:, part] = contract(probs, values, (0, 0)).astype(BF16)
        lse_ref[0, pl.ds(head, 1), :] = top + jnp.log(total)


def attend_back_kernel(info_ref, q_ref, kv_ref, grad_ref, lse_ref, grad_q_ref, grad_kv_ref):
    @pl.when(pl.program_id(0) == 0)
    def _():
        grad_kv_ref[...] = jnp.zeros_like(grad_kv_ref)

    span, allowed = window_of(info_ref)
    for head in range(SLOTS):
        part = pl.ds(head * HEAD, HEAD)
        part_v = pl.ds(WIDE + head * HEAD, HEAD)
        keys, values = kv_ref[span, part], kv_ref[span, part_v]
        query, grad = q_ref[:, part], grad_ref[:, part]
        scores = jnp.where(allowed, contract(keys, query, (1, 1)), -1e30)
        probs = jnp.exp(scores - lse_ref[0, pl.ds(head, 1), :])
        grad_probs = contract(values, grad, (1, 1))
        delta = jnp.sum(probs * grad_probs, axis=0, keepdims=True)
        grad_scores = (probs * (grad_probs - delta)).astype(BF16)
        grad_q_ref[:, part] = contract(grad_scores, keys, (0, 0))
        grad_kv_ref[span, part] += contract(grad_scores, query, (1, 0))
        grad_kv_ref[span, part_v] += contract(probs.astype(BF16), grad, (1, 0))


def block_rows(width):
    return pl.BlockSpec((BLOCK, width), lambda i: (i, 0))


def whole_of(x):
    return pl.BlockSpec(x.shape, lambda i: (0,) * len(x.shape))


LSE = pl.BlockSpec((1, 8, BLOCK), lambda i: (i, 0, 0))
SMEM = pl.BlockSpec(memory_space=pltpu.SMEM)


def attend_heads(info, query, held):
    return pl.pallas_call(
        attend_kernel,
        grid=(CHIPS,),
        in_specs=[SMEM, block_rows(WIDE), whole_of(held)],
        out_specs=(block_rows(WIDE), LSE),
        out_shape=(
            jax.ShapeDtypeStruct(query.shape, BF16),
            jax.ShapeDtypeStruct((CHIPS, 8, BLOCK), F32),
        ),
        cost_estimate=COST,
        compiler_params=pltpu.CompilerParams(vmem_limit_bytes=40 * 2**20),
    )(info, query, held)


def attend_heads_back(info, query, held, grad, lse):
    return pl.pallas_call(
        attend_back_kernel,
        grid=(CHIPS,),
        in_specs=[SMEM, block_rows(WIDE), whole_of(held), block_rows(WIDE), LSE],
        out_specs=(block_rows(WIDE), whole_of(held)),
        out_shape=(
            jax.ShapeDtypeStruct(query.shape, F32),
            jax.ShapeDtypeStruct(held.shape, F32),
        ),
        cost_estimate=COST,
        compiler_params=pltpu.CompilerParams(vmem_limit_bytes=48 * 2**20),
    )(info, query, held, grad, lse)


def dot(a, b):
    return jnp.dot(a, b, preferred_element_type=F32)


def compute(body, ins, outs, scratch=(), small=()):
    vmem = pl.BlockSpec(memory_space=pltpu.VMEM)
    return pl.pallas_call(
        body,
        in_specs=[SMEM] * len(small) + [vmem] * len(ins),
        out_specs=tuple([vmem] * len(outs)),
        out_shape=tuple(jax.ShapeDtypeStruct(shape, dtype) for shape, dtype in outs),
        scratch_shapes=[pltpu.VMEM(shape, dtype) for shape, dtype in scratch],
        cost_estimate=COST,
        compiler_params=pltpu.CompilerParams(vmem_limit_bytes=56 * 2**20),
    )(*small, *ins)


def pieces(ref):
    planes, chips, cores, rows, _ = ref.shape
    for j in range(planes * chips * cores):
        yield (j // (chips * cores), j // cores % chips, j % cores), pl.ds(j * rows, rows)


def normed(values):
    average = jnp.mean(values, axis=-1, keepdims=True)
    centred = values - average
    inv_std = lax.rsqrt(jnp.mean(centred * centred, axis=-1, keepdims=True) + EPS)
    return centred * inv_std, inv_std


def column_sum(values):
    return jnp.sum(values, axis=0, keepdims=True)


HALF = CHIPS // 2


def project_kernel(tokens, parts, vec, bias_kv, bias_q, normed_out, kv_out, q_out, weight):
    for at, rows in pieces(parts):
        weight[rows, :] = parts[at]
    for i in range(2):
        values = tokens[pl.ds(i * HALF, HALF)].astype(F32).reshape(HALF * BLOCK, -1)
        hat, _ = normed(values)
        rows = (hat * vec[0:1, :] + vec[1:2, :]).astype(BF16)
        normed_out[pl.ds(i * HALF * BLOCK, HALF * BLOCK), :] = rows
        projected = dot(rows, weight[...])
        kv = (projected[:, : 2 * WIDE] + bias_kv[...]).astype(BF16)
        kv_out[pl.ds(i * HALF, HALF)] = kv.reshape(HALF, BLOCK, 2 * WIDE)
        query = HEAD ** (-0.5) * (projected[:, 2 * WIDE :] + bias_q[...])
        q_out[pl.ds(i * HALF * BLOCK, HALF * BLOCK), :] = query.astype(BF16)


def project_back_kernel(
    grad_q, grad_kv, grad_before, tokens, rows_in, weight, vec, grad_out, parts, sums, sums_wide, grads, total
):
    for i in range(2):
        span = pl.ds(i * HALF * BLOCK, HALF * BLOCK)
        blocks = pl.ds(i * HALF, HALF)
        both = grad_kv[blocks] + grad_before[blocks].astype(F32)
        both = both.reshape(HALF * BLOCK, 2 * WIDE)
        query = HEAD ** (-0.5) * grad_q[span, :]
        grads[span, : 2 * WIDE] = both.astype(BF16)
        grads[span, 2 * WIDE :] = query.astype(BF16)
        back = contract(grads[span, :], weight[...], (1, 1))
        hat, _ = normed(tokens[blocks].astype(F32).reshape(HALF * BLOCK, -1))
        new = (column_sum(back * hat), column_sum(back), column_sum(both), column_sum(query))
        if i:
            old = (sums[0:1, :], sums[1:2, :], sums_wide[0:1, : 2 * WIDE], sums_wide[0:1, 2 * WIDE :])
            new = tuple(a + b for a, b in zip(old, new))
        sums[0:1, :], sums[1:2, :] = new[:2]
        sums_wide[0:1, : 2 * WIDE], sums_wide[0:1, 2 * WIDE :] = new[2:]
        grad_out[blocks] = back.astype(BF16).reshape(HALF, BLOCK, -1)
    total[...] = contract(rows_in[...], grads[...], (0, 0))
    for at, rows in pieces(parts):
        parts[at] = total[rows, :].astype(BF16)


def head_rows():
    for s in range(CHIPS):
        yield s, s * WIDE, min(WIDE, D - s * WIDE)


def output_kernel(attended, parts, tokens, vec, residual, normed_out, weight):
    for at, rows in pieces(parts):
        weight[rows, :] = parts[at]
    values = tokens[...].astype(F32) + vec[4:5, :]
    for s, first, size in head_rows():
        values += dot(attended[s, :, :size], weight[pl.ds(first, size), :])
    residual[...] = values
    hat, _ = normed(values)
    normed_out[...] = (hat * vec[5:6, :] + vec[6:7, :]).astype(BF16)


def output_back_kernel(
    filled, grads_in, residual, cotangent, attended, weight, vec, grad_residual, heads, parts, sums, total
):
    row = lax.broadcasted_iota(jnp.int32, cotangent.shape, 0)
    cot = jnp.where(row < filled[0], cotangent[...].astype(F32), 0.0)
    grad = grads_in[0].astype(F32)
    for s in range(1, CHIPS):
        grad += grads_in[s].astype(F32)
    hat, inv_std = normed(residual[...])
    back = cot + norm_back(grad, hat, inv_std, vec[5:6, :])
    grad_residual[...] = back
    sums[0:1, :] = column_sum(grad * hat)
    sums[1:2, :] = column_sum(grad)
    sums[2:3, :] = column_sum(back)
    sums[3:4, :] = column_sum(cot)
    rounded = back.astype(BF16)
    for s, first, size in head_rows():
        if size < WIDE:
            heads[s] = jnp.zeros(heads.shape[1:], BF16)
        part = contract(rounded, weight[pl.ds(first, size), :], (1, 1))
        heads[s, :, :size] = part.astype(BF16)
        total[pl.ds(first, size), :] = contract(attended[s, :, :size], rounded, (0, 0))
    for at, rows in pieces(parts):
        parts[at] = total[rows, :].astype(BF16)


def local_split(tokens, seq_lengths, w_qkv, w_out, w_up, w_down, vectors, cotangent):
    count = lax.axis_size("dp")
    planes = count // SPAN
    me = lax.axis_index("dp")
    z, m, c = me // SPAN, (me // CORES) % CHIPS, me % CORES
    along_z = [[p + SPAN * k for k in range(planes)] for p in range(SPAN)]
    in_plane = [
        [SPAN * k + CORES * i + core for i in range(CHIPS)]
        for k in range(planes)
        for core in range(CORES)
    ]

    def gather_z(x):
        return lax.all_gather(x, "dp", axis_index_groups=along_z)

    def scatter(x, groups, axis):
        return lax.psum_scatter(
            x, "dp", axis_index_groups=groups, scatter_dimension=axis, tiled=False
        )

    def own(x, axis):
        return lax.dynamic_index_in_dim(x, c, axis, keepdims=False)

    rows_in = D // count
    hidden = FF // CHIPS
    share = hidden // planes
    rows_ff = FF // count
    heads_of = w_qkv.reshape(rows_in, 3, D)
    heads_of = jnp.concatenate([heads_of[:, 1:], heads_of[:, :1]], axis=1)
    heads_of = jnp.pad(heads_of, ((0, 0), (0, 0), (0, CHIPS * WIDE - D)))
    heads_of = heads_of.reshape(rows_in, 3, CHIPS, WIDE).transpose(2, 0, 1, 3)
    heads_of = heads_of.reshape(CHIPS, rows_in, 3 * WIDE)
    up_slices = w_up.reshape(rows_in, planes, CHIPS, share).transpose(2, 0, 1, 3)
    up_slices = up_slices.reshape(CHIPS, rows_in, hidden)
    vec_own = vectors.reshape(1, -1)
    tokens4, weight_qkv, up_part, vecs, out_part = exchange(
        opening,
        (tokens, heads_of, up_slices, vec_own, w_out.reshape(rows_in, D)),
        [
            ((CHIPS, BLOCK, D), BF16),
            ((planes, CHIPS, CORES, rows_in, 3 * WIDE), BF16),
            (up_slices.shape, BF16),
            ((planes, CHIPS, CORES, *vec_own.shape), BF16),
            ((planes, rows_in, D), BF16),
        ],
        1,
        4 * (CHIPS - 1) + 5 * (planes - 1) + 2,
        5,
    )
    w_down, weight_qkv = lax.optimization_barrier((w_down, weight_qkv))
    down_part = gather_z(w_down.reshape(rows_ff, D))

    blocks = SPAN * z + CORES * jnp.arange(CHIPS, dtype=jnp.int32) + c
    inside, filled = block_layout(seq_lengths, blocks)
    valid4 = (jnp.arange(BLOCK, dtype=jnp.int32)[None, :] < filled[:, None]).reshape(-1, 1)
    filled_own = lax.dynamic_index_in_dim(filled, m, 0, keepdims=False)
    valid = (jnp.arange(BLOCK, dtype=jnp.int32) < filled_own)[:, None]
    info = jnp.concatenate([inside, jnp.reshape(c, (1,))]).astype(jnp.int32)

    vec = vecs.reshape(-1)[: 12 * D].reshape(12, D).astype(F32)

    def head_bias(row):
        padded = jnp.pad(vec[row], (0, CHIPS * WIDE - D)).reshape(CHIPS, WIDE)
        return lax.dynamic_index_in_dim(padded, m, 0, keepdims=False)

    bias_up = vec[8:12].reshape(planes, CHIPS, share)
    bias_up = lax.dynamic_index_in_dim(bias_up, m, 1, keepdims=False).reshape(hidden)
    bias_kv = jnp.concatenate([jnp.zeros((WIDE,), F32), head_bias(3)])
    normed_attn, key_value, query, weight_qkv = compute(
        project_kernel,
        (tokens4, weight_qkv, vec, bias_kv[None], head_bias(2)[None]),
        [
            ((CHIPS * BLOCK, D), BF16),
            ((CHIPS, BLOCK, 2 * WIDE), BF16),
            ((CHIPS * BLOCK, WIDE), BF16),
            ((D, 3 * WIDE), BF16),
        ],
    )
    held, cotangent4, out_part = exchange(
        windows,
        (key_value, cotangent, out_part),
        [
            ((2, CHIPS, CORES, BLOCK, 2 * WIDE), BF16),
            ((CHIPS, BLOCK, D), BF16),
            ((planes, CHIPS, rows_in, D), BF16),
        ],
        2,
        3 + 2 * (CHIPS - 1),
        3,
    )
    up_part, held = lax.optimization_barrier((up_part, held))
    up_part = gather_z(up_part)
    held = held.reshape(2 * SPAN * BLOCK, 2 * WIDE)
    attended_heads, lse = attend_heads(info, query, held)
    attended_own, weight_out = swap(
        3, turned=(attended_heads.reshape(CHIPS, BLOCK, WIDE),), merged=(out_part,)
    )
    residual, normed_mlp, weight_out = compute(
        output_kernel,
        (attended_own, weight_out, tokens, vec),
        [((BLOCK, D), F32), ((BLOCK, D), BF16), ((D, D), BF16)],
    )
    mlp4, weight_up, weight_down = swap(
        4, spread=(normed_mlp,), merged=(up_part, down_part)
    )
    mlp4 = mlp4.reshape(CHIPS * BLOCK, D)

    weight_up = weight_up.reshape(D, hidden)
    weight_down = weight_down.reshape(hidden, D)
    up_pre = dot(mlp4, weight_up) + bias_up
    normal_cdf = 0.5 * (1.0 + lax.erf(up_pre * 2.0 ** (-0.5)))
    activated = (up_pre * normal_cdf).astype(BF16)
    result_part = dot(activated, weight_down).astype(BF16).reshape(CHIPS, BLOCK, D)
    cot4 = jnp.where(valid4, cotangent4.reshape(CHIPS * BLOCK, D), 0)
    grad_act = contract(cot4, weight_down, (1, 1))
    normal_pdf = jnp.exp(-0.5 * up_pre * up_pre) * (2.0 * jnp.pi) ** (-0.5)
    grad_pre = grad_act * (normal_cdf + up_pre * normal_pdf)
    grad_pre_bf = grad_pre.astype(BF16)
    grad_mlp_part = contract(grad_pre_bf, weight_up, (1, 1)).astype(BF16)
    grad_mlp_part = grad_mlp_part.reshape(CHIPS, BLOCK, D)
    grad_bias_up = jnp.sum(grad_pre, axis=0)
    grad_down = contract(activated, cot4, (0, 0)).astype(BF16)
    grad_up = contract(mlp4, grad_pre_bf, (0, 0)).astype(BF16)
    grad_down = grad_down.reshape(planes, CORES, rows_ff, D)
    grad_up = grad_up.reshape(planes, CHIPS, CORES, rows_in, hidden)
    grad_mlp, down_half, up_half = swap(5, turned=(grad_mlp_part,), halves=(grad_down, grad_up))

    def joined(mine, other):
        return (mine.astype(F32) + other.astype(F32)).astype(BF16)

    grad_down, grad_up, grad_mlp = lax.optimization_barrier(
        (joined(own(grad_down, 1), down_half), joined(own(grad_up, 2), up_half), grad_mlp)
    )
    grad_down = scatter(grad_down, along_z, 0)
    grad_up = scatter(grad_up, along_z, 0)
    shard_down = grad_down.astype(F32).reshape(w_down.shape)

    grad_residual, grad_attended, grad_out, sums_out = compute(
        output_back_kernel,
        (grad_mlp, residual, cotangent, attended_own, weight_out, vec),
        [
            ((BLOCK, D), F32),
            ((CHIPS, BLOCK, WIDE), BF16),
            ((planes, CHIPS, CORES, rows_in, D), BF16),
            ((4, D), F32),
        ],
        [((D, D), F32)],
        (jnp.reshape(filled_own, (1,)),),
    )
    grad_heads, out_half = swap(6, turned=(grad_attended,), halves=(grad_out,))
    grad_out = joined(own(grad_out, 2), out_half).transpose(1, 0, 2, 3)

    grad_query, grad_held = attend_heads_back(
        info, query, held, grad_heads.reshape(CHIPS * BLOCK, WIDE), lse
    )
    grad_held = grad_held.reshape(2, CHIPS, CORES, BLOCK, 2 * WIDE)
    out_parts, held_half = swap(
        7, turned=(grad_out,), halves=(grad_held.astype(BF16),), after=(grad_down,)
    )
    grad_out = jnp.sum(out_parts.astype(F32), axis=0).astype(BF16)
    grad_held = own(grad_held, 2) + held_half.astype(F32)
    grad_before, result = exchange(
        windows_back,
        (grad_held[0].astype(BF16), result_part),
        [((CHIPS, BLOCK, 2 * WIDE), BF16), (result_part.shape, BF16)],
        8,
        1 + CHIPS - 1,
        1,
    )
    result = residual + jnp.sum(result.astype(F32), axis=0) + vec[7]
    out_block = jnp.where(valid, result, 0.0).astype(BF16)

    grad_attn_part, grad_qkv, sums_in, sums_wide = compute(
        project_back_kernel,
        (grad_query, grad_held[1], grad_before, tokens4, normed_attn, weight_qkv, vec),
        [
            ((CHIPS, BLOCK, D), BF16),
            ((planes, CHIPS, CORES, rows_in, 3 * WIDE), BF16),
            ((2, D), F32),
            ((1, 3 * WIDE), F32),
        ],
        [((CHIPS * BLOCK, 3 * WIDE), BF16), ((D, 3 * WIDE), F32)],
    )

    def placed(values, width, length):
        start = jnp.zeros((CHIPS * width,), F32)
        return lax.dynamic_update_slice(start, values, (m * width,))[:length]

    placed_up = jnp.where(
        jnp.arange(CHIPS)[None, :, None] == m, grad_bias_up.reshape(planes, 1, share), 0.0
    )
    rows = [
        sums_in.reshape(-1),
        placed(sums_wide[0, 2 * WIDE :], WIDE, D),
        placed(sums_wide[0, WIDE : 2 * WIDE], WIDE, D),
        sums_out[2],
        sums_out[:2].reshape(-1),
        sums_out[3],
        placed_up.reshape(FF),
    ]
    grad_vec = pad_flat(jnp.concatenate(rows), vectors.shape[0] * count)
    grad_vec = grad_vec.reshape(planes, CHIPS, CORES, 1, -1)
    qkv_half, vec_half = swap(9, halves=(grad_qkv, grad_vec), after=(grad_up,))
    grad_qkv = joined(own(grad_qkv, 2), qkv_half)
    grad_vec = own(grad_vec, 2) + vec_half
    ins = (
        grad_qkv,
        grad_vec,
        grad_out,
        grad_attn_part,
        grad_up,
    )
    grad_qkv, grad_vec, grad_out, grad_attn, grad_up = exchange(
        closing,
        ins,
        [(x.shape, x.dtype) for x in ins],
        10,
        2 * (planes * CHIPS - 1) + planes - 1 + 2 * (CHIPS - 1),
        5,
    )
    shard_vec = jnp.sum(grad_vec, axis=(0, 1)).reshape(-1)
    shard_qkv = jnp.sum(grad_qkv.astype(F32), axis=0).reshape(CHIPS, rows_in, 3, WIDE)
    shard_qkv = shard_qkv.transpose(1, 2, 0, 3).reshape(rows_in, 3, CHIPS * WIDE)[:, :, :D]
    shard_qkv = jnp.concatenate([shard_qkv[:, 2:], shard_qkv[:, :2]], axis=1)
    shard_qkv = shard_qkv.reshape(-1)
    shard_up = grad_up.astype(F32).reshape(CHIPS, rows_in, planes, share)
    shard_up = shard_up.transpose(1, 2, 0, 3).reshape(-1)
    shard_out = jnp.sum(grad_out.astype(F32), axis=0).reshape(-1)
    hat_own, inv_own = normed(tokens.astype(F32))
    grad_normed_attn = jnp.sum(grad_attn.astype(F32), axis=0)
    grad_tokens = grad_residual + norm_back(grad_normed_attn, hat_own, inv_own, vec[0])
    return (out_block, grad_tokens, shard_qkv, shard_out, shard_up, shard_down, shard_vec)


def local(*args):
    count = lax.axis_size("dp")
    _, _, w_qkv, w_out, w_up, w_down, vectors, _ = args
    fits = count == SPAN * CHIPS and vectors.shape[0] * count >= 12 * D
    for shard, rows, cols in ((w_qkv, D, 3 * D), (w_out, D, D), (w_up, D, FF), (w_down, FF, D)):
        fits = fits and whole_rows(shard, rows, cols)
    return local_split(*args) if fits else local_gathered(*args)


def solution(mesh):
    in_specs = (P("dp", None), P(), P("dp"), P("dp"), P("dp"), P("dp"), P("dp"), P("dp", None))
    out_specs = (P("dp", None), P("dp", None), P("dp"), P("dp"), P("dp"), P("dp"), P("dp"))
    return jax.shard_map(local, mesh=mesh, in_specs=in_specs, out_specs=out_specs, check_vma=False)
```

```python
import functools

import jax
import jax.numpy as jnp
from jax import lax
from jax.experimental import pallas as pl
from jax.experimental.pallas import tpu as pltpu
from jax.experimental.layout import Layout, with_layout_constraint
from jax.sharding import PartitionSpec as P

D = 1088
HEADS = 17
HEAD = 64
FF = 4352
BLOCK = 128
MAXB = 8


EPS = 1e-05
WIRE = jnp.bfloat16


def shifted(value, axis, steps):
    count = lax.axis_size(axis)
    first, last = (max(0, -steps), min(count, count - steps))
    return lax.ppermute(value, axis, [(source, source + steps) for source in range(first, last)])


def block_layout(seq_lengths, block_ids):
    counts = (seq_lengths + BLOCK - 1) // BLOCK
    order = jnp.arange(counts.shape[0])
    end_pos = jnp.sum(jnp.where(order[None, :] <= order[:, None], counts[None, :], 0), axis=1)
    start_pos = end_pos - counts
    owns_block = (block_ids[:, None] >= start_pos[None, :]) & (
        block_ids[:, None] < end_pos[None, :]
    )
    first_blk = jnp.sum(jnp.where(owns_block, start_pos[None, :], 0), axis=1)
    seq_len = jnp.sum(jnp.where(owns_block, seq_lengths[None, :], 0), axis=1)
    inside = block_ids - first_blk
    filled = jnp.clip(seq_len - inside * BLOCK, 0, BLOCK)
    return (inside, filled)


def window_mask(inside):
    row_ids = jnp.arange(BLOCK, dtype=jnp.int32)[:, None]
    col_ids = jnp.arange(MAXB * BLOCK, dtype=jnp.int32)[None, :]
    slot_ids = col_ids // BLOCK
    return (slot_ids <= inside) & ((slot_ids > 0) | (col_ids <= row_ids))


def layer_norm(values, gain_vec, bias_vec):
    average = jnp.mean(values, axis=-1, keepdims=True)
    centred = values - average
    variance = jnp.mean(centred * centred, axis=-1, keepdims=True)
    inv_std = lax.rsqrt(variance + EPS)
    normalized = centred * inv_std
    return (normalized * gain_vec + bias_vec, normalized, inv_std)


def norm_back(grad_out, normalized, inv_std, gain_vec):
    grad_hat = grad_out * gain_vec
    first_mean = jnp.mean(grad_hat, axis=-1, keepdims=True)
    second_mean = jnp.mean(grad_hat * normalized, axis=-1, keepdims=True)
    return inv_std * (grad_hat - first_mean - normalized * second_mean)


def split_heads(matrix):
    return matrix.reshape(matrix.shape[0], HEADS, HEAD).transpose(1, 0, 2)


def join_heads(matrix):
    return matrix.transpose(1, 0, 2).reshape(matrix.shape[1], HEADS * HEAD)


def head_forward(query, keys, values, allowed):
    scores = jnp.dot(query, keys.T, preferred_element_type=jnp.float32)
    scores = jnp.where(allowed, scores, -1e30)
    row_max = jnp.max(scores, axis=-1)
    row_total = jnp.sum(jnp.exp(scores - row_max[:, None]), axis=-1)
    log_sums = row_max + jnp.log(row_total)
    prob_bf = jnp.where(allowed, jnp.exp(scores - log_sums[:, None]), 0.0).astype(jnp.bfloat16)
    output = jnp.dot(prob_bf, values, preferred_element_type=jnp.float32).astype(jnp.bfloat16)
    return (output, log_sums)


def head_backward(query, keys, values, output, grad_output, log_sums, allowed):
    scores = jnp.dot(query, keys.T, preferred_element_type=jnp.float32)
    probs = jnp.where(allowed, jnp.exp(scores - log_sums[:, None]), 0.0)
    prob_bf = probs.astype(jnp.bfloat16)
    grad_value = jnp.dot(prob_bf.T, grad_output, preferred_element_type=jnp.float32)
    grad_prob = jnp.dot(grad_output, values.T, preferred_element_type=jnp.float32)
    row_delta = jnp.sum(grad_output.astype(jnp.float32) * output.astype(jnp.float32), axis=-1)
    grad_score = (probs * (grad_prob - row_delta[:, None])).astype(jnp.bfloat16)
    grad_query = jnp.dot(grad_score, keys, preferred_element_type=jnp.float32)
    grad_key = jnp.dot(grad_score.T, query, preferred_element_type=jnp.float32)
    return (grad_query, grad_key, grad_value)


def attend(query, keys, values, allowed):
    outputs, log_sums = jax.vmap(head_forward, (0, 0, 0, None))(
        split_heads(query), split_heads(keys), split_heads(values), allowed
    )
    return (join_heads(outputs), log_sums)


def attend_back(query, keys, values, output, grad_output, log_sums, allowed):
    grad_query, grad_key, grad_value = jax.vmap(head_backward, (0, 0, 0, 0, 0, 0, None))(
        split_heads(query),
        split_heads(keys),
        split_heads(values),
        split_heads(output),
        split_heads(grad_output),
        log_sums,
        allowed,
    )
    return (join_heads(grad_query), join_heads(grad_key), join_heads(grad_value))


def whole_rows(shard, rows, cols):
    count = lax.axis_size("dp")
    return shard.shape[0] % cols == 0 and shard.shape[0] * count == rows * cols


def gather_matrix(shard, rows, cols):
    if whole_rows(shard, rows, cols):
        return lax.all_gather(shard.reshape(-1, cols), "dp", axis=0, tiled=True)
    flat = lax.all_gather(shard, "dp", axis=0, tiled=True)
    return flat[: rows * cols].reshape(rows, cols)


def scatter_matrix(grad, shard):
    rows, cols = grad.shape
    grad = with_layout_constraint(grad.astype(WIRE), Layout((0, 1)))
    if whole_rows(shard, rows, cols):
        split = grad.reshape(lax.axis_size("dp"), -1, cols)
        own = lax.psum_scatter(split, "dp", scatter_dimension=0, tiled=False)
        return own.reshape(-1).astype(jnp.float32)
    flat = pad_flat(grad, shard.shape[0] * lax.axis_size("dp"))
    return lax.psum_scatter(flat, "dp", scatter_dimension=0, tiled=True).astype(jnp.float32)


def pad_flat(matrix, length):
    flat = matrix.reshape(-1)
    return jnp.concatenate([flat, jnp.zeros((length - flat.shape[0],), flat.dtype)])


def local_gathered(tokens, seq_lengths, w_qkv, w_out, w_up, w_down, vectors, cotangent):
    device_pos = lax.axis_index("dp")
    inside_all, filled_all = block_layout(seq_lengths, jnp.reshape(device_pos, (1,)))
    inside = inside_all[0]
    valid = jnp.arange(BLOCK, dtype=jnp.int32) < filled_all[0]
    allowed = window_mask(inside)
    vec_length = vectors.shape[0] * lax.axis_size("dp")
    vector_rows = lax.all_gather(vectors, "dp", axis=0, tiled=True)
    vector_rows = vector_rows[: 12 * D].reshape(12, D).astype(jnp.float32)
    weight_qkv = gather_matrix(w_qkv, D, 3 * D)
    weight_out = gather_matrix(w_out, D, D)
    weight_up = gather_matrix(w_up, D, FF)
    weight_down = gather_matrix(w_down, FF, D)
    bias_up = vector_rows[8:12].reshape(FF)
    query_scale = HEAD ** (-0.5)
    inputs = tokens.astype(jnp.float32)
    normed_attn, hat_one, inv_one = layer_norm(inputs, vector_rows[0], vector_rows[1])
    normed_attn = normed_attn.astype(jnp.bfloat16)
    projected = jnp.dot(normed_attn, weight_qkv, preferred_element_type=jnp.float32)
    query = (query_scale * (projected[:, :D] + vector_rows[2])).astype(jnp.bfloat16)
    keys = projected[:, D : 2 * D].astype(jnp.bfloat16)
    values = (projected[:, 2 * D :] + vector_rows[3]).astype(jnp.bfloat16)
    key_value = jnp.stack([keys, values])
    pieces = [key_value]
    for offset in range(1, MAXB):
        pieces.append(shifted(key_value, "dp", offset))
    window_kv = jnp.stack(pieces)
    window_k = window_kv[:, 0].reshape(MAXB * BLOCK, D)
    window_v = window_kv[:, 1].reshape(MAXB * BLOCK, D)
    attended, log_sums = attend(query, window_k, window_v, allowed)
    residual = (
        inputs + jnp.dot(attended, weight_out, preferred_element_type=jnp.float32) + vector_rows[4]
    )
    normed_mlp, hat_two, inv_two = layer_norm(residual, vector_rows[5], vector_rows[6])
    normed_mlp = normed_mlp.astype(jnp.bfloat16)
    up_pre = jnp.dot(normed_mlp, weight_up, preferred_element_type=jnp.float32) + bias_up
    normal_cdf = 0.5 * (1.0 + lax.erf(up_pre * 2.0 ** (-0.5)))
    activated = (up_pre * normal_cdf).astype(jnp.bfloat16)
    result = (
        residual
        + jnp.dot(activated, weight_down, preferred_element_type=jnp.float32)
        + vector_rows[7]
    )
    out_block = jnp.where(valid[:, None], result, 0.0).astype(jnp.bfloat16)
    cot_rows = jnp.where(valid[:, None], cotangent.astype(jnp.float32), 0.0)
    cot_bf = cot_rows.astype(jnp.bfloat16)
    grad_down = jnp.dot(activated.T, cot_bf, preferred_element_type=jnp.float32)
    grad_bias_down = jnp.sum(cot_rows, axis=0)
    grad_act = jnp.dot(cot_bf, weight_down.T, preferred_element_type=jnp.float32)
    normal_pdf = jnp.exp(-0.5 * up_pre * up_pre) * (2.0 * jnp.pi) ** (-0.5)
    grad_pre = grad_act * (normal_cdf + up_pre * normal_pdf)
    grad_pre_bf = grad_pre.astype(jnp.bfloat16)
    grad_up = jnp.dot(normed_mlp.T, grad_pre_bf, preferred_element_type=jnp.float32)
    grad_bias_up = jnp.sum(grad_pre, axis=0)
    grad_normed_mlp = jnp.dot(grad_pre_bf, weight_up.T, preferred_element_type=jnp.float32)
    grad_gain_two = jnp.sum(grad_normed_mlp * hat_two, axis=0)
    grad_bias_two = jnp.sum(grad_normed_mlp, axis=0)
    grad_residual = cot_rows + norm_back(grad_normed_mlp, hat_two, inv_two, vector_rows[5])
    grad_bias_out = jnp.sum(grad_residual, axis=0)
    grad_res_bf = grad_residual.astype(jnp.bfloat16)
    grad_out = jnp.dot(attended.T, grad_res_bf, preferred_element_type=jnp.float32)
    grad_attended = jnp.dot(grad_res_bf, weight_out.T, preferred_element_type=jnp.float32).astype(
        jnp.bfloat16
    )
    grad_down, grad_up, grad_out, grad_attended = lax.optimization_barrier(
        (grad_down.astype(WIRE), grad_up.astype(WIRE), grad_out.astype(WIRE), grad_attended)
    )
    shard_down = scatter_matrix(grad_down, w_down)
    shard_up = scatter_matrix(grad_up, w_up)
    shard_out = scatter_matrix(grad_out, w_out)
    grad_query, grad_key, grad_value = attend_back(
        query, window_k, window_v, attended, grad_attended, log_sums, allowed
    )
    grad_query, grad_key, grad_value, shard_down = lax.optimization_barrier(
        (grad_query, grad_key, grad_value, shard_down)
    )
    window_grads = jnp.stack(
        [grad_key.reshape(MAXB, BLOCK, D), grad_value.reshape(MAXB, BLOCK, D)], axis=1
    )
    sent_grads = window_grads.astype(WIRE)
    own_grads = window_grads[0]
    for offset in range(1, MAXB):
        own_grads = own_grads + shifted(sent_grads[offset], "dp", -offset).astype(jnp.float32)
    grad_query = query_scale * grad_query
    grad_project = jnp.concatenate([grad_query, own_grads[0], own_grads[1]], axis=1).astype(
        jnp.bfloat16
    )
    grad_project, shard_up, shard_out = lax.optimization_barrier(
        (grad_project, shard_up, shard_out)
    )
    grad_bias_q = jnp.sum(grad_query, axis=0)
    grad_bias_v = jnp.sum(own_grads[1], axis=0)
    grad_qkv = jnp.dot(normed_attn.T, grad_project, preferred_element_type=jnp.float32)
    grad_normed_attn = jnp.dot(grad_project, weight_qkv.T, preferred_element_type=jnp.float32)
    grad_gain_one = jnp.sum(grad_normed_attn * hat_one, axis=0)
    grad_bias_one = jnp.sum(grad_normed_attn, axis=0)
    grad_tokens = grad_residual + norm_back(grad_normed_attn, hat_one, inv_one, vector_rows[0])
    grad_vectors = jnp.concatenate(
        [
            jnp.stack(
                [
                    grad_gain_one,
                    grad_bias_one,
                    grad_bias_q,
                    grad_bias_v,
                    grad_bias_out,
                    grad_gain_two,
                    grad_bias_two,
                    grad_bias_down,
                ]
            ),
            grad_bias_up.reshape(4, D),
        ],
        axis=0,
    )
    shard_qkv = scatter_matrix(grad_qkv, w_qkv)
    shard_vec = lax.psum_scatter(
        pad_flat(grad_vectors, vec_length), "dp", scatter_dimension=0, tiled=True
    )
    return (out_block, grad_tokens, shard_qkv, shard_out, shard_up, shard_down, shard_vec)


CORES = 2
CHIPS = 4
SPAN = CORES * CHIPS
SLOTS = -(-HEADS // CHIPS)
WIDE = SLOTS * HEAD
WINDOW = MAXB * BLOCK
MESH = pl.DeviceIdType.MESH
HBM = pl.BlockSpec(memory_space=pl.ANY)
F32 = jnp.float32
COST = pl.CostEstimate(flops=0, transcendentals=0, bytes_accessed=48 * 2**20)
BF16 = jnp.bfloat16


class Place:
    def __init__(self):
        self.me = lax.axis_index("dp")
        self.planes = lax.axis_size("dp") // SPAN
        self.z = self.me // SPAN
        self.m = lax.rem(self.me // CORES, CHIPS)
        self.c = lax.rem(self.me, CORES)
        self.sibling = self.me + 1 - 2 * self.c

    def index(self, z, m):
        return z * SPAN + m * CORES + self.c

    def ahead(self, dz, dm):
        return (
            lax.rem(self.z + (dz + self.planes) % self.planes, self.planes),
            lax.rem(self.m + (dm + CHIPS) % CHIPS, CHIPS),
        )


def exchange_body(plan, n_in, n_out, n_after, *refs):
    ins, refs = refs[:n_in], refs[n_in + n_after :]
    outs, (send_sem, recv_sem, local_sem) = refs[:n_out], refs[n_out:]
    partners, kept, sends, forwards = plan(Place(), ins, outs)
    barrier = pltpu.get_barrier_semaphore()
    for partner in partners:
        pl.semaphore_signal(barrier, inc=1, device_id=(partner,), device_id_type=MESH)
    pl.semaphore_wait(barrier, len(partners))

    def remote(slot, source, target, partner):
        return pltpu.make_async_remote_copy(
            src_ref=source,
            dst_ref=target,
            send_sem=send_sem.at[slot],
            recv_sem=recv_sem.at[slot],
            device_id=(partner,),
            device_id_type=MESH,
        )

    going = [(remote(slot, *send), None, None) for slot, send in enumerate(sends)]
    for copy, _, _ in going:
        copy.start()

    def do(condition, action):
        if condition is None:
            action()
        else:
            pl.when(condition)(action)
    staying = [
        pltpu.make_async_copy(source, target, local_sem.at[slot])
        for slot, (source, target) in enumerate(kept)
    ]
    for copy in staying:
        copy.start()
    landed = set()
    if forwards:
        for copy in staying:
            copy.wait()
    for triggers, source, target, partner, *conditions in forwards:
        for trigger in triggers:
            if trigger not in landed:
                copy, _, receives = going[trigger]
                do(receives, copy.wait_recv)
                landed.add(trigger)
        copy = remote(len(going), source, target, partner)
        sends_if, receives_if = conditions or (None, None)
        going.append((copy, sends_if, receives_if))
        do(sends_if, copy.start)
    for slot, (copy, sends_if, receives_if) in enumerate(going):
        do(sends_if, copy.wait_send)
        if slot not in landed:
            do(receives_if, copy.wait_recv)
    if not forwards:
        for copy in staying:
            copy.wait()


def exchange(plan, ins, outs, ident, copies, stays, far=0, after=()):
    return pl.pallas_call(
        functools.partial(exchange_body, plan, len(ins), len(outs), len(after)),
        out_shape=tuple(jax.ShapeDtypeStruct(shape, dtype) for shape, dtype in outs),
        in_specs=[pl.BlockSpec(memory_space=pltpu.VMEM)] * (len(ins) - far) + [HBM] * (far + len(after)),
        out_specs=tuple([HBM] * len(outs)),
        scratch_shapes=[
            pltpu.SemaphoreType.DMA((copies,)),
            pltpu.SemaphoreType.DMA((copies,)),
            pltpu.SemaphoreType.DMA((max(stays, 1),)),
        ],
        cost_estimate=COST,
        compiler_params=pltpu.CompilerParams(
            collective_id=ident, has_side_effects=True, vmem_limit_bytes=40 * 2**20
        ),
    )(*ins, *after)


def same_parity(at):
    return [
        at.index(*at.ahead(dz, dm))
        for dz in range(at.planes)
        for dm in range(CHIPS)
        if dz or dm
    ]


def opening(at, ins, outs):
    tokens, w_qkv, w_up, vectors, w_out = ins
    tokens_out, qkv_out, up_out, vectors_out, rows_out = outs
    kept = [
        (w_qkv.at[at.m], qkv_out.at[at.z, at.m, at.c]),
        (vectors, vectors_out.at[at.z, at.m, at.c]),
        (tokens, tokens_out.at[at.m]),
        (w_up.at[at.m], up_out.at[at.m]),
        (w_out, rows_out.at[at.z]),
    ]
    peers = [at.ahead(0, dm)[1] for dm in range(1, CHIPS)]
    first = [(w_qkv.at[m], qkv_out.at[at.z, at.m, at.c], at.index(at.z, m)) for m in peers]
    first += [(vectors, vectors_out.at[at.z, at.m, at.c], at.index(at.z, m)) for m in peers]
    rest = [(tokens, tokens_out.at[at.m], at.index(at.z, m)) for m in peers]
    rest += [(w_up.at[m], up_out.at[at.m], at.index(at.z, m)) for m in peers]
    sends = first
    forwards, columns = [], []
    last = at.planes - 1
    here = list(range(CHIPS - 1))

    def slab(out, plane):
        return out.at[jnp.clip(plane, 0, last), :, at.c]

    def hop(triggers, step, k):
        origin, next_plane = at.z - step * k, at.z + step
        sends_if = (next_plane >= 0) & (next_plane <= last) & (origin >= 0) & (origin <= last)
        came = at.z - step * (k + 1)
        receives_if = (came >= 0) & (came <= last)
        part = slab(qkv_out, origin)
        peer = at.index(lax.rem(next_plane + at.planes, at.planes), at.m)
        forwards.append((triggers, part, part, peer, sends_if, receives_if))
        return len(sends) + len(forwards) - 1

    ends = {step: hop(here, step, 0) for step in (1, -1)}
    own = slab(qkv_out, at.z)
    forwards.append((here, own, own, at.sibling))
    own = slab(vectors_out, at.z)
    here = [CHIPS - 1 + i for i in here]
    for dz in range(1, at.planes):
        columns.append((len(sends) + len(forwards), slab(vectors_out, at.ahead(-dz, 0)[0])))
        forwards.append((here, own, own, at.index(at.ahead(dz, 0)[0], at.m)))
    forwards.append((here, own, own, at.sibling))
    for dz in range(1, at.planes):
        rest.append((w_out, rows_out.at[at.z], at.index(at.ahead(dz, 0)[0], at.m)))
    forwards += [([], *send) for send in rest]
    for k in range(1, at.planes):
        for step in (1, -1):
            arrived = ends[step]
            if k < last:
                ends[step] = hop([arrived], step, k)
            origin = at.z - step * k
            came = (origin >= 0) & (origin <= last)
            part = slab(qkv_out, origin)
            forwards.append(([arrived], part, part, at.sibling, came, came))
    for slot, part in columns:
        forwards.append(([slot], part, part, at.sibling))
    partners = [at.index(at.z, m) for m in peers] + [at.sibling]
    partners += [at.index(at.ahead(dz, 0)[0], at.m) for dz in range(1, at.planes)]
    return partners, kept, sends, forwards


def windows(at, ins, outs):
    own, cotangent, rows = ins
    held, cotangent_out, rows_out = outs
    here, before = held.at[1, :, at.c], held.at[0, :, at.c]
    after = at.index(at.ahead(1, 0)[0], at.m)
    prior = at.index(at.ahead(-1, 0)[0], at.m)
    partners, kept, sends, _ = across(0, 1, 0, 0, at, (cotangent,), (cotangent_out,))
    column = rows_out.at[:, at.m]
    kept.append((rows, column))
    sends += [(rows, column, peer) for peer in partners]
    sends = [(own, before, after), (own, here, at.sibling), *sends]
    forwards = [([0], before, before, at.sibling)]
    return [after, prior, at.sibling, *partners], [(own, here), *kept], sends, forwards


def windows_back(at, ins, outs):
    (grads, partial), (grads_out, partial_out) = ins, outs
    after = at.index(at.ahead(1, 0)[0], at.m)
    prior = at.index(at.ahead(-1, 0)[0], at.m)
    partners, kept, sends, _ = across(1, 0, 0, 0, at, (partial,), (partial_out,))
    return [after, prior, *partners], kept, [(grads, grads_out, prior), *sends], []


def across(turned, spread, merged, halves, at, ins, outs):
    kept, sends, partners = [], [], []
    for dm in range(1, CHIPS) if turned + spread else ():
        m = at.ahead(0, dm)[1]
        peer = at.index(at.z, m)
        partners.append(peer)
        for k in range(turned):
            sends.append((ins[k].at[m], outs[k].at[at.m], peer))
        for k in range(turned, turned + spread):
            sends.append((ins[k], outs[k].at[at.m], peer))
    for k in range(turned):
        kept.append((ins[k].at[at.m], outs[k].at[at.m]))
    for k in range(turned, turned + spread):
        kept.append((ins[k], outs[k].at[at.m]))
    if halves + merged:
        partners.append(at.sibling)
    for k in range(turned + spread, turned + spread + merged):
        mine = outs[k].at[(*(slice(None),) * (len(ins[k].shape) - 2), at.c)]
        sends.append((ins[k], mine, at.sibling))
        kept.append((ins[k], mine))
    for k in range(turned + spread + merged, len(ins)):
        lead = (slice(None),) * (len(ins[k].shape) - 3)
        sends.append((ins[k].at[(*lead, 1 - at.c)], outs[k], at.sibling))
    return partners, kept, sends, []


def closing(at, ins, outs):
    grads, vectors, rows = ins[:3]
    grads_out, vectors_out, rows_out = outs[:3]
    kept = [
        (grads.at[at.z, at.m], grads_out.at[at.z, at.m]),
        (vectors.at[at.z, at.m], vectors_out.at[at.z, at.m]),
        (rows.at[at.z], rows_out.at[at.z]),
    ]
    _, kept_in, sends_in, _ = across(len(ins) - 3, 0, 0, 0, at, ins[3:], outs[3:])
    sends = []
    for dz in reversed(range(at.planes)):
        for dm in range(CHIPS):
            if dz or dm:
                z, m = at.ahead(dz, dm)
                peer = at.index(z, m)
                sends.append((grads.at[z, m], grads_out.at[at.z, at.m], peer))
                sends.append((vectors.at[z, m], vectors_out.at[at.z, at.m], peer))
                if dm == 0:
                    sends.append((rows.at[z], rows_out.at[at.z], peer))
    return same_parity(at), kept + kept_in, sends + sends_in, []


def swap(ident, turned=(), spread=(), merged=(), halves=(), after=()):
    outs = [(x.shape, x.dtype) for x in turned]
    outs += [((CHIPS, *x.shape), x.dtype) for x in spread]
    outs += [((*x.shape[:-2], CORES, *x.shape[-2:]), x.dtype) for x in merged]
    outs += [((*x.shape[:-3], *x.shape[-2:]), x.dtype) for x in halves]
    plan = functools.partial(across, len(turned), len(spread), len(merged), len(halves))
    stays = len(turned) + len(spread)
    copies = (CHIPS - 1) * stays + len(halves) + len(merged)
    ins = (*turned, *spread, *merged, *halves)
    return exchange(plan, ins, outs, ident, copies, stays + len(merged), len(halves), after)


def by_window(info_ref, run):
    step = pl.program_id(0)
    inside = info_ref[step]

    def with_slots(slots):
        first = CORES * step + info_ref[CHIPS] + 1 + MAXB - slots
        start = pl.multiple_of(first * BLOCK, BLOCK)
        row = lax.broadcasted_iota(jnp.int32, (slots * BLOCK, BLOCK), 0)
        query = lax.broadcasted_iota(jnp.int32, (slots * BLOCK, BLOCK), 1)
        slot = slots - 1 - lax.shift_right_logical(row, 7)
        column = lax.bitwise_and(row, BLOCK - 1)
        allowed = (slot <= inside) & ((slot > 0) | (column <= query))
        run(pl.ds(start, slots * BLOCK), allowed)

    pl.when(inside >= MAXB // 2)(lambda: with_slots(MAXB))
    pl.when(inside < MAXB // 2)(lambda: with_slots(MAXB // 2))


def contract(a, b, over):
    return lax.dot_general(a, b, (((over[0],), (over[1],)), ((), ())), preferred_element_type=F32)


def attend_kernel(info_ref, q_ref, kv_ref, _, out_ref, lse_ref):
    def run(span, allowed):
        for head in range(SLOTS):
            part = pl.ds(head * HEAD, HEAD)
            keys = kv_ref[span, part]
            values = kv_ref[span, pl.ds(WIDE + head * HEAD, HEAD)]
            scores = jnp.where(allowed, contract(keys, q_ref[:, part], (1, 1)), -1e30)
            top = jnp.max(scores, axis=0, keepdims=True)
            powers = jnp.exp(scores - top)
            total = jnp.sum(powers, axis=0, keepdims=True)
            probs = (powers * (1.0 / total)).astype(BF16)
            out_ref[:, part] = contract(probs, values, (0, 0)).astype(BF16)
            lse_ref[0, pl.ds(head, 1), :] = top + jnp.log(total)

    by_window(info_ref, run)


def attend_back_kernel(info_ref, q_ref, kv_ref, grad_ref, lse_ref, grad_q_ref, grad_kv_ref, rounded_ref):
    @pl.when(pl.program_id(0) == 0)
    def _():
        grad_kv_ref[...] = jnp.zeros_like(grad_kv_ref)

    def run(span, allowed):
        for head in range(SLOTS):
            part = pl.ds(head * HEAD, HEAD)
            part_v = pl.ds(WIDE + head * HEAD, HEAD)
            keys, values = kv_ref[span, part], kv_ref[span, part_v]
            query, grad = q_ref[:, part], grad_ref[:, part]
            scores = jnp.where(allowed, contract(keys, query, (1, 1)), -1e30)
            probs = jnp.exp(scores - lse_ref[0, pl.ds(head, 1), :])
            grad_probs = contract(values, grad, (1, 1))
            delta = jnp.sum(probs * grad_probs, axis=0, keepdims=True)
            grad_scores = (probs * (grad_probs - delta)).astype(BF16)
            grad_q_ref[:, part] = contract(grad_scores, keys, (0, 0))
            grad_kv_ref[span, part] += contract(grad_scores, query, (1, 0))
            grad_kv_ref[span, part_v] += contract(probs.astype(BF16), grad, (1, 0))

    by_window(info_ref, run)

    @pl.when(pl.program_id(0) == CHIPS - 1)
    def _():
        rounded_ref[...] = grad_kv_ref[...].astype(BF16)


def block_rows(width):
    return pl.BlockSpec((BLOCK, width), lambda i: (i, 0))


def whole_of(x):
    return pl.BlockSpec(x.shape, lambda i: (0,) * len(x.shape))


LSE = pl.BlockSpec((1, 8, BLOCK), lambda i: (i, 0, 0))
SMEM = pl.BlockSpec(memory_space=pltpu.SMEM)


def attend_heads(info, query, held, after):
    return pl.pallas_call(
        attend_kernel,
        grid=(CHIPS,),
        in_specs=[SMEM, block_rows(WIDE), whole_of(held), HBM],
        out_specs=(block_rows(WIDE), LSE),
        out_shape=(
            jax.ShapeDtypeStruct(query.shape, BF16),
            jax.ShapeDtypeStruct((CHIPS, 8, BLOCK), F32),
        ),
        cost_estimate=COST,
        compiler_params=pltpu.CompilerParams(vmem_limit_bytes=40 * 2**20),
    )(info, query, held, after)


def attend_heads_back(info, query, held, grad, lse):
    return pl.pallas_call(
        attend_back_kernel,
        grid=(CHIPS,),
        in_specs=[SMEM, block_rows(WIDE), whole_of(held), block_rows(WIDE), LSE],
        out_specs=(block_rows(WIDE), whole_of(held), whole_of(held)),
        out_shape=(
            jax.ShapeDtypeStruct(query.shape, F32),
            jax.ShapeDtypeStruct(held.shape, F32),
            jax.ShapeDtypeStruct(held.shape, BF16),
        ),
        cost_estimate=COST,
        compiler_params=pltpu.CompilerParams(vmem_limit_bytes=48 * 2**20),
    )(info, query, held, grad, lse)


def dot(a, b):
    return jnp.dot(a, b, preferred_element_type=F32)


def compute(body, ins, outs, scratch=(), small=()):
    vmem = pl.BlockSpec(memory_space=pltpu.VMEM)
    return pl.pallas_call(
        body,
        in_specs=[SMEM] * len(small) + [vmem] * len(ins),
        out_specs=tuple([vmem] * len(outs)),
        out_shape=tuple(jax.ShapeDtypeStruct(shape, dtype) for shape, dtype in outs),
        scratch_shapes=[pltpu.VMEM(shape, dtype) for shape, dtype in scratch],
        cost_estimate=COST,
        compiler_params=pltpu.CompilerParams(vmem_limit_bytes=56 * 2**20),
    )(*small, *ins)


def pieces(ref):
    planes, chips, cores, rows, _ = ref.shape
    for j in range(planes * chips * cores):
        yield (j // (chips * cores), j // cores % chips, j % cores), pl.ds(j * rows, rows)


def normed(values):
    average = jnp.mean(values, axis=-1, keepdims=True)
    centred = values - average
    inv_std = lax.rsqrt(jnp.mean(centred * centred, axis=-1, keepdims=True) + EPS)
    return centred * inv_std, inv_std


def column_sum(values):
    return jnp.sum(values, axis=0, keepdims=True)


HALF = CHIPS // 2


def project_kernel(tokens, parts, vec, bias_kv, bias_q, normed_out, kv_out, q_out, weight):
    for at, rows in pieces(parts):
        weight[rows, :] = parts[at]
    for i in range(2):
        values = tokens[pl.ds(i * HALF, HALF)].astype(F32).reshape(HALF * BLOCK, -1)
        hat, _ = normed(values)
        rows = (hat * vec[0:1, :] + vec[1:2, :]).astype(BF16)
        normed_out[pl.ds(i * HALF * BLOCK, HALF * BLOCK), :] = rows
        projected = dot(rows, weight[...])
        kv = (projected[:, : 2 * WIDE] + bias_kv[...]).astype(BF16)
        kv_out[pl.ds(i * HALF, HALF)] = kv.reshape(HALF, BLOCK, 2 * WIDE)
        query = HEAD ** (-0.5) * (projected[:, 2 * WIDE :] + bias_q[...])
        q_out[pl.ds(i * HALF * BLOCK, HALF * BLOCK), :] = query.astype(BF16)


def project_back_kernel(
    grad_q, grad_kv, grad_before, tokens, rows_in, weight, vec, grad_out, parts, sums, sums_wide, grads, total
):
    for i in range(2):
        span = pl.ds(i * HALF * BLOCK, HALF * BLOCK)
        blocks = pl.ds(i * HALF, HALF)
        both = grad_kv[blocks] + grad_before[blocks].astype(F32)
        both = both.reshape(HALF * BLOCK, 2 * WIDE)
        query = HEAD ** (-0.5) * grad_q[span, :]
        grads[span, : 2 * WIDE] = both.astype(BF16)
        grads[span, 2 * WIDE :] = query.astype(BF16)
        back = contract(grads[span, :], weight[...], (1, 1))
        hat, _ = normed(tokens[blocks].astype(F32).reshape(HALF * BLOCK, -1))
        new = (column_sum(back * hat), column_sum(back), column_sum(both), column_sum(query))
        if i:
            old = (sums[0:1, :], sums[1:2, :], sums_wide[0:1, : 2 * WIDE], sums_wide[0:1, 2 * WIDE :])
            new = tuple(a + b for a, b in zip(old, new))
        sums[0:1, :], sums[1:2, :] = new[:2]
        sums_wide[0:1, : 2 * WIDE], sums_wide[0:1, 2 * WIDE :] = new[2:]
        grad_out[blocks] = back.astype(BF16).reshape(HALF, BLOCK, -1)
    total[...] = contract(rows_in[...], grads[...], (0, 0))
    for at, rows in pieces(parts):
        parts[at] = total[rows, :].astype(BF16)


def head_rows():
    for s in range(CHIPS):
        yield s, s * WIDE, min(WIDE, D - s * WIDE)


def output_kernel(attended, parts, tokens, vec, residual, normed_out, weight):
    for at, rows in pieces(parts):
        weight[rows, :] = parts[at]
    values = tokens[...].astype(F32) + vec[4:5, :]
    for s, first, size in head_rows():
        values += dot(attended[s, :, :size], weight[pl.ds(first, size), :])
    residual[...] = values
    hat, _ = normed(values)
    normed_out[...] = (hat * vec[5:6, :] + vec[6:7, :]).astype(BF16)


def output_back_kernel(
    filled, grads_in, residual, cotangent, attended, weight, vec, grad_residual, heads, parts, sums, total
):
    row = lax.broadcasted_iota(jnp.int32, cotangent.shape, 0)
    cot = jnp.where(row < filled[0], cotangent[...].astype(F32), 0.0)
    grad = grads_in[0].astype(F32)
    for s in range(1, CHIPS):
        grad += grads_in[s].astype(F32)
    hat, inv_std = normed(residual[...])
    back = cot + norm_back(grad, hat, inv_std, vec[5:6, :])
    grad_residual[...] = back
    sums[0:1, :] = column_sum(grad * hat)
    sums[1:2, :] = column_sum(grad)
    sums[2:3, :] = column_sum(back)
    sums[3:4, :] = column_sum(cot)
    rounded = back.astype(BF16)
    for s, first, size in head_rows():
        if size < WIDE:
            heads[s] = jnp.zeros(heads.shape[1:], BF16)
        part = contract(rounded, weight[pl.ds(first, size), :], (1, 1))
        heads[s, :, :size] = part.astype(BF16)
        total[pl.ds(first, size), :] = contract(attended[s, :, :size], rounded, (0, 0))
    for at, rows in pieces(parts):
        parts[at] = total[rows, :].astype(BF16)


def feed_kernel(
    filled, rows_in, parts, down, bias, cotangent, result, grad_rows, grad_down, grad_up, sums,
    up, active, grads, cot, total,
):
    for at, rows in pieces(parts):
        up[rows, :] = parts[at]
    for i in range(2):
        span = pl.ds(i * HALF * BLOCK, HALF * BLOCK)
        for k in range(i * HALF, (i + 1) * HALF):
            row = lax.broadcasted_iota(jnp.int32, cotangent.shape[1:], 0)
            block = jnp.where(row < filled[k], cotangent[k].astype(F32), 0.0)
            cot[pl.ds(k * BLOCK, BLOCK), :] = block.astype(BF16)
        rows = rows_in[pl.ds(i * HALF, HALF)].reshape(HALF * BLOCK, -1)
        pre = dot(rows, up[...]) + bias[...]
        normal_cdf = 0.5 * (1.0 + lax.erf(pre * 2.0 ** (-0.5)))
        active[span, :] = (pre * normal_cdf).astype(BF16)
        normal_pdf = jnp.exp(-0.5 * pre * pre) * (2.0 * jnp.pi) ** (-0.5)
        back = contract(cot[span, :], down[...], (1, 1)) * (normal_cdf + pre * normal_pdf)
        grads[span, :] = back.astype(BF16)
        new = column_sum(back)
        sums[...] = sums[...] + new if i else new
        part = dot(active[span, :], down[...])
        result[pl.ds(i * HALF, HALF)] = part.astype(BF16).reshape(HALF, BLOCK, -1)
        part = contract(grads[span, :], up[...], (1, 1))
        grad_rows[pl.ds(i * HALF, HALF)] = part.astype(BF16).reshape(HALF, BLOCK, -1)
    total[...] = contract(active[...], cot[...], (0, 0))
    planes, cores, size, _ = grad_down.shape
    for j in range(planes * cores):
        grad_down[j // cores, j % cores] = total[pl.ds(j * size, size), :].astype(BF16)
    total[...] = contract(rows_in[...].reshape(CHIPS * BLOCK, -1), grads[...], (0, 0))
    for at, rows in pieces(grad_up):
        grad_up[at] = total[rows, :].astype(BF16)


def local_split(tokens, seq_lengths, w_qkv, w_out, w_up, w_down, vectors, cotangent):
    count = lax.axis_size("dp")
    planes = count // SPAN
    me = lax.axis_index("dp")
    z, m, c = me // SPAN, (me // CORES) % CHIPS, me % CORES
    along_z = [[p + SPAN * k for k in range(planes)] for p in range(SPAN)]
    in_plane = [
        [SPAN * k + CORES * i + core for i in range(CHIPS)]
        for k in range(planes)
        for core in range(CORES)
    ]

    def gather_z(x):
        return lax.all_gather(x, "dp", axis_index_groups=along_z)

    def scatter(x, groups, axis):
        return lax.psum_scatter(
            x, "dp", axis_index_groups=groups, scatter_dimension=axis, tiled=False
        )

    def own(x, axis):
        return lax.dynamic_index_in_dim(x, c, axis, keepdims=False)

    rows_in = D // count
    hidden = FF // CHIPS
    share = hidden // planes
    rows_ff = FF // count
    heads_of = w_qkv.reshape(rows_in, 3, D)
    heads_of = jnp.concatenate([heads_of[:, 1:], heads_of[:, :1]], axis=1)
    heads_of = jnp.pad(heads_of, ((0, 0), (0, 0), (0, CHIPS * WIDE - D)))
    heads_of = heads_of.reshape(rows_in, 3, CHIPS, WIDE).transpose(2, 0, 1, 3)
    heads_of = heads_of.reshape(CHIPS, rows_in, 3 * WIDE)
    up_slices = w_up.reshape(rows_in, planes, CHIPS, share).transpose(2, 0, 1, 3)
    up_slices = up_slices.reshape(CHIPS, rows_in, hidden)
    vec_own = vectors.reshape(1, -1)
    tokens4, weight_qkv, up_part, vecs, out_part = exchange(
        opening,
        (tokens, heads_of, up_slices, vec_own, w_out.reshape(rows_in, D)),
        [
            ((CHIPS, BLOCK, D), BF16),
            ((planes, CHIPS, CORES, rows_in, 3 * WIDE), BF16),
            (up_slices.shape, BF16),
            ((planes, CHIPS, CORES, *vec_own.shape), BF16),
            ((planes, rows_in, D), BF16),
        ],
        1,
        4 * (CHIPS - 1) + 9 * (planes - 1) + 4,
        5,
    )
    w_down, weight_qkv = lax.optimization_barrier((w_down, weight_qkv))
    down_part = gather_z(w_down.reshape(rows_ff, D))

    blocks = SPAN * z + CORES * jnp.arange(CHIPS, dtype=jnp.int32) + c
    inside, filled = block_layout(seq_lengths, blocks)
    filled_own = lax.dynamic_index_in_dim(filled, m, 0, keepdims=False)
    valid = (jnp.arange(BLOCK, dtype=jnp.int32) < filled_own)[:, None]
    info = jnp.concatenate([inside, jnp.reshape(c, (1,))]).astype(jnp.int32)

    vec = vecs.reshape(-1)[: 12 * D].reshape(12, D).astype(F32)

    def head_bias(row):
        padded = jnp.pad(vec[row], (0, CHIPS * WIDE - D)).reshape(CHIPS, WIDE)
        return lax.dynamic_index_in_dim(padded, m, 0, keepdims=False)

    bias_up = vec[8:12].reshape(planes, CHIPS, share)
    bias_up = lax.dynamic_index_in_dim(bias_up, m, 1, keepdims=False).reshape(hidden)
    bias_kv = jnp.concatenate([jnp.zeros((WIDE,), F32), head_bias(3)])
    normed_attn, key_value, query, weight_qkv = compute(
        project_kernel,
        (tokens4, weight_qkv, vec, bias_kv[None], head_bias(2)[None]),
        [
            ((CHIPS * BLOCK, D), BF16),
            ((CHIPS, BLOCK, 2 * WIDE), BF16),
            ((CHIPS * BLOCK, WIDE), BF16),
            ((D, 3 * WIDE), BF16),
        ],
    )
    held, cotangent4, out_part = exchange(
        windows,
        (key_value, cotangent, out_part),
        [
            ((2, CHIPS, CORES, BLOCK, 2 * WIDE), BF16),
            ((CHIPS, BLOCK, D), BF16),
            ((planes, CHIPS, rows_in, D), BF16),
        ],
        2,
        3 + 2 * (CHIPS - 1),
        3,
    )
    up_part, held = lax.optimization_barrier((up_part, held))
    up_part = gather_z(up_part)
    held = held.reshape(2 * SPAN * BLOCK, 2 * WIDE)
    attended_heads, lse = attend_heads(info, query, held, down_part)
    attended_own, weight_out = swap(
        3, turned=(attended_heads.reshape(CHIPS, BLOCK, WIDE),), merged=(out_part,)
    )
    residual, normed_mlp, weight_out = compute(
        output_kernel,
        (attended_own, weight_out, tokens, vec),
        [((BLOCK, D), F32), ((BLOCK, D), BF16), ((D, D), BF16)],
    )
    mlp4, weight_up, weight_down = swap(
        4, spread=(normed_mlp,), merged=(up_part, down_part)
    )
    rows, square = CHIPS * BLOCK, (D, hidden)
    result_part, grad_mlp_part, grad_down, grad_up, grad_bias_up = compute(
        feed_kernel,
        (mlp4, weight_up, weight_down.reshape(hidden, D), bias_up[None], cotangent4),
        [
            (mlp4.shape, BF16),
            (mlp4.shape, BF16),
            ((planes, CORES, rows_ff, D), BF16),
            ((planes, CHIPS, CORES, rows_in, hidden), BF16),
            ((1, hidden), F32),
        ],
        [(square, BF16), ((rows, hidden), BF16), ((rows, hidden), BF16), ((rows, D), BF16), (square, F32)],
        (filled,),
    )
    grad_mlp, down_half, up_half = swap(5, turned=(grad_mlp_part,), halves=(grad_down, grad_up))

    def joined(mine, other):
        return (mine.astype(F32) + other.astype(F32)).astype(BF16)

    grad_down, grad_up, grad_mlp = lax.optimization_barrier(
        (joined(own(grad_down, 1), down_half), joined(own(grad_up, 2), up_half), grad_mlp)
    )
    grad_down = scatter(grad_down, along_z, 0)
    grad_up = scatter(grad_up, along_z, 0)
    shard_down = grad_down.astype(F32).reshape(w_down.shape)

    grad_residual, grad_attended, grad_out, sums_out = compute(
        output_back_kernel,
        (grad_mlp, residual, cotangent, attended_own, weight_out, vec),
        [
            ((BLOCK, D), F32),
            ((CHIPS, BLOCK, WIDE), BF16),
            ((planes, CHIPS, CORES, rows_in, D), BF16),
            ((4, D), F32),
        ],
        [((D, D), F32)],
        (jnp.reshape(filled_own, (1,)),),
    )
    grad_heads, out_half = swap(6, turned=(grad_attended,), halves=(grad_out,))
    grad_out = joined(own(grad_out, 2), out_half).transpose(1, 0, 2, 3)

    grad_query, grad_held, held_rounded = attend_heads_back(
        info, query, held, grad_heads.reshape(CHIPS * BLOCK, WIDE), lse
    )
    grad_held = grad_held.reshape(2, CHIPS, CORES, BLOCK, 2 * WIDE)
    out_parts, held_half = swap(
        7, turned=(grad_out,), halves=(held_rounded.reshape(grad_held.shape),), after=(grad_down,)
    )
    grad_out = jnp.sum(out_parts.astype(F32), axis=0).astype(BF16)
    grad_held = own(grad_held, 2) + held_half.astype(F32)
    grad_before, result = exchange(
        windows_back,
        (grad_held[0].astype(BF16), result_part),
        [((CHIPS, BLOCK, 2 * WIDE), BF16), (result_part.shape, BF16)],
        8,
        1 + CHIPS - 1,
        1,
    )
    result = residual + jnp.sum(result.astype(F32), axis=0) + vec[7]
    out_block = jnp.where(valid, result, 0.0).astype(BF16)

    grad_attn_part, grad_qkv, sums_in, sums_wide = compute(
        project_back_kernel,
        (grad_query, grad_held[1], grad_before, tokens4, normed_attn, weight_qkv, vec),
        [
            ((CHIPS, BLOCK, D), BF16),
            ((planes, CHIPS, CORES, rows_in, 3 * WIDE), BF16),
            ((2, D), F32),
            ((1, 3 * WIDE), F32),
        ],
        [((CHIPS * BLOCK, 3 * WIDE), BF16), ((D, 3 * WIDE), F32)],
    )

    def placed(values, width, length):
        start = jnp.zeros((CHIPS * width,), F32)
        return lax.dynamic_update_slice(start, values, (m * width,))[:length]

    placed_up = jnp.where(
        jnp.arange(CHIPS)[None, :, None] == m, grad_bias_up.reshape(planes, 1, share), 0.0
    )
    rows = [
        sums_in.reshape(-1),
        placed(sums_wide[0, 2 * WIDE :], WIDE, D),
        placed(sums_wide[0, WIDE : 2 * WIDE], WIDE, D),
        sums_out[2],
        sums_out[:2].reshape(-1),
        sums_out[3],
        placed_up.reshape(FF),
    ]
    grad_vec = pad_flat(jnp.concatenate(rows), vectors.shape[0] * count)
    grad_vec = grad_vec.reshape(planes, CHIPS, CORES, 1, -1)
    qkv_half, vec_half = swap(9, halves=(grad_qkv, grad_vec), after=(grad_up,))
    grad_qkv = joined(own(grad_qkv, 2), qkv_half)
    grad_vec = own(grad_vec, 2) + vec_half
    ins = (
        grad_qkv,
        grad_vec,
        grad_out,
        grad_attn_part,
        grad_up,
    )
    grad_qkv, grad_vec, grad_out, grad_attn, grad_up = exchange(
        closing,
        ins,
        [(x.shape, x.dtype) for x in ins],
        10,
        2 * (planes * CHIPS - 1) + planes - 1 + 2 * (CHIPS - 1),
        5,
    )
    shard_vec = jnp.sum(grad_vec, axis=(0, 1)).reshape(-1)
    shard_qkv = jnp.sum(grad_qkv.astype(F32), axis=0).reshape(CHIPS, rows_in, 3, WIDE)
    shard_qkv = shard_qkv.transpose(1, 2, 0, 3).reshape(rows_in, 3, CHIPS * WIDE)[:, :, :D]
    shard_qkv = jnp.concatenate([shard_qkv[:, 2:], shard_qkv[:, :2]], axis=1)
    shard_qkv = shard_qkv.reshape(-1)
    shard_up = grad_up.astype(F32).reshape(CHIPS, rows_in, planes, share)
    shard_up = shard_up.transpose(1, 2, 0, 3).reshape(-1)
    shard_out = jnp.sum(grad_out.astype(F32), axis=0).reshape(-1)
    hat_own, inv_own = normed(tokens.astype(F32))
    grad_normed_attn = jnp.sum(grad_attn.astype(F32), axis=0)
    grad_tokens = grad_residual + norm_back(grad_normed_attn, hat_own, inv_own, vec[0])
    return (out_block, grad_tokens, shard_qkv, shard_out, shard_up, shard_down, shard_vec)


def local(*args):
    count = lax.axis_size("dp")
    _, _, w_qkv, w_out, w_up, w_down, vectors, _ = args
    fits = count == SPAN * CHIPS and vectors.shape[0] * count >= 12 * D
    for shard, rows, cols in ((w_qkv, D, 3 * D), (w_out, D, D), (w_up, D, FF), (w_down, FF, D)):
        fits = fits and whole_rows(shard, rows, cols)
    return local_split(*args) if fits else local_gathered(*args)


def solution(mesh):
    in_specs = (P("dp", None), P(), P("dp"), P("dp"), P("dp"), P("dp"), P("dp"), P("dp", None))
    out_specs = (P("dp", None), P("dp", None), P("dp"), P("dp"), P("dp"), P("dp"), P("dp"))
    return jax.shard_map(local, mesh=mesh, in_specs=in_specs, out_specs=out_specs, check_vma=False)
```
